32 devices in a mesh: table: 8 (over y, x, core), rep: 4 (over z).
Axes of the slice: x: 2, y: 2, z: 4, core: 2. Of those that a mesh axis runs over, the one named last changes fastest.
Arguments:
- feature_table: bfloat16 [73728, 1024], P('table'), may hold values from -6 to 6
- neighbour_query_weight: bfloat16 [1024, 1024], replicated, may hold values from -0.1875 to 0.1875
- query_bias: float32 [1024], replicated, may hold values from -1.8 to 1.8
- mix_weight: bfloat16 [2048, 1024], replicated, may hold values from -0.125 to 0.125
- mix_bias: float32 [1024], replicated, may hold values from -1.8 to 1.8
- lookup_ids: int32 [6144, 51], P(('table', 'rep')), may hold values from 0 to 73727, as said below
- present_counts: int32 [6144], P(('table', 'rep')), may hold values from 5 to 50, as said below
- importance: float32 [6144, 50], P(('table', 'rep')), may hold values from 0.75 to 1
- embed_cot: bfloat16 [6144, 1024], P(('table', 'rep')), may hold values from -6 to 6
Outputs:
- embed: bfloat16 [6144, 1024], P(('table', 'rep'))
- table_grad: float32 [73728, 1024], P('table', 'rep')
- query_weight_grad: float32 [1024, 1024], replicated
- query_bias_grad: float32 [1024], replicated
- mix_weight_grad: float32 [2048, 1024], replicated
- mix_bias_grad: float32 [1024], replicated
- statistics: float32 [2], replicated
The draws below stay inside these ranges and needn't reach their ends.
Inputs may be any that keep to these rules, and one draw needn't show every extreme that they name: `lookup_ids`: within the 192 rows of one device (rows in the order of table+rep), the slots whose id lies in one table index's range (id // 9216) number at most 2448, and one range takes exactly 2448 of them. Of that device's present slots (slot 0, and neighbour slot j + 1 where j < the row's count) at most 1368 lie in one range; on every device one range takes exactly 1368. `present_counts`: the 192 targets of one device come in pairs whose counts add up to one value for that device, from 30 to 55; on the first device it is 55.
All inputs are finite; a program needn't handle non-finite values.
Results may differ from the reference program's by a relative error of at most 0.014.
The reference program's roundings to bfloat16 on the way count: a program that leaves them out, or rounds other values in their place, can miss the bound.
Values may be sent and summed in bfloat16 or wider, within the bound.
No kernel may reach another device: no remote copies, remote signals or barrier semaphores. Data moves between devices by JAX's collectives and lax.ppermute only.
A program may use at most 384 MiB of HBM per device.

```python
import jax
import jax.numpy as jnp
from jax import lax

D = 1024
K = 50
B_DEV = 192
SLOTS = 51
ROWS_OWN = 9216
NODES = 73728
TARGETS = 6144
CAP = 2448
CAP_LIVE = 1368
N_TABLE = 8


def device_block(key, block_index):
    slot_total = B_DEV * SLOTS
    block_key = jax.random.fold_in(jax.random.fold_in(key, 7), block_index)
    sum_key, pair_key, turn_key, hot_key, order_key, row_key = jax.random.split(block_key, 6)
    pair_sum = jnp.where(block_index == 0, K + 5, jax.random.randint(sum_key, (), K - 20, K + 6)).astype(jnp.int32)
    least = jnp.maximum(5, pair_sum - K)
    most = jnp.minimum(K, pair_sum - 5)
    first = jax.random.randint(pair_key, (B_DEV // 2,), least, most + 1).astype(jnp.int32)
    counts = jax.random.permutation(turn_key, jnp.concatenate([first, pair_sum - first]))
    slot_index = jnp.arange(SLOTS, dtype=jnp.int32)
    live = ((slot_index[None, :] == 0) | (slot_index[None, :] - 1 < counts[:, None])).reshape(slot_total)
    hot_live = jnp.int32(CAP_LIVE)
    hot_dead = CAP - hot_live
    hottest = jax.random.randint(hot_key, (), 0, N_TABLE).astype(jnp.int32)
    order = jax.random.permutation(order_key, slot_total)
    live_order = live[order].astype(jnp.int32)
    rank_live = jnp.cumsum(live_order) - 1
    rank_dead = jnp.cumsum(1 - live_order) - 1
    rank = jnp.where(live_order == 1, rank_live, rank_dead)
    quota = jnp.where(live_order == 1, hot_live, hot_dead)
    owner_order = jnp.where(rank < quota, hottest, (hottest + 1 + (rank - quota) % (N_TABLE - 1)) % N_TABLE)
    owner_of = jnp.zeros((slot_total,), jnp.int32).at[order].set(owner_order.astype(jnp.int32))
    local_rows = jax.random.randint(row_key, (slot_total,), 0, ROWS_OWN).astype(jnp.int32)
    node_ids = (owner_of * ROWS_OWN + local_rows).reshape(B_DEV, SLOTS)
    return (node_ids.astype(jnp.int32), counts.astype(jnp.int32))


def draw_both(key):
    return lax.map(lambda index: device_block(key, index), jnp.arange(TARGETS // B_DEV, dtype=jnp.int32))


def draw_lookup_ids(key, part):
    node_ids, counts = draw_both(key)
    return node_ids.reshape(TARGETS, SLOTS).astype(jnp.int32)


def draw_present_counts(key, part):
    node_ids, counts = draw_both(key)
    return counts.reshape(TARGETS).astype(jnp.int32)


def block_levels(stream_key, extent, pieces, low, top_value):
    level = 1.0
    for dim, blocks in pieces:
        steps = jax.random.uniform(jax.random.fold_in(jax.random.fold_in(stream_key, 6), dim), (blocks,), jnp.float32, low / len(pieces), top_value / len(pieces))
        level = level * jnp.repeat(jnp.exp(steps), extent[dim] // blocks).reshape((-1,) + (1,) * (len(extent) - 1 - dim))
    return level


def gaussian(stream_key, dims, scale, bound, pieces=(), kind=jnp.bfloat16):
    loudness = block_levels(stream_key, dims, pieces, -0.22, 0.18) if pieces else 1.0
    values = jax.random.normal(stream_key, dims, jnp.float32) * scale * loudness
    return jnp.minimum(jnp.maximum(values, -bound), bound).astype(kind)


def setup_inputs(seed: int = 0) -> dict:
    seeds = jax.random.split(jax.random.key(seed), 10)
    feature_table = gaussian(seeds[0], (NODES, D), 1.0, 6.0, ((0, 8),))
    neighbour_query_weight = gaussian(seeds[1], (D, D), D ** -0.5, 0.1875)
    query_bias = gaussian(seeds[2], (D,), 0.3, 1.8, (), jnp.float32)
    mix_weight = gaussian(seeds[3], (2 * D, D), (2 * D) ** -0.5, 0.125)
    mix_bias = gaussian(seeds[4], (D,), 0.3, 1.8, (), jnp.float32)
    lookup_ids = draw_lookup_ids(jax.random.fold_in(seeds[9], 71), 0)
    present_counts = draw_present_counts(jax.random.fold_in(seeds[9], 71), 0)
    importance = jnp.clip(0.75 + 0.25 * jax.random.uniform(seeds[7], (TARGETS, K), jnp.float32) ** block_levels(seeds[7], (TARGETS, K), ((0, 32),), -0.2, 0.2), 0.75, 1.0)
    embed_cot = gaussian(seeds[8], (TARGETS, D), 1.0, 6.0, ((0, 32),))
    return dict(feature_table=feature_table, neighbour_query_weight=neighbour_query_weight, query_bias=query_bias, mix_weight=mix_weight, mix_bias=mix_bias, lookup_ids=lookup_ids, present_counts=present_counts, importance=importance, embed_cot=embed_cot)


@jax.custom_vjp
def lower_precision(v):
    return lax.optimization_barrier(v.astype(jnp.bfloat16)).astype(jnp.float32)

@jax.custom_vjp
def lower_precision_backward(v):
    return v

def low_keep(v):
    return (lower_precision(v), None)

def low_pass(kept, grad):
    return (grad,)

def back_keep(v):
    return (v, None)

def back_low(kept, grad):
    return (lower_precision(grad),)
lower_precision.defvjp(low_keep, low_pass)
lower_precision_backward.defvjp(back_keep, back_low)

def reference(feature_table, neighbour_query_weight, query_bias, mix_weight, mix_bias, lookup_ids, present_counts, importance, embed_cot):
    largest_index = lax.Precision.HIGHEST
    present = (jnp.arange(K, dtype=jnp.int32)[None, :] < present_counts[:, None]).astype(jnp.float32)
    masked_weight = importance * present
    row_portions = lower_precision(masked_weight / lax.optimization_barrier(jnp.sum(masked_weight, axis=1, keepdims=True)))
    block_rows = min(64, TARGETS)
    block_ids = lookup_ids.reshape(TARGETS // block_rows, block_rows, SLOTS)
    block_shares = row_portions.reshape(TARGETS // block_rows, block_rows, K)

    def forward(table_full, query_weight_whole, query_offset_bias, mix_full, bias_mix):

        def one_block(inputs):
            ids_here, local_row_portions = inputs
            gathered_rows = lower_precision_backward(table_full[ids_here])
            before_relu = lower_precision_backward(jnp.einsum('wsa,ai->wsi', gathered_rows[:, 1:, :], query_weight_whole, precision=largest_index) + query_offset_bias)
            hidden_output = lower_precision(jax.nn.relu(before_relu))
            pooled_neighbours = lower_precision(jnp.einsum('ef,efq->eq', local_row_portions, hidden_output, precision=largest_index))
            joined = jnp.concatenate([gathered_rows[:, 0, :], pooled_neighbours], axis=1)
            mixed = lower_precision_backward(jnp.dot(joined, mix_full, precision=largest_index) + bias_mix)
            activation = jax.nn.relu(mixed)
            return activation * lax.rsqrt(lax.optimization_barrier(jnp.mean(activation * activation, axis=1, keepdims=True)) + 1e-06)
        result = lax.map(jax.checkpoint(one_block), (block_ids, block_shares))
        return result.reshape(TARGETS, D)
    embed, pullback = jax.vjp(forward, feature_table.astype(jnp.float32), neighbour_query_weight.astype(jnp.float32), query_bias, mix_weight.astype(jnp.float32), mix_bias)
    grads = pullback(embed_cot.astype(jnp.float32))
    statistics = jnp.stack([jnp.sum(present), jnp.sum(masked_weight)]) / TARGETS
    return (embed.astype(jnp.bfloat16), grads[0], grads[1], grads[2], grads[3], grads[4], statistics)
```

```python
import functools

import jax
import jax.numpy as jnp
from jax import lax
from jax.experimental import pallas as pl
from jax.experimental.pallas import tpu as pltpu
from jax.sharding import PartitionSpec as P

F32 = jnp.float32
BF16 = jnp.bfloat16
I32 = jnp.int32
LANES = 128
SUBLANES = 8
ROW_BLOCK = 512
SHIFT = 256
UNROLL = 4
VMEM_BYTES = 60 << 20


def row_at(ref, row):
    return ref[pl.ds(pl.multiple_of(row * SUBLANES, SUBLANES), SUBLANES), :]


def put_row(ref, row, value):
    ref[pl.ds(pl.multiple_of(row * SUBLANES, SUBLANES), SUBLANES), :] = value


def clear_rows(ref, rows):
    zero = jnp.zeros((SUBLANES * SUBLANES, LANES), F32)

    def step(i, carry):
        ref[pl.ds(pl.multiple_of(i * SUBLANES * SUBLANES, SUBLANES), SUBLANES * SUBLANES), :] = zero
        return carry

    lax.fori_loop(0, rows // SUBLANES, step, 0)


def walk(first, last, entry):
    count = last - first
    groups = count // UNROLL

    def group(i, carry):
        for u in range(UNROLL):
            entry(first + i * UNROLL + u)
        return carry

    def single(k, carry):
        entry(k)
        return carry

    lax.fori_loop(0, groups, group, 0)
    lax.fori_loop(first + groups * UNROLL, last, single, 0)


def forward_kernel(blocks, bounds, table, query, bias, codes, shares, hidden, pooled, hidden_rows, pooled_rows):
    step = pl.program_id(0)
    width = table.shape[1]
    chunks = width // LANES
    sub = 128

    @pl.when(step < blocks)
    def _():
        def part(j, carry):
            start = pl.multiple_of(j * sub, sub)
            pre = jnp.dot(table[pl.ds(start, sub), :], query[...], preferred_element_type=F32) + bias[...]
            tiny = jnp.finfo(BF16).tiny
            kept = jnp.where(pre > 0, jnp.maximum(pre, tiny), 0.0).astype(BF16)
            hidden[pl.ds(start, sub), :] = kept
            wide = kept.astype(F32)
            base = (step * ROW_BLOCK + start) * SUBLANES
            for g in range(sub // SUBLANES):
                for c in range(chunks):
                    hidden_rows[pl.ds(base + g * SUBLANES * SUBLANES + c, SUBLANES, stride=SUBLANES), :] = wide[
                        g * SUBLANES : (g + 1) * SUBLANES, c * LANES : (c + 1) * LANES
                    ]
            return carry

        lax.fori_loop(0, ROW_BLOCK // sub, part, 0)

    @pl.when(step >= blocks)
    def _():
        device = step - blocks
        targets = pooled.shape[0]
        clear_rows(pooled_rows, targets)

        def entry(k):
            code = codes[0, 0, k]
            node = lax.shift_right_logical(code, 8)
            target = code & (SHIFT - 1)
            put_row(
                pooled_rows,
                target,
                row_at(pooled_rows, target) + shares[0, 0, k] * row_at(hidden_rows, node),
            )

        walk(bounds[device, 0], bounds[device, 1], entry)

        def part(g, carry):
            for c in range(chunks):
                pooled[
                    pl.ds(pl.multiple_of(g * SUBLANES, SUBLANES), SUBLANES), c * LANES : (c + 1) * LANES
                ] = pooled_rows[pl.ds(g * SUBLANES * SUBLANES + c, SUBLANES, stride=SUBLANES), :]
            return carry

        lax.fori_loop(0, targets // SUBLANES, part, 0)


def owner_forward(table, query, bias, codes, shares, bounds, targets):
    rows, width = table.shape
    blocks = rows // ROW_BLOCK
    devices, _, length = codes.shape
    return pl.pallas_call(
        functools.partial(forward_kernel, blocks),
        grid_spec=pltpu.PrefetchScalarGridSpec(
            num_scalar_prefetch=1,
            grid=(blocks + devices,),
            in_specs=[
                pl.BlockSpec((ROW_BLOCK, width), lambda i, b: (jnp.minimum(i, blocks - 1), 0)),
                pl.BlockSpec((width, width), lambda i, b: (0, 0)),
                pl.BlockSpec((1, width), lambda i, b: (0, 0)),
                pl.BlockSpec(
                    (1, 1, length),
                    lambda i, b: (jnp.maximum(i - blocks, 0), 0, 0),
                    memory_space=pltpu.SMEM,
                ),
                pl.BlockSpec(
                    (1, 1, length),
                    lambda i, b: (jnp.maximum(i - blocks, 0), 0, 0),
                    memory_space=pltpu.SMEM,
                ),
            ],
            out_specs=[
                pl.BlockSpec((ROW_BLOCK, width), lambda i, b: (jnp.minimum(i, blocks - 1), 0)),
                pl.BlockSpec((targets, width), lambda i, b: (jnp.maximum(i - blocks, 0), 0)),
            ],
            scratch_shapes=[
                pltpu.VMEM((rows * SUBLANES, LANES), F32),
                pltpu.VMEM((targets * SUBLANES, LANES), F32),
            ],
        ),
        out_shape=[
            jax.ShapeDtypeStruct((rows, width), BF16),
            jax.ShapeDtypeStruct((devices * targets, width), F32),
        ],
        compiler_params=pltpu.CompilerParams(vmem_limit_bytes=VMEM_BYTES),
        cost_estimate=pl.CostEstimate(
            flops=2 * rows * width * width, bytes_accessed=4 * rows * width, transcendentals=0
        ),
        name="owner_forward",
    )(bounds, table, query, bias.reshape(1, width), codes, shares)


def backward_kernel(
    requesters, place, bounds, codes, shares, grads, hidden, table, grad_pre, weight_grad, bias_grad, total, rows_here
):
    step = pl.program_id(0)
    targets, width = grads.shape
    chunks = width // LANES
    tile = SUBLANES * SUBLANES

    @pl.when(step == 0)
    def _():
        clear_rows(total, total.shape[0] // SUBLANES)

    @pl.when(step < requesters)
    def _():
        def spread(g, carry):
            both = grads[pl.ds(pl.multiple_of(g * 16, 16), 16), :].astype(F32)
            for h in range(2):
                for c in range(chunks):
                    rows_here[pl.ds((g * 2 + h) * tile + c, SUBLANES, stride=SUBLANES), :] = both[
                        h * SUBLANES : (h + 1) * SUBLANES, c * LANES : (c + 1) * LANES
                    ]
            return carry

        lax.fori_loop(0, targets // 16, spread, 0)

        def entry(k):
            code = codes[0, 0, k]
            node = lax.shift_right_logical(code, 8)
            target = code & (SHIFT - 1)
            put_row(total, node, row_at(total, node) + shares[0, 0, k] * row_at(rows_here, target))

        walk(bounds[step, 0], bounds[step, 1], entry)

    @pl.when(step == requesters)
    def _():
        weight_grad[...] = jnp.zeros_like(weight_grad)
        bias_grad[...] = jnp.zeros_like(bias_grad)

    @pl.when(step >= requesters)
    def _():
        base = (step - requesters) * ROW_BLOCK // SUBLANES

        def part(g, carry):
            where = pl.ds(pl.multiple_of(g * 16, 16), 16)
            for c in range(chunks):
                lane = slice(c * LANES, (c + 1) * LANES)
                halves = [
                    total[pl.ds((base + g * 2 + h) * tile + c, SUBLANES, stride=SUBLANES), :] for h in range(2)
                ]
                both = jnp.where(
                    hidden[where, lane].astype(F32) > 0, jnp.concatenate(halves, axis=0), 0.0
                )
                grad_pre[where, lane] = both.astype(BF16)
                bias_grad[:, lane] += both[:SUBLANES] + both[SUBLANES:]
            return carry

        lax.fori_loop(0, ROW_BLOCK // 16, part, 0)
        weight_grad[...] += lax.dot_general(
            table[...], grad_pre[...], (((0,), (0,)), ((), ())), preferred_element_type=F32
        )


def owner_backward(table, hidden, grads, codes, shares, bounds, place, groups, targets):
    rows, width = table.shape
    blocks = rows // ROW_BLOCK
    requesters, _, length = codes.shape
    owners = requesters // groups
    part = width // groups

    def node_block(i, place, bounds):
        return (jnp.maximum(i - requesters, 0), 0)

    def list_block(i, place, bounds):
        return (jnp.minimum(i, requesters - 1), 0, 0)

    def grad_block(i, place, bounds):
        k = jnp.minimum(i, requesters - 1)
        return (lax.rem(k, owners) * groups + lax.div(k, owners), 0)

    return pl.pallas_call(
        functools.partial(backward_kernel, requesters),
        grid_spec=pltpu.PrefetchScalarGridSpec(
            num_scalar_prefetch=2,
            grid=(requesters + blocks,),
            in_specs=[
                pl.BlockSpec((1, 1, length), list_block, memory_space=pltpu.SMEM),
                pl.BlockSpec((1, 1, length), list_block, memory_space=pltpu.SMEM),
                pl.BlockSpec((targets, width), grad_block),
                pl.BlockSpec((ROW_BLOCK, width), node_block),
                pl.BlockSpec(
                    (ROW_BLOCK, part), lambda i, place, bounds: (jnp.maximum(i - requesters, 0), place[0])
                ),
            ],
            out_specs=[
                pl.BlockSpec((ROW_BLOCK, width), node_block),
                pl.BlockSpec((part, width), lambda i, place, bounds: (0, 0)),
                pl.BlockSpec((SUBLANES, width), lambda i, place, bounds: (0, 0)),
            ],
            scratch_shapes=[
                pltpu.VMEM((rows * SUBLANES, LANES), F32),
                pltpu.VMEM((targets * SUBLANES, LANES), F32),
            ],
        ),
        out_shape=[
            jax.ShapeDtypeStruct((rows, width), BF16),
            jax.ShapeDtypeStruct((part, width), F32),
            jax.ShapeDtypeStruct((SUBLANES, width), F32),
        ],
        compiler_params=pltpu.CompilerParams(vmem_limit_bytes=VMEM_BYTES),
        cost_estimate=pl.CostEstimate(
            flops=2 * rows * width * width * 2, bytes_accessed=6 * rows * width, transcendentals=0
        ),
        name="owner_backward",
    )(place, bounds, codes, shares, grads, hidden, table)


def table_kernel(requesters, place, bounds, codes, grad_mixed, mix, grad_pre, query, out, bias_grad, self_total, here):
    step = pl.program_id(0)
    targets = grad_mixed.shape[0]

    @pl.when(step == 0)
    def _():
        self_total[...] = jnp.zeros_like(self_total)
        bias_grad[...] = jnp.zeros_like(bias_grad)

    @pl.when(step < requesters)
    def _():
        here[...] = lax.dot_general(
            grad_mixed[...], mix[...], (((1,), (1,)), ((), ())), preferred_element_type=F32
        )
        sums = grad_mixed[...].astype(F32).reshape(targets // SUBLANES, SUBLANES, grad_mixed.shape[1])
        bias_grad[...] += jnp.sum(sums, axis=0)

        def entry(k):
            code = codes[0, 0, k]
            node = lax.shift_right_logical(code, 8)
            target = code & (SHIFT - 1)
            self_total[pl.ds(node, 1), :] += here[pl.ds(target, 1), :]

        walk(bounds[step, 2], bounds[step, 3], entry)

    @pl.when(step >= requesters)
    def _():
        start = pl.multiple_of((step - requesters) * ROW_BLOCK, ROW_BLOCK)
        out[...] = self_total[pl.ds(start, ROW_BLOCK), :] + lax.dot_general(
            grad_pre[...], query[...], (((1,), (1,)), ((), ())), preferred_element_type=F32
        )


def owner_table_grad(grad_mixed, mix, grad_pre, query, codes, bounds, place, groups, targets):
    rows, width = grad_pre.shape
    blocks = rows // ROW_BLOCK
    requesters, _, length = codes.shape
    owners = requesters // groups
    part = width // groups

    def grad_block(i, place, bounds):
        k = jnp.minimum(i, requesters - 1)
        return (lax.rem(k, owners) * groups + lax.div(k, owners), 0)

    return pl.pallas_call(
        functools.partial(table_kernel, requesters),
        grid_spec=pltpu.PrefetchScalarGridSpec(
            num_scalar_prefetch=2,
            grid=(requesters + blocks,),
            in_specs=[
                pl.BlockSpec(
                    (1, 1, length),
                    lambda i, place, bounds: (jnp.minimum(i, requesters - 1), 0, 0),
                    memory_space=pltpu.SMEM,
                ),
                pl.BlockSpec((targets, width), grad_block),
                pl.BlockSpec((part, width), lambda i, place, bounds: (place[0], 0)),
                pl.BlockSpec((ROW_BLOCK, width), lambda i, place, bounds: (jnp.maximum(i - requesters, 0), 0)),
                pl.BlockSpec((part, width), lambda i, place, bounds: (place[0], 0)),
            ],
            out_specs=[
                pl.BlockSpec((ROW_BLOCK, part), lambda i, place, bounds: (jnp.maximum(i - requesters, 0), 0)),
                pl.BlockSpec((SUBLANES, width), lambda i, place, bounds: (0, 0)),
            ],
            scratch_shapes=[pltpu.VMEM((rows, part), F32), pltpu.VMEM((targets, part), F32)],
        ),
        out_shape=[
            jax.ShapeDtypeStruct((rows, part), F32),
            jax.ShapeDtypeStruct((SUBLANES, width), F32),
        ],
        compiler_params=pltpu.CompilerParams(vmem_limit_bytes=VMEM_BYTES),
        cost_estimate=pl.CostEstimate(
            flops=2 * rows * width * part, bytes_accessed=8 * rows * part, transcendentals=0
        ),
        name="owner_table_grad",
    )(place, bounds, codes, grad_mixed, mix, grad_pre, query)


def padded(values, length):
    return jnp.pad(values, (0, length - values.shape[0]))


def local(
    feature_table,
    neighbour_query_weight,
    query_bias,
    mix_weight,
    mix_bias,
    lookup_ids,
    present_counts,
    importance,
    embed_cot,
):
    owners = lax.axis_size("table")
    groups = lax.axis_size("rep")
    devices = owners * groups
    rows_owned, width = feature_table.shape
    batch_rows, slot_count = lookup_ids.shape
    near = slot_count - 1
    owner = lax.axis_index("table").astype(I32)
    group = lax.axis_index("rep").astype(I32)

    own_ids = lax.all_gather(lookup_ids[:, 0], "table", axis=0, tiled=True)
    wanted = own_ids - owner * rows_owned
    mine = (wanted >= 0) & (wanted < rows_owned)
    found = feature_table[jnp.clip(wanted, 0, rows_owned - 1)]
    found = jnp.where(mine[:, None], found, jnp.zeros((), BF16))
    self_rows = lax.psum_scatter(found, "table", scatter_dimension=0, tiled=True)

    present = (jnp.arange(near, dtype=I32)[None, :] < present_counts[:, None]).astype(F32)
    masked_weight = importance * present
    shares = lax.reduce_precision(masked_weight / jnp.sum(masked_weight, axis=1, keepdims=True), 8, 7)
    live_most = batch_rows // 2 * (near + 5)
    length = -(-live_most // LANES) * LANES
    target = jnp.arange(batch_rows, dtype=I32)
    keys = jnp.where(present > 0, lookup_ids[:, 1:] * SHIFT + target[:, None], jnp.iinfo(I32).max)
    keys, sorted_shares = lax.sort((keys.reshape(-1), shares.reshape(-1)), num_keys=1, is_stable=False)
    keys = keys[:live_most]
    sorted_shares = sorted_shares[:live_most]
    own_keys = lax.sort(lookup_ids[:, 0] * SHIFT + target)
    edges = jnp.arange(owners + 1, dtype=I32) * (rows_owned * SHIFT)
    starts = jnp.sum((keys[None, :] < edges[:, None]).astype(I32), axis=1)
    own_starts = jnp.sum((own_keys[None, :] < edges[:, None]).astype(I32), axis=1)
    own_length = SHIFT
    meta = jnp.concatenate(
        [
            starts.astype(F32),
            own_starts.astype(F32),
            jnp.stack([jnp.sum(present), jnp.sum(masked_weight)]),
        ]
    )
    meta_length = -(-meta.shape[0] // LANES) * LANES

    def as_code(key):
        return (key % (rows_owned * SHIFT)).astype(F32)

    request = jnp.concatenate(
        [
            padded(as_code(keys), length),
            padded(sorted_shares, length),
            padded(as_code(own_keys), own_length),
            padded(meta, meta_length),
        ]
    )
    request, _ = lax.optimization_barrier((request, found))
    plane = lax.all_gather(request, "table", axis=0)
    every = lax.all_gather(plane, "rep", axis=0).reshape(devices, -1)

    def unpack(lists):
        count = lists.shape[0]
        at = 2 * length
        codes = lists[:, :length].astype(I32).reshape(count, 1, length)
        parts = lists[:, length:at].reshape(count, 1, length)
        own_codes = lists[:, at : at + own_length].astype(I32).reshape(count, 1, own_length)
        notes = lists[:, at + own_length :]
        first = lax.dynamic_slice(notes, (0, owner), (count, 2))
        own_first = lax.dynamic_slice(notes, (0, owner + owners + 1), (count, 2))
        bounds = jnp.concatenate([first, own_first], axis=1).astype(I32)
        sums = jnp.sum(notes[:, 2 * (owners + 1) : 2 * (owners + 1) + 2], axis=0)
        return codes, parts, own_codes, bounds, sums

    codes, parts, _, bounds, _ = unpack(plane)
    hidden, pooled_parts = owner_forward(
        feature_table, neighbour_query_weight, query_bias, codes, parts, bounds, batch_rows
    )
    pooled_parts, self_rows = lax.optimization_barrier((pooled_parts, self_rows))
    pooled = lax.psum_scatter(pooled_parts, "table", scatter_dimension=0, tiled=True)
    pooled = lax.reduce_precision(pooled, 8, 7).astype(BF16)

    joined = jnp.concatenate([self_rows, pooled], axis=1)
    mixed = jnp.dot(joined, mix_weight, preferred_element_type=F32) + mix_bias
    activation = jax.nn.relu(mixed)
    inverse = lax.rsqrt(jnp.mean(activation * activation, axis=1, keepdims=True) + 1e-06)
    embed = (activation * inverse).astype(BF16)
    cotangent = embed_cot.astype(F32)
    grad_act = inverse * cotangent - activation * (inverse * inverse * inverse) * jnp.mean(
        activation * cotangent, axis=1, keepdims=True
    )
    grad_mixed = jnp.where(mixed > 0, grad_act, 0.0).astype(BF16)
    grad_pooled = lax.dot_general(
        grad_mixed, mix_weight[width:], (((1,), (1,)), ((), ())), preferred_element_type=F32
    ).astype(BF16)
    all_pooled = lax.all_gather(grad_pooled, ("table", "rep"), axis=0, tiled=True)
    all_mixed = lax.all_gather(grad_mixed, ("table", "rep"), axis=0, tiled=True)
    mix_part = 2 * width // devices
    columns = lax.all_to_all(
        joined.reshape(batch_rows, devices, mix_part).transpose(1, 0, 2),
        ("table", "rep"),
        split_axis=0,
        concat_axis=0,
        tiled=True,
    ).reshape(devices * batch_rows, mix_part)

    all_codes, all_parts, all_own_codes, all_bounds, sums = unpack(every)
    place = group.reshape(1)
    grad_pre, query_part, query_bias_part = owner_backward(
        feature_table, hidden, all_pooled, all_codes, all_parts, all_bounds, place, groups, batch_rows
    )
    table_grad, mix_bias_part = owner_table_grad(
        all_mixed, mix_weight, grad_pre, neighbour_query_weight, all_own_codes, all_bounds, place, groups, batch_rows
    )

    query_rows = width // devices
    bias_rows = 16
    outgoing = jnp.concatenate(
        [
            query_part.reshape(owners, query_rows, width),
            jnp.broadcast_to(
                jnp.pad(jnp.sum(query_bias_part, axis=0, keepdims=True), ((0, bias_rows - 1), (0, 0)))[None],
                (owners, bias_rows, width),
            ),
        ],
        axis=1,
    ).astype(BF16)
    summed = jnp.sum(
        lax.all_to_all(outgoing, "table", split_axis=0, concat_axis=0, tiled=True).astype(F32), axis=0
    )
    query_bias_grad = summed[query_rows]
    mix_rows = lax.dot_general(
        columns, all_mixed, (((0,), (0,)), ((), ())), preferred_element_type=F32
    )
    gathered = lax.all_gather(
        jnp.concatenate([summed[:query_rows], mix_rows], axis=0).astype(BF16), ("table", "rep"), axis=0
    ).reshape(owners, groups, query_rows + mix_part, width)
    query_weight_grad = (
        gathered[:, :, :query_rows].transpose(1, 0, 2, 3).reshape(width, width).astype(F32)
    )
    mix_weight_grad = gathered[:, :, query_rows:].reshape(2 * width, width).astype(F32)
    mix_bias_grad = jnp.sum(mix_bias_part, axis=0)
    statistics = sums / (batch_rows * devices)
    return (
        embed,
        table_grad,
        query_weight_grad,
        query_bias_grad,
        mix_weight_grad,
        mix_bias_grad,
        statistics,
    )


def solution(mesh):
    in_specs = (
        P("table", None),
        P(),
        P(),
        P(),
        P(),
        P(("table", "rep"), None),
        P(("table", "rep")),
        P(("table", "rep"), None),
        P(("table", "rep"), None),
    )
    out_specs = (P(("table", "rep"), None), P("table", "rep"), P(), P(), P(), P(), P())
    return jax.shard_map(local, mesh=mesh, in_specs=in_specs, out_specs=out_specs, check_vma=False)
```

```python
import functools

import jax
import jax.numpy as jnp
from jax import lax
from jax.experimental import pallas as pl
from jax.experimental.pallas import tpu as pltpu
from jax.sharding import PartitionSpec as P

F32 = jnp.float32
BF16 = jnp.bfloat16
I32 = jnp.int32
LANES = 128
SUBLANES = 8
ROW_BLOCK = 512
SHIFT = 256
PART_BLOCK = 384
WINDOW = 1536
UNROLL = 4
VMEM_BYTES = 60 << 20


def row_at(ref, row):
    return ref[pl.ds(pl.multiple_of(row * SUBLANES, SUBLANES), SUBLANES), :]


def put_row(ref, row, value):
    ref[pl.ds(pl.multiple_of(row * SUBLANES, SUBLANES), SUBLANES), :] = value


def clear_rows(ref, rows):
    zero = jnp.zeros((SUBLANES * SUBLANES, LANES), F32)

    def step(i, carry):
        ref[pl.ds(pl.multiple_of(i * SUBLANES * SUBLANES, SUBLANES), SUBLANES * SUBLANES), :] = zero
        return carry

    lax.fori_loop(0, rows // SUBLANES, step, 0)


def walk(first, last, entry):
    count = last - first
    groups = count // UNROLL

    def group(i, carry):
        for u in range(UNROLL):
            entry(first + i * UNROLL + u)
        return carry

    def single(k, carry):
        entry(k)
        return carry

    lax.fori_loop(0, groups, group, 0)
    lax.fori_loop(first + groups * UNROLL, last, single, 0)


def window_start(first, length):
    return pl.multiple_of(jnp.minimum(lax.div(first, LANES) * LANES, length - WINDOW), LANES)


def forward_kernel(blocks, length, bounds, table, query, bias, codes, shares, hidden, pooled, hidden_rows, pooled_rows):
    step = pl.program_id(0)
    width = table.shape[1]
    chunks = width // LANES
    sub = 128

    @pl.when(step < blocks)
    def _():
        def part(j, carry):
            start = pl.multiple_of(j * sub, sub)
            pre = jnp.dot(table[pl.ds(start, sub), :], query[...], preferred_element_type=F32) + bias[...]
            tiny = jnp.finfo(BF16).tiny
            kept = jnp.where(pre > 0, jnp.maximum(pre, tiny), 0.0).astype(BF16)
            hidden[pl.ds(start, sub), :] = kept
            wide = kept.astype(F32)
            base = (step * ROW_BLOCK + start) * SUBLANES
            for g in range(sub // SUBLANES):
                for c in range(chunks):
                    hidden_rows[pl.ds(base + g * SUBLANES * SUBLANES + c, SUBLANES, stride=SUBLANES), :] = wide[
                        g * SUBLANES : (g + 1) * SUBLANES, c * LANES : (c + 1) * LANES
                    ]
            return carry

        lax.fori_loop(0, ROW_BLOCK // sub, part, 0)

    @pl.when(step >= blocks)
    def _():
        device = step - blocks
        targets = pooled.shape[0]
        clear_rows(pooled_rows, targets)

        def entry(k):
            code = codes[0, 0, k]
            node = lax.shift_right_logical(code, 8)
            target = code & (SHIFT - 1)
            put_row(
                pooled_rows,
                target,
                row_at(pooled_rows, target) + shares[0, 0, k] * row_at(hidden_rows, node),
            )

        base = window_start(bounds[device, 0], length)
        walk(bounds[device, 0] - base, bounds[device, 1] - base, entry)

        def part(g, carry):
            for c in range(chunks):
                pooled[
                    pl.ds(pl.multiple_of(g * SUBLANES, SUBLANES), SUBLANES), c * LANES : (c + 1) * LANES
                ] = pooled_rows[pl.ds(g * SUBLANES * SUBLANES + c, SUBLANES, stride=SUBLANES), :]
            return carry

        lax.fori_loop(0, targets // SUBLANES, part, 0)


def owner_forward(table, query, bias, codes, shares, bounds, targets):
    rows, width = table.shape
    blocks = rows // ROW_BLOCK
    devices, _, length = codes.shape

    def list_block(i, bounds):
        k = jnp.maximum(i - blocks, 0)
        return (k, 0, window_start(bounds[k, 0], length))

    window = (pl.Element(1), pl.Element(1), pl.Element(WINDOW))
    return pl.pallas_call(
        functools.partial(forward_kernel, blocks, length),
        grid_spec=pltpu.PrefetchScalarGridSpec(
            num_scalar_prefetch=1,
            grid=(blocks + devices,),
            in_specs=[
                pl.BlockSpec((ROW_BLOCK, width), lambda i, b: (jnp.minimum(i, blocks - 1), 0)),
                pl.BlockSpec((width, width), lambda i, b: (0, 0)),
                pl.BlockSpec((1, width), lambda i, b: (0, 0)),
                pl.BlockSpec(window, list_block, memory_space=pltpu.SMEM),
                pl.BlockSpec(window, list_block, memory_space=pltpu.SMEM),
            ],
            out_specs=[
                pl.BlockSpec((ROW_BLOCK, width), lambda i, b: (jnp.minimum(i, blocks - 1), 0)),
                pl.BlockSpec((targets, width), lambda i, b: (jnp.maximum(i - blocks, 0), 0)),
            ],
            scratch_shapes=[
                pltpu.VMEM((rows * SUBLANES, LANES), F32),
                pltpu.VMEM((targets * SUBLANES, LANES), F32),
            ],
        ),
        out_shape=[
            jax.ShapeDtypeStruct((rows, width), BF16),
            jax.ShapeDtypeStruct((devices * targets, width), F32),
        ],
        compiler_params=pltpu.CompilerParams(vmem_limit_bytes=VMEM_BYTES),
        cost_estimate=pl.CostEstimate(
            flops=2 * rows * width * width, bytes_accessed=4 * rows * width, transcendentals=0
        ),
        name="owner_forward",
    )(bounds, table, query, bias.reshape(1, width), codes, shares)


def spread_rows(source, rows_here):
    targets, width = source.shape
    chunks = width // LANES
    tile = SUBLANES * SUBLANES

    def part(g, sums):
        both = source[pl.ds(pl.multiple_of(g * 16, 16), 16), :].astype(F32)
        for h in range(2):
            for c in range(chunks):
                rows_here[pl.ds((g * 2 + h) * tile + c, SUBLANES, stride=SUBLANES), :] = both[
                    h * SUBLANES : (h + 1) * SUBLANES, c * LANES : (c + 1) * LANES
                ]
        return sums + both[:SUBLANES] + both[SUBLANES:]

    return lax.fori_loop(0, targets // 16, part, jnp.zeros((SUBLANES, width), F32))


def backward_kernel(
    requesters,
    length,
    place,
    bounds,
    codes,
    shares,
    self_codes,
    grads,
    hidden,
    table,
    mix_self,
    mix_pooled,
    query,
    table_grad,
    weight_grad,
    query_bias_grad,
    mix_bias_grad,
    near_total,
    self_total,
    rows_here,
    near_sums,
    self_sums,
    weight_sum,
):
    step = pl.program_id(0)
    block, width = hidden.shape
    rows = near_total.shape[0] // SUBLANES
    chunks = width // LANES
    tile = SUBLANES * SUBLANES
    groups, _, part_width = table_grad.shape

    @pl.when(step == 0)
    def _():
        clear_rows(near_total, rows)
        clear_rows(self_total, rows)
        mix_bias_grad[...] = jnp.zeros_like(mix_bias_grad)
        query_bias_grad[...] = jnp.zeros_like(query_bias_grad)
        weight_sum[...] = jnp.zeros_like(weight_sum)

    @pl.when(step < requesters)
    def _():
        mix_bias_grad[...] += spread_rows(grads, rows_here)
        first_row = place[0] * rows

        def parts_of(code):
            return lax.shift_right_logical(code, 8) - first_row, code & (SHIFT - 1)

        base = window_start(bounds[step, 0], length)

        def entry(k):
            node, target = parts_of(codes[0, 0, k])
            put_row(near_total, node, row_at(near_total, node) + shares[0, 0, k] * row_at(rows_here, target))

        walk(bounds[step, 0] - base, bounds[step, 1] - base, entry)

        def self_entry(k):
            node, target = parts_of(self_codes[0, 0, k])
            put_row(self_total, node, row_at(self_total, node) + row_at(rows_here, target))

        walk(bounds[step, 2], bounds[step, 3], self_entry)

    @pl.when(step >= requesters)
    def _():
        base = (step - requesters) * (block // SUBLANES)

        def part(g, carry):
            where = pl.ds(pl.multiple_of(g * 16, 16), 16)
            for total, sums in ((near_total, near_sums), (self_total, self_sums)):
                for c in range(chunks):
                    halves = [
                        total[pl.ds((base + g * 2 + h) * tile + c, SUBLANES, stride=SUBLANES), :] for h in range(2)
                    ]
                    sums[where, c * LANES : (c + 1) * LANES] = jnp.concatenate(halves, axis=0).astype(BF16)
            return carry

        lax.fori_loop(0, block // 16, part, 0)
        turned = (((1,), (1,)), ((), ()))
        raw = lax.dot_general(near_sums[...], mix_pooled[...], turned, preferred_element_type=F32)
        grad_pre = jnp.where(hidden[...].astype(F32) > 0, raw, 0.0)
        query_bias_grad[...] += jnp.sum(grad_pre.reshape(block // SUBLANES, SUBLANES, width), axis=0)
        grad_pre = grad_pre.astype(BF16)
        weight_sum[...] += lax.dot_general(
            table[...], grad_pre, (((0,), (0,)), ((), ())), preferred_element_type=F32
        )
        grad = lax.dot_general(grad_pre, query[...], turned, preferred_element_type=F32) + lax.dot_general(
            self_sums[...], mix_self[...], turned, preferred_element_type=F32
        )
        for q in range(groups):
            table_grad[q] = grad[:, q * part_width : (q + 1) * part_width].astype(BF16)

    @pl.when(step == pl.num_programs(0) - 1)
    def _():
        weight_grad[...] = weight_sum[...].astype(BF16)


def owner_backward(table, hidden, grads, mix, query, codes, shares, self_codes, bounds, place, owners, groups, targets):
    rows_owned, width = table.shape
    rows = rows_owned // groups
    blocks = rows // PART_BLOCK
    requesters, _, length = codes.shape
    self_length = self_codes.shape[2]

    def requester(i):
        return jnp.minimum(i, requesters - 1)

    def node_block(i, place, bounds):
        return (place[0] * blocks + jnp.maximum(i - requesters, 0), 0)

    def list_block(i, place, bounds):
        k = requester(i)
        return (k, 0, window_start(bounds[k, 0], length))

    def grad_block(i, place, bounds):
        k = requester(i)
        return (lax.rem(k, owners) * groups + lax.div(k, owners), 0)

    def whole(shape, row=0):
        return pl.BlockSpec(shape, lambda i, place, bounds: (row, 0), pipeline_mode=pl.Buffered(1))

    window = (pl.Element(1), pl.Element(1), pl.Element(WINDOW))
    return pl.pallas_call(
        functools.partial(backward_kernel, requesters, length),
        grid_spec=pltpu.PrefetchScalarGridSpec(
            num_scalar_prefetch=2,
            grid=(requesters + blocks,),
            in_specs=[
                pl.BlockSpec(window, list_block, memory_space=pltpu.SMEM),
                pl.BlockSpec(window, list_block, memory_space=pltpu.SMEM),
                pl.BlockSpec(
                    (1, 1, self_length), lambda i, place, bounds: (requester(i), 0, 0), memory_space=pltpu.SMEM
                ),
                pl.BlockSpec((targets, width), grad_block),
                pl.BlockSpec((PART_BLOCK, width), node_block),
                pl.BlockSpec((PART_BLOCK, width), node_block),
                whole((width, width), 0),
                whole((width, width), 1),
                whole((width, width)),
            ],
            out_specs=[
                pl.BlockSpec(
                    (groups, PART_BLOCK, width // groups),
                    lambda i, place, bounds: (0, jnp.maximum(i - requesters, 0), 0),
                ),
                pl.BlockSpec((width, width), lambda i, place, bounds: (0, 0)),
                pl.BlockSpec((SUBLANES, width), lambda i, place, bounds: (0, 0)),
                pl.BlockSpec((SUBLANES, width), lambda i, place, bounds: (0, 0)),
            ],
            scratch_shapes=[
                pltpu.VMEM((rows * SUBLANES, LANES), F32),
                pltpu.VMEM((rows * SUBLANES, LANES), F32),
                pltpu.VMEM((targets * SUBLANES, LANES), F32),
                pltpu.VMEM((PART_BLOCK, width), BF16),
                pltpu.VMEM((PART_BLOCK, width), BF16),
                pltpu.VMEM((width, width), F32),
            ],
        ),
        out_shape=[
            jax.ShapeDtypeStruct((groups, rows, width // groups), BF16),
            jax.ShapeDtypeStruct((width, width), BF16),
            jax.ShapeDtypeStruct((SUBLANES, width), F32),
            jax.ShapeDtypeStruct((SUBLANES, width), F32),
        ],
        compiler_params=pltpu.CompilerParams(vmem_limit_bytes=VMEM_BYTES),
        cost_estimate=pl.CostEstimate(
            flops=8 * rows * width * width, bytes_accessed=4 * requesters * targets * width, transcendentals=0
        ),
        name="owner_backward",
    )(place, bounds, codes, shares, self_codes, grads, hidden, table, mix, mix, query)


def padded(values, length):
    return jnp.pad(values, (0, length - values.shape[0]))


def local(
    feature_table,
    neighbour_query_weight,
    query_bias,
    mix_weight,
    mix_bias,
    lookup_ids,
    present_counts,
    importance,
    embed_cot,
):
    owners = lax.axis_size("table")
    groups = lax.axis_size("rep")
    devices = owners * groups
    rows_owned, width = feature_table.shape
    batch_rows, slot_count = lookup_ids.shape
    near = slot_count - 1
    owner = lax.axis_index("table").astype(I32)
    group = lax.axis_index("rep").astype(I32)

    own_ids = lax.all_gather(lookup_ids[:, 0], "table", axis=0, tiled=True)
    wanted = own_ids - owner * rows_owned
    mine = (wanted >= 0) & (wanted < rows_owned)
    found = feature_table[jnp.clip(wanted, 0, rows_owned - 1)]
    found = jnp.where(mine[:, None], found, jnp.zeros((), BF16))
    self_rows = lax.psum_scatter(found, "table", scatter_dimension=0, tiled=True)

    present = (jnp.arange(near, dtype=I32)[None, :] < present_counts[:, None]).astype(F32)
    masked_weight = importance * present
    shares = lax.reduce_precision(masked_weight / jnp.sum(masked_weight, axis=1, keepdims=True), 8, 7)
    live_most = batch_rows // 2 * (near + 5)
    length = -(-live_most // LANES) * LANES
    target = jnp.arange(batch_rows, dtype=I32)
    keys = jnp.where(present > 0, lookup_ids[:, 1:] * SHIFT + target[:, None], jnp.iinfo(I32).max)
    keys, sorted_shares = lax.sort((keys.reshape(-1), shares.reshape(-1)), num_keys=1, is_stable=False)
    keys = keys[:live_most]
    sorted_shares = sorted_shares[:live_most]
    own_keys = lax.sort(lookup_ids[:, 0] * SHIFT + target)
    edges = jnp.arange(devices + 1, dtype=I32) * (rows_owned // groups * SHIFT)
    starts = jnp.sum((keys[None, :] < edges[:, None]).astype(I32), axis=1)
    own_starts = jnp.sum((own_keys[None, :] < edges[:, None]).astype(I32), axis=1)
    own_length = SHIFT
    meta = jnp.concatenate(
        [
            starts.astype(F32),
            own_starts.astype(F32),
            jnp.stack([jnp.sum(present), jnp.sum(masked_weight)]),
        ]
    )
    meta_length = -(-meta.shape[0] // LANES) * LANES

    def as_code(key):
        return (key % (rows_owned * SHIFT)).astype(F32)

    request = jnp.concatenate(
        [
            padded(as_code(keys), length),
            padded(sorted_shares, length),
            padded(as_code(own_keys), own_length),
            padded(meta, meta_length),
        ]
    )
    request, _ = lax.optimization_barrier((request, found))
    plane = lax.all_gather(request, "table", axis=0)
    every = lax.all_gather(plane, "rep", axis=0).reshape(devices, -1)

    def unpack(lists, start, stride):
        count = lists.shape[0]
        at = 2 * length
        codes = lists[:, :length].astype(I32).reshape(count, 1, length)
        parts = lists[:, length:at].reshape(count, 1, length)
        own_codes = lists[:, at : at + own_length].astype(I32).reshape(count, 1, own_length)
        notes = lists[:, at + own_length :]
        first = lax.dynamic_slice(notes, (0, start), (count, stride + 1))[:, ::stride]
        own_first = lax.dynamic_slice(notes, (0, start + devices + 1), (count, stride + 1))[:, ::stride]
        bounds = jnp.concatenate([first, own_first], axis=1).astype(I32)
        sums = jnp.sum(notes[:, 2 * (devices + 1) : 2 * (devices + 1) + 2], axis=0)
        return codes, parts, own_codes, bounds, sums

    codes, parts, _, bounds, _ = unpack(plane, owner * groups, groups)
    hidden, pooled_parts = owner_forward(
        feature_table, neighbour_query_weight, query_bias, codes, parts, bounds, batch_rows
    )
    pooled_parts, self_rows = lax.optimization_barrier((pooled_parts, self_rows))
    pooled = lax.psum_scatter(pooled_parts, "table", scatter_dimension=0, tiled=True)
    pooled = lax.reduce_precision(pooled, 8, 7).astype(BF16)

    joined = jnp.concatenate([self_rows, pooled], axis=1)
    mixed = jnp.dot(joined, mix_weight, preferred_element_type=F32) + mix_bias
    activation = jax.nn.relu(mixed)
    inverse = lax.rsqrt(jnp.mean(activation * activation, axis=1, keepdims=True) + 1e-06)
    embed = (activation * inverse).astype(BF16)
    cotangent = embed_cot.astype(F32)
    grad_act = inverse * cotangent - activation * (inverse * inverse * inverse) * jnp.mean(
        activation * cotangent, axis=1, keepdims=True
    )
    grad_mixed = jnp.where(mixed > 0, grad_act, 0.0).astype(BF16)
    all_mixed = lax.all_gather(grad_mixed, ("table", "rep"), axis=0, tiled=True)
    mix_part = 2 * width // devices
    columns = lax.all_to_all(
        joined.reshape(batch_rows, devices, mix_part).transpose(1, 0, 2),
        ("table", "rep"),
        split_axis=0,
        concat_axis=0,
        tiled=True,
    ).reshape(devices * batch_rows, mix_part)

    mix_rows = lax.dot_general(
        columns, all_mixed, (((0,), (0,)), ((), ())), preferred_element_type=F32
    ).astype(BF16)
    mix_weight_grad = lax.all_gather(mix_rows, ("table", "rep"), axis=0, tiled=True).astype(F32)

    all_codes, all_parts, all_own_codes, all_bounds, sums = unpack(every, owner * groups + group, 1)
    place = group.reshape(1)
    table_part, query_part, query_bias_part, mix_bias_part = owner_backward(
        feature_table,
        hidden,
        all_mixed,
        mix_weight,
        neighbour_query_weight,
        all_codes,
        all_parts,
        all_own_codes,
        all_bounds,
        place,
        owners,
        groups,
        batch_rows,
    )
    mix_bias_grad = jnp.sum(mix_bias_part, axis=0)

    query_rows = width // devices
    bias_rows = 16
    incoming = lax.all_to_all(
        query_part.reshape(devices, query_rows, width), ("table", "rep"), split_axis=0, concat_axis=0, tiled=True
    )
    summed = jnp.sum(incoming.astype(F32), axis=0)
    bias_part = jnp.pad(jnp.sum(query_bias_part, axis=0, keepdims=True), ((0, bias_rows - 1), (0, 0)))
    gathered = lax.all_gather(
        jnp.concatenate([summed, bias_part], axis=0).astype(BF16), ("table", "rep"), axis=0
    ).astype(F32)
    query_weight_grad = gathered[:, :query_rows].reshape(width, width)
    query_bias_grad = jnp.sum(gathered[:, query_rows], axis=0)
    table_grad = lax.all_to_all(table_part, "rep", split_axis=0, concat_axis=0, tiled=True)
    table_grad = table_grad.reshape(rows_owned, width // groups).astype(F32)
    statistics = sums / (batch_rows * devices)
    return (
        embed,
        table_grad,
        query_weight_grad,
        query_bias_grad,
        mix_weight_grad,
        mix_bias_grad,
        statistics,
    )


def solution(mesh):
    in_specs = (
        P("table", None),
        P(),
        P(),
        P(),
        P(),
        P(("table", "rep"), None),
        P(("table", "rep")),
        P(("table", "rep"), None),
        P(("table", "rep"), None),
    )
    out_specs = (P(("table", "rep"), None), P("table", "rep"), P(), P(), P(), P(), P())
    return jax.shard_map(local, mesh=mesh, in_specs=in_specs, out_specs=out_specs, check_vma=False)
```

```python
import functools

import jax
import jax.numpy as jnp
from jax import lax
from jax.experimental import pallas as pl
from jax.experimental.pallas import tpu as pltpu
from jax.sharding import PartitionSpec as P

F32 = jnp.float32
BF16 = jnp.bfloat16
I32 = jnp.int32
LANES = 128
SUBLANES = 8
ROW_BLOCK = 512
SHIFT = 256
SPLIT = 2
WINDOW = 1536
UNROLL = 4
VMEM_BYTES = 60 << 20


def row_at(ref, row):
    return ref[pl.ds(pl.multiple_of(row * SUBLANES, SUBLANES), SUBLANES), :]


def put_row(ref, row, value):
    ref[pl.ds(pl.multiple_of(row * SUBLANES, SUBLANES), SUBLANES), :] = value


def clear_rows(ref, rows):
    zero = jnp.zeros((SUBLANES * SUBLANES, LANES), F32)

    def step(i, carry):
        ref[pl.ds(pl.multiple_of(i * SUBLANES * SUBLANES, SUBLANES), SUBLANES * SUBLANES), :] = zero
        return carry

    lax.fori_loop(0, rows // SUBLANES, step, 0)


def walk(first, last, entry):
    count = last - first
    groups = count // UNROLL

    def group(i, carry):
        for u in range(UNROLL):
            entry(first + i * UNROLL + u)
        return carry

    def single(k, carry):
        entry(k)
        return carry

    lax.fori_loop(0, groups, group, 0)
    lax.fori_loop(first + groups * UNROLL, last, single, 0)


def window_start(first, length):
    return pl.multiple_of(jnp.minimum(lax.div(first, LANES) * LANES, length - WINDOW), LANES)


def forward_kernel(blocks, length, bounds, table, query, bias, codes, shares, hidden, pooled, hidden_rows, pooled_rows):
    step = pl.program_id(0)
    width = table.shape[1]
    chunks = width // LANES
    sub = 128

    @pl.when(step < blocks)
    def _():
        def part(j, carry):
            start = pl.multiple_of(j * sub, sub)
            pre = jnp.dot(table[pl.ds(start, sub), :], query[...], preferred_element_type=F32) + bias[...]
            tiny = jnp.finfo(BF16).tiny
            kept = jnp.where(pre > 0, jnp.maximum(pre, tiny), 0.0).astype(BF16)
            hidden[pl.ds(start, sub), :] = kept
            wide = kept.astype(F32)
            base = (step * ROW_BLOCK + start) * SUBLANES
            for g in range(sub // SUBLANES):
                for c in range(chunks):
                    hidden_rows[pl.ds(base + g * SUBLANES * SUBLANES + c, SUBLANES, stride=SUBLANES), :] = wide[
                        g * SUBLANES : (g + 1) * SUBLANES, c * LANES : (c + 1) * LANES
                    ]
            return carry

        lax.fori_loop(0, ROW_BLOCK // sub, part, 0)

    @pl.when(step >= blocks)
    def _():
        device = step - blocks
        targets = pooled.shape[0]
        clear_rows(pooled_rows, targets)

        def entry(k):
            code = codes[0, 0, k]
            node = lax.shift_right_logical(code, 8)
            target = code & (SHIFT - 1)
            put_row(
                pooled_rows,
                target,
                row_at(pooled_rows, target) + shares[0, 0, k] * row_at(hidden_rows, node),
            )

        base = window_start(bounds[device, 0], length)
        walk(bounds[device, 0] - base, bounds[device, 1] - base, entry)

        def part(g, carry):
            for c in range(chunks):
                pooled[
                    pl.ds(pl.multiple_of(g * SUBLANES, SUBLANES), SUBLANES), c * LANES : (c + 1) * LANES
                ] = pooled_rows[pl.ds(g * SUBLANES * SUBLANES + c, SUBLANES, stride=SUBLANES), :]
            return carry

        lax.fori_loop(0, targets // SUBLANES, part, 0)


def owner_forward(table, query, bias, codes, shares, bounds, targets):
    rows, width = table.shape
    blocks = rows // ROW_BLOCK
    devices, _, length = codes.shape

    def list_block(i, bounds):
        k = jnp.maximum(i - blocks, 0)
        return (k, 0, window_start(bounds[k, 0], length))

    window = (pl.Element(1), pl.Element(1), pl.Element(WINDOW))
    return pl.pallas_call(
        functools.partial(forward_kernel, blocks, length),
        grid_spec=pltpu.PrefetchScalarGridSpec(
            num_scalar_prefetch=1,
            grid=(blocks + devices,),
            in_specs=[
                pl.BlockSpec((ROW_BLOCK, width), lambda i, b: (jnp.minimum(i, blocks - 1), 0)),
                pl.BlockSpec((width, width), lambda i, b: (0, 0)),
                pl.BlockSpec((1, width), lambda i, b: (0, 0)),
                pl.BlockSpec(window, list_block, memory_space=pltpu.SMEM),
                pl.BlockSpec(window, list_block, memory_space=pltpu.SMEM),
            ],
            out_specs=[
                pl.BlockSpec((ROW_BLOCK, width), lambda i, b: (jnp.minimum(i, blocks - 1), 0)),
                pl.BlockSpec((targets, width), lambda i, b: (jnp.maximum(i - blocks, 0), 0)),
            ],
            scratch_shapes=[
                pltpu.VMEM((rows * SUBLANES, LANES), F32),
                pltpu.VMEM((targets * SUBLANES, LANES), F32),
            ],
        ),
        out_shape=[
            jax.ShapeDtypeStruct((rows, width), BF16),
            jax.ShapeDtypeStruct((devices * targets, width), F32),
        ],
        compiler_params=pltpu.CompilerParams(vmem_limit_bytes=VMEM_BYTES),
        cost_estimate=pl.CostEstimate(
            flops=2 * rows * width * width, bytes_accessed=4 * rows * width, transcendentals=0
        ),
        name="owner_forward",
    )(bounds, table, query, bias.reshape(1, width), codes, shares)


def spread_rows(source, rows_here):
    targets, width = source.shape
    chunks = width // LANES
    tile = SUBLANES * SUBLANES

    def part(g, sums):
        both = source[pl.ds(pl.multiple_of(g * 16, 16), 16), :].astype(F32)
        for h in range(2):
            for c in range(chunks):
                rows_here[pl.ds((g * 2 + h) * tile + c, SUBLANES, stride=SUBLANES), :] = both[
                    h * SUBLANES : (h + 1) * SUBLANES, c * LANES : (c + 1) * LANES
                ]
        return sums + both[:SUBLANES] + both[SUBLANES:]

    return lax.fori_loop(0, targets // 16, part, jnp.zeros((SUBLANES, width), F32))


def backward_kernel(
    requesters,
    length,
    place,
    bounds,
    codes,
    shares,
    self_codes,
    grads,
    hidden,
    table_own,
    table_other,
    self_own,
    self_other,
    mix_pooled,
    query_own,
    query_other,
    table_grad,
    table_send,
    weight_grad,
    weight_send,
    query_bias_grad,
    mix_bias_grad,
    near_total,
    self_total,
    rows_here,
    near_sums,
    self_sums,
    weight_sum,
):
    step = pl.program_id(0)
    block, width = hidden.shape
    rows = near_total.shape[0] // SUBLANES
    chunks = width // LANES
    tile = SUBLANES * SUBLANES

    @pl.when(step == 0)
    def _():
        clear_rows(near_total, rows)
        clear_rows(self_total, rows)
        mix_bias_grad[...] = jnp.zeros_like(mix_bias_grad)
        query_bias_grad[...] = jnp.zeros_like(query_bias_grad)
        weight_grad[...] = jnp.zeros_like(weight_grad)
        weight_sum[...] = jnp.zeros_like(weight_sum)

    @pl.when(step < requesters)
    def _():
        mix_bias_grad[...] += spread_rows(grads, rows_here)
        first_row = lax.rem(place[0], SPLIT) * rows

        def parts_of(code):
            return lax.shift_right_logical(code, 8) - first_row, code & (SHIFT - 1)

        base = window_start(bounds[step, 0], length)

        def entry(k):
            node, target = parts_of(codes[0, 0, k])
            put_row(near_total, node, row_at(near_total, node) + shares[0, 0, k] * row_at(rows_here, target))

        walk(bounds[step, 0] - base, bounds[step, 1] - base, entry)

        def self_entry(k):
            node, target = parts_of(self_codes[0, 0, k])
            put_row(self_total, node, row_at(self_total, node) + row_at(rows_here, target))

        walk(bounds[step, 2], bounds[step, 3], self_entry)

    @pl.when(step >= requesters)
    def _():
        base = (step - requesters) * (block // SUBLANES)

        def part(g, carry):
            where = pl.ds(pl.multiple_of(g * 16, 16), 16)
            for total, sums in ((near_total, near_sums), (self_total, self_sums)):
                for c in range(chunks):
                    halves = [
                        total[pl.ds((base + g * 2 + h) * tile + c, SUBLANES, stride=SUBLANES), :] for h in range(2)
                    ]
                    sums[where, c * LANES : (c + 1) * LANES] = jnp.concatenate(halves, axis=0).astype(BF16)
            return carry

        lax.fori_loop(0, block // 16, part, 0)
        turned = (((1,), (1,)), ((), ()))
        raw = lax.dot_general(near_sums[...], mix_pooled[...], turned, preferred_element_type=F32)
        grad_pre = jnp.where(hidden[...].astype(F32) > 0, raw, 0.0)
        query_bias_grad[...] += jnp.sum(grad_pre.reshape(block // SUBLANES, SUBLANES, width), axis=0)
        grad_pre = grad_pre.astype(BF16)
        down = (((0,), (0,)), ((), ()))
        weight_grad[...] += lax.dot_general(table_own[...], grad_pre, down, preferred_element_type=F32)
        weight_sum[...] += lax.dot_general(table_other[...], grad_pre, down, preferred_element_type=F32)
        table_grad[...] = lax.dot_general(
            grad_pre, query_own[...], turned, preferred_element_type=F32
        ) + lax.dot_general(self_sums[...], self_own[...], turned, preferred_element_type=F32)
        table_send[...] = (
            lax.dot_general(grad_pre, query_other[...], turned, preferred_element_type=F32)
            + lax.dot_general(self_sums[...], self_other[...], turned, preferred_element_type=F32)
        ).astype(BF16)

    @pl.when(step == pl.num_programs(0) - 1)
    def _():
        weight_send[...] = weight_sum[...].astype(BF16)


def owner_backward(table, hidden, grads, mix, query, codes, shares, self_codes, bounds, place, owners, groups, targets):
    rows_owned, width = table.shape
    rows = rows_owned // SPLIT
    blocks = rows // ROW_BLOCK
    requesters, _, length = codes.shape
    self_length = self_codes.shape[2]
    part = width // groups

    def requester(i):
        return jnp.minimum(i, requesters - 1)

    def node_row(i, place):
        return lax.rem(place[0], SPLIT) * blocks + jnp.maximum(i - requesters, 0)

    def list_block(i, place, bounds):
        k = requester(i)
        return (k, 0, window_start(bounds[k, 0], length))

    def grad_block(i, place, bounds):
        k = requester(i)
        return (lax.rem(k, owners) * groups + lax.div(k, owners), 0)

    def weights(which):
        return pl.BlockSpec(
            (part, width), lambda i, place, bounds: (place[which], 0), pipeline_mode=pl.Buffered(1)
        )

    def table_columns(which):
        return pl.BlockSpec((ROW_BLOCK, part), lambda i, place, bounds: (node_row(i, place), place[which]))

    def fixed(shape):
        return pl.BlockSpec(shape, lambda i, place, bounds: (0, 0))

    window = (pl.Element(1), pl.Element(1), pl.Element(WINDOW))
    return pl.pallas_call(
        functools.partial(backward_kernel, requesters, length),
        grid_spec=pltpu.PrefetchScalarGridSpec(
            num_scalar_prefetch=2,
            grid=(requesters + blocks,),
            in_specs=[
                pl.BlockSpec(window, list_block, memory_space=pltpu.SMEM),
                pl.BlockSpec(window, list_block, memory_space=pltpu.SMEM),
                pl.BlockSpec(
                    (1, 1, self_length), lambda i, place, bounds: (requester(i), 0, 0), memory_space=pltpu.SMEM
                ),
                pl.BlockSpec((targets, width), grad_block),
                pl.BlockSpec((ROW_BLOCK, width), lambda i, place, bounds: (node_row(i, place), 0)),
                table_columns(0),
                table_columns(1),
                weights(0),
                weights(1),
                pl.BlockSpec((width, width), lambda i, place, bounds: (1, 0), pipeline_mode=pl.Buffered(1)),
                weights(0),
                weights(1),
            ],
            out_specs=[
                pl.BlockSpec((ROW_BLOCK, part), lambda i, place, bounds: (node_row(i, place), 0)),
                pl.BlockSpec((ROW_BLOCK, part), lambda i, place, bounds: (jnp.maximum(i - requesters, 0), 0)),
                fixed((part, width)),
                fixed((part, width)),
                fixed((SUBLANES, width)),
                fixed((SUBLANES, width)),
            ],
            scratch_shapes=[
                pltpu.VMEM((rows * SUBLANES, LANES), F32),
                pltpu.VMEM((rows * SUBLANES, LANES), F32),
                pltpu.VMEM((targets * SUBLANES, LANES), F32),
                pltpu.VMEM((ROW_BLOCK, width), BF16),
                pltpu.VMEM((ROW_BLOCK, width), BF16),
                pltpu.VMEM((part, width), F32),
            ],
        ),
        out_shape=[
            jax.ShapeDtypeStruct((rows_owned, part), F32),
            jax.ShapeDtypeStruct((rows, part), BF16),
            jax.ShapeDtypeStruct((part, width), F32),
            jax.ShapeDtypeStruct((part, width), BF16),
            jax.ShapeDtypeStruct((SUBLANES, width), F32),
            jax.ShapeDtypeStruct((SUBLANES, width), F32),
        ],
        compiler_params=pltpu.CompilerParams(vmem_limit_bytes=VMEM_BYTES),
        cost_estimate=pl.CostEstimate(
            flops=8 * rows * width * width, bytes_accessed=4 * requesters * targets * width, transcendentals=0
        ),
        name="owner_backward",
    )(
        place,
        bounds,
        codes,
        shares,
        self_codes,
        grads,
        hidden,
        table,
        table,
        mix,
        mix,
        mix,
        query,
        query,
    )


def padded(values, length):
    return jnp.pad(values, (0, length - values.shape[0]))


def local(
    feature_table,
    neighbour_query_weight,
    query_bias,
    mix_weight,
    mix_bias,
    lookup_ids,
    present_counts,
    importance,
    embed_cot,
):
    owners = lax.axis_size("table")
    groups = lax.axis_size("rep")
    devices = owners * groups
    rows_owned, width = feature_table.shape
    batch_rows, slot_count = lookup_ids.shape
    near = slot_count - 1
    owner = lax.axis_index("table").astype(I32)
    group = lax.axis_index("rep").astype(I32)

    own_ids = lax.all_gather(lookup_ids[:, 0], "table", axis=0, tiled=True)
    wanted = own_ids - owner * rows_owned
    mine = (wanted >= 0) & (wanted < rows_owned)
    found = feature_table[jnp.clip(wanted, 0, rows_owned - 1)]
    found = jnp.where(mine[:, None], found, jnp.zeros((), BF16))
    self_rows = lax.psum_scatter(found, "table", scatter_dimension=0, tiled=True)

    present = (jnp.arange(near, dtype=I32)[None, :] < present_counts[:, None]).astype(F32)
    masked_weight = importance * present
    shares = lax.reduce_precision(masked_weight / jnp.sum(masked_weight, axis=1, keepdims=True), 8, 7)
    live_most = batch_rows // 2 * (near + 5)
    length = -(-live_most // LANES) * LANES
    target = jnp.arange(batch_rows, dtype=I32)
    keys = jnp.where(present > 0, lookup_ids[:, 1:] * SHIFT + target[:, None], jnp.iinfo(I32).max)
    keys, sorted_shares = lax.sort((keys.reshape(-1), shares.reshape(-1)), num_keys=1, is_stable=False)
    keys = keys[:live_most]
    sorted_shares = sorted_shares[:live_most]
    own_keys = lax.sort(lookup_ids[:, 0] * SHIFT + target)
    edges = jnp.arange(owners * SPLIT + 1, dtype=I32) * (rows_owned // SPLIT * SHIFT)
    starts = jnp.sum((keys[None, :] < edges[:, None]).astype(I32), axis=1)
    own_starts = jnp.sum((own_keys[None, :] < edges[:, None]).astype(I32), axis=1)
    own_length = SHIFT
    meta = jnp.concatenate(
        [
            starts.astype(F32),
            own_starts.astype(F32),
            jnp.stack([jnp.sum(present), jnp.sum(masked_weight)]),
        ]
    )
    meta_length = -(-meta.shape[0] // LANES) * LANES

    def as_code(key):
        return (key % (rows_owned * SHIFT)).astype(F32)

    request = jnp.concatenate(
        [
            padded(as_code(keys), length),
            padded(sorted_shares, length),
            padded(as_code(own_keys), own_length),
            padded(meta, meta_length),
        ]
    )
    request, _ = lax.optimization_barrier((request, found))
    plane = lax.all_gather(request, "table", axis=0)
    every = lax.all_gather(plane, "rep", axis=0).reshape(devices, -1)

    def unpack(lists, start, stride):
        count = lists.shape[0]
        at = 2 * length
        codes = lists[:, :length].astype(I32).reshape(count, 1, length)
        parts = lists[:, length:at].reshape(count, 1, length)
        own_codes = lists[:, at : at + own_length].astype(I32).reshape(count, 1, own_length)
        notes = lists[:, at + own_length :]
        first = lax.dynamic_slice(notes, (0, start), (count, stride + 1))[:, ::stride]
        own_first = lax.dynamic_slice(notes, (0, start + owners * SPLIT + 1), (count, stride + 1))[:, ::stride]
        bounds = jnp.concatenate([first, own_first], axis=1).astype(I32)
        sums = jnp.sum(notes[:, 2 * (owners * SPLIT + 1) : 2 * (owners * SPLIT + 2)], axis=0)
        return codes, parts, own_codes, bounds, sums

    codes, parts, _, bounds, _ = unpack(plane, owner * SPLIT, SPLIT)
    hidden, pooled_parts = owner_forward(
        feature_table, neighbour_query_weight, query_bias, codes, parts, bounds, batch_rows
    )
    pooled_parts, self_rows = lax.optimization_barrier((pooled_parts, self_rows))
    pooled = lax.psum_scatter(pooled_parts, "table", scatter_dimension=0, tiled=True)
    pooled = lax.reduce_precision(pooled, 8, 7).astype(BF16)

    joined = jnp.concatenate([self_rows, pooled], axis=1)
    mixed = jnp.dot(joined, mix_weight, preferred_element_type=F32) + mix_bias
    activation = jax.nn.relu(mixed)
    inverse = lax.rsqrt(jnp.mean(activation * activation, axis=1, keepdims=True) + 1e-06)
    embed = (activation * inverse).astype(BF16)
    cotangent = embed_cot.astype(F32)
    grad_act = inverse * cotangent - activation * (inverse * inverse * inverse) * jnp.mean(
        activation * cotangent, axis=1, keepdims=True
    )
    grad_mixed = jnp.where(mixed > 0, grad_act, 0.0).astype(BF16)
    all_mixed = lax.all_gather(grad_mixed, ("table", "rep"), axis=0, tiled=True)
    mix_part = 2 * width // devices
    columns = lax.all_to_all(
        joined.reshape(batch_rows, devices, mix_part).transpose(1, 0, 2),
        ("table", "rep"),
        split_axis=0,
        concat_axis=0,
        tiled=True,
    ).reshape(devices * batch_rows, mix_part)

    mix_rows = lax.dot_general(
        columns, all_mixed, (((0,), (0,)), ((), ())), preferred_element_type=F32
    ).astype(BF16)
    mix_weight_grad = lax.all_gather(mix_rows, ("table", "rep"), axis=0, tiled=True).astype(F32)

    half = lax.rem(group, SPLIT)
    partner = group + 1 - 2 * half
    swap = [(i, i + 1 - 2 * (i % SPLIT)) for i in range(groups)]
    all_codes, all_parts, all_own_codes, all_bounds, sums = unpack(every, owner * SPLIT + half, 1)
    table_grad, table_send, query_part, query_send, query_bias_part, mix_bias_part = owner_backward(
        feature_table,
        hidden,
        all_mixed,
        mix_weight,
        neighbour_query_weight,
        all_codes,
        all_parts,
        all_own_codes,
        all_bounds,
        jnp.stack([group, partner]),
        owners,
        groups,
        batch_rows,
    )
    mix_bias_grad = jnp.sum(mix_bias_part, axis=0)

    query_rows = width // devices
    bias_rows = 16
    query_part = query_part + lax.ppermute(query_send, "rep", swap).astype(F32)
    table_got = lax.ppermute(table_send, "rep", swap)
    incoming = lax.all_to_all(
        query_part.astype(BF16).reshape(owners, query_rows, width), "table", split_axis=0, concat_axis=0, tiled=True
    )
    summed = jnp.sum(incoming.astype(F32), axis=0)
    bias_part = jnp.pad(jnp.sum(query_bias_part, axis=0, keepdims=True), ((0, bias_rows - 1), (0, 0)))
    gathered = lax.all_gather(
        jnp.concatenate([summed, bias_part], axis=0).astype(BF16), ("table", "rep"), axis=0
    ).reshape(owners, groups, query_rows + bias_rows, width)
    query_weight_grad = (
        gathered[:, :, :query_rows].transpose(1, 0, 2, 3).reshape(width, width).astype(F32)
    )
    query_bias_grad = jnp.sum(gathered[:, :SPLIT, query_rows].astype(F32), axis=(0, 1))
    table_grad = lax.dynamic_update_slice(
        table_grad, table_got.astype(F32), ((1 - half) * (rows_owned // SPLIT), 0)
    )
    statistics = sums / (batch_rows * devices)
    return (
        embed,
        table_grad,
        query_weight_grad,
        query_bias_grad,
        mix_weight_grad,
        mix_bias_grad,
        statistics,
    )


def solution(mesh):
    in_specs = (
        P("table", None),
        P(),
        P(),
        P(),
        P(),
        P(("table", "rep"), None),
        P(("table", "rep")),
        P(("table", "rep"), None),
        P(("table", "rep"), None),
    )
    out_specs = (P(("table", "rep"), None), P("table", "rep"), P(), P(), P(), P(), P())
    return jax.shard_map(local, mesh=mesh, in_specs=in_specs, out_specs=out_specs, check_vma=False)
```

```python
import functools

import jax
import jax.numpy as jnp
from jax import lax
from jax.experimental import pallas as pl
from jax.experimental.pallas import tpu as pltpu
from jax.sharding import PartitionSpec as P

F32 = jnp.float32
BF16 = jnp.bfloat16
I32 = jnp.int32
LANES = 128
SUBLANES = 8
ROW_BLOCK = 512
SHIFT = 256
SPLIT = 2
WINDOW = 1536
UNROLL = 4
VMEM_BYTES = 60 << 20


def row_at(ref, row):
    return ref[pl.ds(pl.multiple_of(row * SUBLANES, SUBLANES), SUBLANES), :]


def put_row(ref, row, value):
    ref[pl.ds(pl.multiple_of(row * SUBLANES, SUBLANES), SUBLANES), :] = value


def clear_rows(ref, rows):
    zero = jnp.zeros((SUBLANES * SUBLANES, LANES), F32)

    def step(i, carry):
        ref[pl.ds(pl.multiple_of(i * SUBLANES * SUBLANES, SUBLANES), SUBLANES * SUBLANES), :] = zero
        return carry

    lax.fori_loop(0, rows // SUBLANES, step, 0)


def walk(first, last, entry):
    count = last - first
    groups = count // UNROLL

    def group(i, carry):
        for u in range(UNROLL):
            entry(first + i * UNROLL + u)
        return carry

    def single(k, carry):
        entry(k)
        return carry

    lax.fori_loop(0, groups, group, 0)
    lax.fori_loop(first + groups * UNROLL, last, single, 0)


def window_start(first, length):
    return pl.multiple_of(jnp.minimum(lax.div(first, LANES) * LANES, length - WINDOW), LANES)


def forward_kernel(blocks, length, bounds, table, query, bias, codes, shares, hidden, pooled, hidden_rows, pooled_rows):
    step = pl.program_id(0)
    width = table.shape[1]
    chunks = width // LANES
    sub = 128

    @pl.when(step < blocks)
    def _():
        def part(j, carry):
            start = pl.multiple_of(j * sub, sub)
            pre = jnp.dot(table[pl.ds(start, sub), :], query[...], preferred_element_type=F32) + bias[...]
            tiny = jnp.finfo(BF16).tiny
            kept = jnp.where(pre > 0, jnp.maximum(pre, tiny), 0.0).astype(BF16)
            hidden[pl.ds(start, sub), :] = kept
            wide = kept.astype(F32)
            base = (step * ROW_BLOCK + start) * SUBLANES
            for g in range(sub // SUBLANES):
                for c in range(chunks):
                    hidden_rows[pl.ds(base + g * SUBLANES * SUBLANES + c, SUBLANES, stride=SUBLANES), :] = wide[
                        g * SUBLANES : (g + 1) * SUBLANES, c * LANES : (c + 1) * LANES
                    ]
            return carry

        lax.fori_loop(0, ROW_BLOCK // sub, part, 0)

    @pl.when(step >= blocks)
    def _():
        device = step - blocks
        targets = pooled.shape[0]
        clear_rows(pooled_rows, targets)

        def entry(k):
            code = codes[0, 0, k]
            node = lax.shift_right_logical(code, 8)
            target = code & (SHIFT - 1)
            put_row(
                pooled_rows,
                target,
                row_at(pooled_rows, target) + shares[0, 0, k] * row_at(hidden_rows, node),
            )

        base = window_start(bounds[device, 0], length)
        walk(bounds[device, 0] - base, bounds[device, 1] - base, entry)

        def part(g, carry):
            for c in range(chunks):
                pooled[
                    pl.ds(pl.multiple_of(g * SUBLANES, SUBLANES), SUBLANES), c * LANES : (c + 1) * LANES
                ] = pooled_rows[pl.ds(g * SUBLANES * SUBLANES + c, SUBLANES, stride=SUBLANES), :]
            return carry

        lax.fori_loop(0, targets // SUBLANES, part, 0)


def owner_forward(table, query, bias, codes, shares, bounds, targets):
    rows, width = table.shape
    blocks = rows // ROW_BLOCK
    devices, _, length = codes.shape

    def list_block(i, bounds):
        k = jnp.maximum(i - blocks, 0)
        return (k, 0, window_start(bounds[k, 0], length))

    window = (pl.Element(1), pl.Element(1), pl.Element(WINDOW))
    return pl.pallas_call(
        functools.partial(forward_kernel, blocks, length),
        grid_spec=pltpu.PrefetchScalarGridSpec(
            num_scalar_prefetch=1,
            grid=(blocks + devices,),
            in_specs=[
                pl.BlockSpec((ROW_BLOCK, width), lambda i, b: (jnp.minimum(i, blocks - 1), 0)),
                pl.BlockSpec((width, width), lambda i, b: (0, 0)),
                pl.BlockSpec((1, width), lambda i, b: (0, 0)),
                pl.BlockSpec(window, list_block, memory_space=pltpu.SMEM),
                pl.BlockSpec(window, list_block, memory_space=pltpu.SMEM),
            ],
            out_specs=[
                pl.BlockSpec((ROW_BLOCK, width), lambda i, b: (jnp.minimum(i, blocks - 1), 0)),
                pl.BlockSpec((targets, width), lambda i, b: (jnp.maximum(i - blocks, 0), 0)),
            ],
            scratch_shapes=[
                pltpu.VMEM((rows * SUBLANES, LANES), F32),
                pltpu.VMEM((targets * SUBLANES, LANES), F32),
            ],
        ),
        out_shape=[
            jax.ShapeDtypeStruct((rows, width), BF16),
            jax.ShapeDtypeStruct((devices * targets, width), F32),
        ],
        compiler_params=pltpu.CompilerParams(vmem_limit_bytes=VMEM_BYTES),
        cost_estimate=pl.CostEstimate(
            flops=2 * rows * width * width, bytes_accessed=4 * rows * width, transcendentals=0
        ),
        name="owner_forward",
    )(bounds, table, query, bias.reshape(1, width), codes, shares)


def spread_rows(source, rows_here):
    targets, width = source.shape
    chunks = width // LANES
    tile = SUBLANES * SUBLANES

    def part(g, sums):
        both = source[pl.ds(pl.multiple_of(g * 16, 16), 16), :].astype(F32)
        for h in range(2):
            for c in range(chunks):
                rows_here[pl.ds((g * 2 + h) * tile + c, SUBLANES, stride=SUBLANES), :] = both[
                    h * SUBLANES : (h + 1) * SUBLANES, c * LANES : (c + 1) * LANES
                ]
        return sums + both[:SUBLANES] + both[SUBLANES:]

    return lax.fori_loop(0, targets // 16, part, jnp.zeros((SUBLANES, width), F32))


def backward_kernel(
    requesters,
    length,
    place,
    bounds,
    codes,
    shares,
    self_codes,
    grads,
    hidden,
    table_own,
    table_other,
    self_own,
    self_other,
    mix_pooled,
    query_own,
    query_other,
    table_grad,
    send_first,
    send_last,
    weight_grad,
    weight_send,
    query_bias_grad,
    mix_bias_grad,
    near_total,
    self_total,
    rows_here,
    near_sums,
    self_sums,
    weight_sum,
):
    step = pl.program_id(0)
    block, width = hidden.shape
    rows = near_total.shape[0] // SUBLANES
    chunks = width // LANES
    tile = SUBLANES * SUBLANES

    @pl.when(step == 0)
    def _():
        clear_rows(near_total, rows)
        clear_rows(self_total, rows)
        mix_bias_grad[...] = jnp.zeros_like(mix_bias_grad)
        query_bias_grad[...] = jnp.zeros_like(query_bias_grad)
        weight_grad[...] = jnp.zeros_like(weight_grad)
        weight_sum[...] = jnp.zeros_like(weight_sum)

    @pl.when(step < requesters)
    def _():
        mix_bias_grad[...] += spread_rows(grads, rows_here)
        first_row = lax.rem(place[0], SPLIT) * rows

        def parts_of(code):
            return lax.shift_right_logical(code, 8) - first_row, code & (SHIFT - 1)

        base = window_start(bounds[step, 0], length)

        def entry(k):
            node, target = parts_of(codes[0, 0, k])
            put_row(near_total, node, row_at(near_total, node) + shares[0, 0, k] * row_at(rows_here, target))

        walk(bounds[step, 0] - base, bounds[step, 1] - base, entry)

        def self_entry(k):
            node, target = parts_of(self_codes[0, 0, k])
            put_row(self_total, node, row_at(self_total, node) + row_at(rows_here, target))

        walk(bounds[step, 2], bounds[step, 3], self_entry)

    @pl.when(step >= requesters)
    def _():
        base = (step - requesters) * (block // SUBLANES)

        def part(g, carry):
            where = pl.ds(pl.multiple_of(g * 16, 16), 16)
            for total, sums in ((near_total, near_sums), (self_total, self_sums)):
                for c in range(chunks):
                    halves = [
                        total[pl.ds((base + g * 2 + h) * tile + c, SUBLANES, stride=SUBLANES), :] for h in range(2)
                    ]
                    sums[where, c * LANES : (c + 1) * LANES] = jnp.concatenate(halves, axis=0).astype(BF16)
            return carry

        lax.fori_loop(0, block // 16, part, 0)
        turned = (((1,), (1,)), ((), ()))
        raw = lax.dot_general(near_sums[...], mix_pooled[...], turned, preferred_element_type=F32)
        grad_pre = jnp.where(hidden[...].astype(F32) > 0, raw, 0.0)
        query_bias_grad[...] += jnp.sum(grad_pre.reshape(block // SUBLANES, SUBLANES, width), axis=0)
        grad_pre = grad_pre.astype(BF16)
        down = (((0,), (0,)), ((), ()))
        weight_grad[...] += lax.dot_general(table_own[...], grad_pre, down, preferred_element_type=F32)
        weight_sum[...] += lax.dot_general(table_other[...], grad_pre, down, preferred_element_type=F32)
        table_grad[...] = lax.dot_general(
            grad_pre, query_own[...], turned, preferred_element_type=F32
        ) + lax.dot_general(self_sums[...], self_own[...], turned, preferred_element_type=F32)
        send = (
            lax.dot_general(grad_pre, query_other[...], turned, preferred_element_type=F32)
            + lax.dot_general(self_sums[...], self_other[...], turned, preferred_element_type=F32)
        ).astype(BF16)
        send_first[...] = send[:, : send_first.shape[1]]
        send_last[...] = send[:, send_first.shape[1] :]

    @pl.when(step == pl.num_programs(0) - 1)
    def _():
        weight_send[...] = weight_sum[...].astype(BF16)


def owner_backward(table, hidden, grads, mix, query, codes, shares, self_codes, bounds, place, owners, groups, targets):
    rows_owned, width = table.shape
    rows = rows_owned // SPLIT
    blocks = rows // ROW_BLOCK
    requesters, _, length = codes.shape
    self_length = self_codes.shape[2]
    part = width // groups

    def requester(i):
        return jnp.minimum(i, requesters - 1)

    def node_row(i, place):
        return lax.rem(place[0], SPLIT) * blocks + jnp.maximum(i - requesters, 0)

    def list_block(i, place, bounds):
        k = requester(i)
        return (k, 0, window_start(bounds[k, 0], length))

    def grad_block(i, place, bounds):
        k = requester(i)
        return (lax.rem(k, owners) * groups + lax.div(k, owners), 0)

    def weights(which):
        return pl.BlockSpec(
            (part, width), lambda i, place, bounds: (place[which], 0), pipeline_mode=pl.Buffered(1)
        )

    def table_columns(which):
        return pl.BlockSpec((ROW_BLOCK, part), lambda i, place, bounds: (node_row(i, place), place[which]))

    def fixed(shape):
        return pl.BlockSpec(shape, lambda i, place, bounds: (0, 0))

    window = (pl.Element(1), pl.Element(1), pl.Element(WINDOW))
    return pl.pallas_call(
        functools.partial(backward_kernel, requesters, length),
        grid_spec=pltpu.PrefetchScalarGridSpec(
            num_scalar_prefetch=2,
            grid=(requesters + blocks,),
            in_specs=[
                pl.BlockSpec(window, list_block, memory_space=pltpu.SMEM),
                pl.BlockSpec(window, list_block, memory_space=pltpu.SMEM),
                pl.BlockSpec(
                    (1, 1, self_length), lambda i, place, bounds: (requester(i), 0, 0), memory_space=pltpu.SMEM
                ),
                pl.BlockSpec((targets, width), grad_block),
                pl.BlockSpec((ROW_BLOCK, width), lambda i, place, bounds: (node_row(i, place), 0)),
                table_columns(0),
                table_columns(1),
                weights(0),
                weights(1),
                pl.BlockSpec((width, width), lambda i, place, bounds: (1, 0), pipeline_mode=pl.Buffered(1)),
                weights(0),
                weights(1),
            ],
            out_specs=[
                pl.BlockSpec((ROW_BLOCK, part), lambda i, place, bounds: (node_row(i, place), 0)),
                pl.BlockSpec((ROW_BLOCK, part // 2), lambda i, place, bounds: (jnp.maximum(i - requesters, 0), 0)),
                pl.BlockSpec((ROW_BLOCK, part // 2), lambda i, place, bounds: (jnp.maximum(i - requesters, 0), 0)),
                fixed((part, width)),
                fixed((part, width)),
                fixed((SUBLANES, width)),
                fixed((SUBLANES, width)),
            ],
            scratch_shapes=[
                pltpu.VMEM((rows * SUBLANES, LANES), F32),
                pltpu.VMEM((rows * SUBLANES, LANES), F32),
                pltpu.VMEM((targets * SUBLANES, LANES), F32),
                pltpu.VMEM((ROW_BLOCK, width), BF16),
                pltpu.VMEM((ROW_BLOCK, width), BF16),
                pltpu.VMEM((part, width), F32),
            ],
        ),
        out_shape=[
            jax.ShapeDtypeStruct((rows_owned, part), F32),
            jax.ShapeDtypeStruct((rows, part // 2), BF16),
            jax.ShapeDtypeStruct((rows, part // 2), BF16),
            jax.ShapeDtypeStruct((part, width), F32),
            jax.ShapeDtypeStruct((part, width), BF16),
            jax.ShapeDtypeStruct((SUBLANES, width), F32),
            jax.ShapeDtypeStruct((SUBLANES, width), F32),
        ],
        compiler_params=pltpu.CompilerParams(vmem_limit_bytes=VMEM_BYTES),
        cost_estimate=pl.CostEstimate(
            flops=8 * rows * width * width, bytes_accessed=4 * requesters * targets * width, transcendentals=0
        ),
        name="owner_backward",
    )(
        place,
        bounds,
        codes,
        shares,
        self_codes,
        grads,
        hidden,
        table,
        table,
        mix,
        mix,
        mix,
        query,
        query,
    )


def padded(values, length):
    return jnp.pad(values, (0, length - values.shape[0]))


def local(
    feature_table,
    neighbour_query_weight,
    query_bias,
    mix_weight,
    mix_bias,
    lookup_ids,
    present_counts,
    importance,
    embed_cot,
):
    owners = lax.axis_size("table")
    groups = lax.axis_size("rep")
    devices = owners * groups
    rows_owned, width = feature_table.shape
    batch_rows, slot_count = lookup_ids.shape
    near = slot_count - 1
    owner = lax.axis_index("table").astype(I32)
    group = lax.axis_index("rep").astype(I32)

    present = (jnp.arange(near, dtype=I32)[None, :] < present_counts[:, None]).astype(F32)
    masked_weight = importance * present
    shares = lax.reduce_precision(masked_weight / jnp.sum(masked_weight, axis=1, keepdims=True), 8, 7)
    live_most = batch_rows // 2 * (near + 5)
    length = -(-live_most // LANES) * LANES
    target = jnp.arange(batch_rows, dtype=I32)
    keys = jnp.where(present > 0, lookup_ids[:, 1:] * SHIFT + target[:, None], jnp.iinfo(I32).max)
    keys, sorted_shares = lax.sort((keys.reshape(-1), shares.reshape(-1)), num_keys=1, is_stable=False)
    keys = keys[:live_most]
    sorted_shares = sorted_shares[:live_most]
    own_keys = lax.sort(lookup_ids[:, 0] * SHIFT + target)
    edges = jnp.arange(owners * SPLIT + 1, dtype=I32) * (rows_owned // SPLIT * SHIFT)
    starts = jnp.sum((keys[None, :] < edges[:, None]).astype(I32), axis=1)
    own_starts = jnp.sum((own_keys[None, :] < edges[:, None]).astype(I32), axis=1)
    own_length = SHIFT
    meta = jnp.concatenate(
        [
            starts.astype(F32),
            own_starts.astype(F32),
            jnp.stack([jnp.sum(present), jnp.sum(masked_weight)]),
        ]
    )
    meta_length = -(-meta.shape[0] // LANES) * LANES

    def as_code(key):
        return (key % (rows_owned * SHIFT)).astype(F32)

    request = jnp.concatenate(
        [
            padded(as_code(keys), length),
            padded(sorted_shares, length),
            padded(as_code(own_keys), own_length),
            padded(meta, meta_length),
            padded(lookup_ids[:, 0].astype(F32), own_length),
        ]
    )
    plane = lax.all_gather(request, "table", axis=0)

    own_ids = plane[:, -own_length:][:, :batch_rows].astype(I32).reshape(-1)
    wanted = own_ids - owner * rows_owned
    mine = (wanted >= 0) & (wanted < rows_owned)
    found = feature_table[jnp.clip(wanted, 0, rows_owned - 1)]
    found = jnp.where(mine[:, None], found, jnp.zeros((), BF16))
    self_rows = lax.psum_scatter(found, "table", scatter_dimension=0, tiled=True)
    every = lax.all_gather(plane, "rep", axis=0).reshape(devices, -1)

    def unpack(lists, start, stride):
        count = lists.shape[0]
        at = 2 * length
        codes = lists[:, :length].astype(I32).reshape(count, 1, length)
        parts = lists[:, length:at].reshape(count, 1, length)
        own_codes = lists[:, at : at + own_length].astype(I32).reshape(count, 1, own_length)
        notes = lists[:, at + own_length :]
        first = lax.dynamic_slice(notes, (0, start), (count, stride + 1))[:, ::stride]
        own_first = lax.dynamic_slice(notes, (0, start + owners * SPLIT + 1), (count, stride + 1))[:, ::stride]
        bounds = jnp.concatenate([first, own_first], axis=1).astype(I32)
        sums = jnp.sum(notes[:, 2 * (owners * SPLIT + 1) : 2 * (owners * SPLIT + 2)], axis=0)
        return codes, parts, own_codes, bounds, sums

    codes, parts, _, bounds, _ = unpack(plane, owner * SPLIT, SPLIT)
    bounds, _ = lax.optimization_barrier((bounds, found))
    hidden, pooled_parts = owner_forward(
        feature_table, neighbour_query_weight, query_bias, codes, parts, bounds, batch_rows
    )
    pooled_parts, self_rows = lax.optimization_barrier((pooled_parts, self_rows))
    pooled = lax.psum_scatter(pooled_parts, "table", scatter_dimension=0, tiled=True)
    half = lax.rem(group, SPLIT)
    pooled, lists = lax.optimization_barrier((pooled, unpack(every, owner * SPLIT + half, 1)))
    all_codes, all_parts, all_own_codes, all_bounds, sums = lists
    pooled = lax.reduce_precision(pooled, 8, 7).astype(BF16)

    joined = jnp.concatenate([self_rows, pooled], axis=1)
    mixed = jnp.dot(joined, mix_weight, preferred_element_type=F32) + mix_bias
    activation = jax.nn.relu(mixed)
    inverse = lax.rsqrt(jnp.mean(activation * activation, axis=1, keepdims=True) + 1e-06)
    embed = (activation * inverse).astype(BF16)
    cotangent = embed_cot.astype(F32)
    grad_act = inverse * cotangent - activation * (inverse * inverse * inverse) * jnp.mean(
        activation * cotangent, axis=1, keepdims=True
    )
    grad_mixed = jnp.where(mixed > 0, grad_act, 0.0).astype(BF16)
    all_mixed = lax.all_gather(grad_mixed, ("table", "rep"), axis=0, tiled=True)
    mix_part = 2 * width // devices
    columns = lax.all_to_all(
        joined.reshape(batch_rows, devices, mix_part).transpose(1, 0, 2),
        ("table", "rep"),
        split_axis=0,
        concat_axis=0,
        tiled=True,
    ).reshape(devices * batch_rows, mix_part)

    mix_rows = lax.dot_general(
        columns, all_mixed, (((0,), (0,)), ((), ())), preferred_element_type=F32
    ).astype(BF16)
    all_mixed, mix_rows = lax.optimization_barrier((all_mixed, mix_rows))
    mix_gathered = lax.all_gather(mix_rows, ("table", "rep"), axis=0, tiled=True)

    partner = group + 1 - 2 * half
    swap = [(i, i + 1 - 2 * (i % SPLIT)) for i in range(groups)]
    table_grad, send_first, send_last, query_part, query_send, query_bias_part, mix_bias_part = owner_backward(
        feature_table,
        hidden,
        all_mixed,
        mix_weight,
        neighbour_query_weight,
        all_codes,
        all_parts,
        all_own_codes,
        all_bounds,
        jnp.stack([group, partner]),
        owners,
        groups,
        batch_rows,
    )
    mix_bias_grad = jnp.sum(mix_bias_part, axis=0)

    query_rows = width // devices
    bias_rows = 16
    query_part = query_part + lax.ppermute(query_send, "rep", swap).astype(F32)
    send_first, mix_gathered = lax.optimization_barrier((send_first, mix_gathered))
    mix_weight_grad = mix_gathered.astype(F32)
    got_first = lax.ppermute(send_first, "rep", swap)
    incoming = lax.all_to_all(
        query_part.astype(BF16).reshape(owners, query_rows, width), "table", split_axis=0, concat_axis=0, tiled=True
    )
    summed = jnp.sum(incoming.astype(F32), axis=0)
    bias_part = jnp.pad(jnp.sum(query_bias_part, axis=0, keepdims=True), ((0, bias_rows - 1), (0, 0)))
    summed, got_first = lax.optimization_barrier((summed, got_first))
    got_last = lax.ppermute(send_last, "rep", swap)
    table_got = jnp.concatenate([got_first, got_last], axis=1)
    gathered = lax.all_gather(
        jnp.concatenate([summed, bias_part], axis=0).astype(BF16), ("table", "rep"), axis=0
    ).reshape(owners, groups, query_rows + bias_rows, width)
    query_weight_grad = (
        gathered[:, :, :query_rows].transpose(1, 0, 2, 3).reshape(width, width).astype(F32)
    )
    query_bias_grad = jnp.sum(gathered[:, :SPLIT, query_rows].astype(F32), axis=(0, 1))
    table_grad = lax.dynamic_update_slice(
        table_grad, table_got.astype(F32), ((1 - half) * (rows_owned // SPLIT), 0)
    )
    statistics = sums / (batch_rows * devices)
    return (
        embed,
        table_grad,
        query_weight_grad,
        query_bias_grad,
        mix_weight_grad,
        mix_bias_grad,
        statistics,
    )


def solution(mesh):
    in_specs = (
        P("table", None),
        P(),
        P(),
        P(),
        P(),
        P(("table", "rep"), None),
        P(("table", "rep")),
        P(("table", "rep"), None),
        P(("table", "rep"), None),
    )
    out_specs = (P(("table", "rep"), None), P("table", "rep"), P(), P(), P(), P(), P())
    return jax.shard_map(local, mesh=mesh, in_specs=in_specs, out_specs=out_specs, check_vma=False)
```

```python
import functools

import jax
import jax.numpy as jnp
from jax import lax
from jax.experimental import pallas as pl
from jax.experimental.pallas import tpu as pltpu
from jax.sharding import PartitionSpec as P

F32 = jnp.float32
BF16 = jnp.bfloat16
I32 = jnp.int32
LANES = 128
SUBLANES = 8
ROW_BLOCK = 512
SHIFT = 256
SPLIT = 2
WINDOW = 1536
UNROLL = 4
VMEM_BYTES = 60 << 20


def row_at(ref, row):
    return ref[pl.ds(pl.multiple_of(row * SUBLANES, SUBLANES), SUBLANES), :]


def put_row(ref, row, value):
    ref[pl.ds(pl.multiple_of(row * SUBLANES, SUBLANES), SUBLANES), :] = value


def clear_rows(ref, rows):
    zero = jnp.zeros((SUBLANES * SUBLANES, LANES), F32)

    def step(i, carry):
        ref[pl.ds(pl.multiple_of(i * SUBLANES * SUBLANES, SUBLANES), SUBLANES * SUBLANES), :] = zero
        return carry

    lax.fori_loop(0, rows // SUBLANES, step, 0)


def walk(first, last, entry):
    count = last - first
    groups = count // UNROLL

    def group(i, carry):
        for u in range(UNROLL):
            entry(first + i * UNROLL + u)
        return carry

    def single(k, carry):
        entry(k)
        return carry

    lax.fori_loop(0, groups, group, 0)
    lax.fori_loop(first + groups * UNROLL, last, single, 0)


def window_start(first, length):
    return pl.multiple_of(jnp.minimum(lax.div(first, LANES) * LANES, length - WINDOW), LANES)


def forward_kernel(blocks, length, bounds, table, query, bias, codes, shares, hidden, pooled, hidden_rows, pooled_rows):
    step = pl.program_id(0)
    width = table.shape[1]
    chunks = width // LANES
    sub = 128

    @pl.when(step < blocks)
    def _():
        def part(j, carry):
            start = pl.multiple_of(j * sub, sub)
            pre = jnp.dot(table[pl.ds(start, sub), :], query[...], preferred_element_type=F32) + bias[...]
            tiny = jnp.finfo(BF16).tiny
            kept = jnp.where(pre > 0, jnp.maximum(pre, tiny), 0.0).astype(BF16)
            hidden[pl.ds(start, sub), :] = kept
            wide = kept.astype(F32)
            base = (step * ROW_BLOCK + start) * SUBLANES
            for g in range(sub // SUBLANES):
                for c in range(chunks):
                    hidden_rows[pl.ds(base + g * SUBLANES * SUBLANES + c, SUBLANES, stride=SUBLANES), :] = wide[
                        g * SUBLANES : (g + 1) * SUBLANES, c * LANES : (c + 1) * LANES
                    ]
            return carry

        lax.fori_loop(0, ROW_BLOCK // sub, part, 0)

    @pl.when(step >= blocks)
    def _():
        device = step - blocks
        targets = pooled.shape[0]
        clear_rows(pooled_rows, targets)

        def entry(k):
            code = codes[0, 0, k]
            node = lax.shift_right_logical(code, 8)
            target = code & (SHIFT - 1)
            put_row(
                pooled_rows,
                target,
                row_at(pooled_rows, target) + shares[0, 0, k] * row_at(hidden_rows, node),
            )

        base = window_start(bounds[device, 0], length)
        walk(bounds[device, 0] - base, bounds[device, 1] - base, entry)

        def part(g, carry):
            for c in range(chunks):
                pooled[
                    pl.ds(pl.multiple_of(g * SUBLANES, SUBLANES), SUBLANES), c * LANES : (c + 1) * LANES
                ] = pooled_rows[pl.ds(g * SUBLANES * SUBLANES + c, SUBLANES, stride=SUBLANES), :]
            return carry

        lax.fori_loop(0, targets // SUBLANES, part, 0)


def owner_forward(table, query, bias, codes, shares, bounds, targets):
    rows, width = table.shape
    blocks = rows // ROW_BLOCK
    devices, _, length = codes.shape

    def list_block(i, bounds):
        k = jnp.maximum(i - blocks, 0)
        return (k, 0, window_start(bounds[k, 0], length))

    window = (pl.Element(1), pl.Element(1), pl.Element(WINDOW))
    return pl.pallas_call(
        functools.partial(forward_kernel, blocks, length),
        grid_spec=pltpu.PrefetchScalarGridSpec(
            num_scalar_prefetch=1,
            grid=(blocks + devices,),
            in_specs=[
                pl.BlockSpec((ROW_BLOCK, width), lambda i, b: (jnp.minimum(i, blocks - 1), 0)),
                pl.BlockSpec((width, width), lambda i, b: (0, 0)),
                pl.BlockSpec((1, width), lambda i, b: (0, 0)),
                pl.BlockSpec(window, list_block, memory_space=pltpu.SMEM),
                pl.BlockSpec(window, list_block, memory_space=pltpu.SMEM),
            ],
            out_specs=[
                pl.BlockSpec((ROW_BLOCK, width), lambda i, b: (jnp.minimum(i, blocks - 1), 0)),
                pl.BlockSpec((targets, width), lambda i, b: (jnp.maximum(i - blocks, 0), 0)),
            ],
            scratch_shapes=[
                pltpu.VMEM((rows * SUBLANES, LANES), F32),
                pltpu.VMEM((targets * SUBLANES, LANES), F32),
            ],
        ),
        out_shape=[
            jax.ShapeDtypeStruct((rows, width), BF16),
            jax.ShapeDtypeStruct((devices * targets, width), F32),
        ],
        compiler_params=pltpu.CompilerParams(vmem_limit_bytes=VMEM_BYTES),
        cost_estimate=pl.CostEstimate(
            flops=2 * rows * width * width, bytes_accessed=4 * rows * width, transcendentals=0
        ),
        name="owner_forward",
    )(bounds, table, query, bias.reshape(1, width), codes, shares)


def spread_rows(source, rows_here):
    targets, width = source.shape
    chunks = width // LANES
    tile = SUBLANES * SUBLANES

    def part(g, sums):
        both = source[pl.ds(pl.multiple_of(g * 16, 16), 16), :].astype(F32)
        for h in range(2):
            for c in range(chunks):
                rows_here[pl.ds((g * 2 + h) * tile + c, SUBLANES, stride=SUBLANES), :] = both[
                    h * SUBLANES : (h + 1) * SUBLANES, c * LANES : (c + 1) * LANES
                ]
        return sums + both[:SUBLANES] + both[SUBLANES:]

    return lax.fori_loop(0, targets // 16, part, jnp.zeros((SUBLANES, width), F32))


def backward_kernel(
    requesters,
    length,
    place,
    bounds,
    codes,
    shares,
    self_codes,
    grads,
    hidden,
    table_own,
    table_other,
    mix_pooled,
    grad_pre,
    self_sums,
    weight_grad,
    weight_send,
    query_bias_grad,
    mix_bias_grad,
    near_total,
    self_total,
    rows_here,
    near_sums,
    weight_sum,
):
    step = pl.program_id(0)
    block, width = hidden.shape
    rows = near_total.shape[0] // SUBLANES
    chunks = width // LANES
    tile = SUBLANES * SUBLANES

    @pl.when(step == 0)
    def _():
        clear_rows(near_total, rows)
        clear_rows(self_total, rows)
        mix_bias_grad[...] = jnp.zeros_like(mix_bias_grad)
        query_bias_grad[...] = jnp.zeros_like(query_bias_grad)
        weight_grad[...] = jnp.zeros_like(weight_grad)
        weight_sum[...] = jnp.zeros_like(weight_sum)

    @pl.when(step < requesters)
    def _():
        mix_bias_grad[...] += spread_rows(grads, rows_here)
        first_row = lax.rem(place[0], SPLIT) * rows

        def parts_of(code):
            return lax.shift_right_logical(code, 8) - first_row, code & (SHIFT - 1)

        base = window_start(bounds[step, 0], length)

        def entry(k):
            node, target = parts_of(codes[0, 0, k])
            put_row(near_total, node, row_at(near_total, node) + shares[0, 0, k] * row_at(rows_here, target))

        walk(bounds[step, 0] - base, bounds[step, 1] - base, entry)

        def self_entry(k):
            node, target = parts_of(self_codes[0, 0, k])
            put_row(self_total, node, row_at(self_total, node) + row_at(rows_here, target))

        walk(bounds[step, 2], bounds[step, 3], self_entry)

    @pl.when(step >= requesters)
    def _():
        base = (step - requesters) * (block // SUBLANES)

        def part(g, carry):
            where = pl.ds(pl.multiple_of(g * 16, 16), 16)
            for total, sums in ((near_total, near_sums), (self_total, self_sums)):
                for c in range(chunks):
                    halves = [
                        total[pl.ds((base + g * 2 + h) * tile + c, SUBLANES, stride=SUBLANES), :] for h in range(2)
                    ]
                    sums[where, c * LANES : (c + 1) * LANES] = jnp.concatenate(halves, axis=0).astype(BF16)
            return carry

        lax.fori_loop(0, block // 16, part, 0)
        turned = (((1,), (1,)), ((), ()))
        raw = lax.dot_general(near_sums[...], mix_pooled[...], turned, preferred_element_type=F32)
        wide = jnp.where(hidden[...].astype(F32) > 0, raw, 0.0)
        query_bias_grad[...] += jnp.sum(wide.reshape(block // SUBLANES, SUBLANES, width), axis=0)
        kept = wide.astype(BF16)
        grad_pre[...] = kept
        down = (((0,), (0,)), ((), ()))
        weight_grad[...] += lax.dot_general(table_own[...], kept, down, preferred_element_type=F32)
        weight_sum[...] += lax.dot_general(table_other[...], kept, down, preferred_element_type=F32)

    @pl.when(step == pl.num_programs(0) - 1)
    def _():
        weight_send[...] = weight_sum[...].astype(BF16)


def owner_backward(table, hidden, grads, mix, codes, shares, self_codes, bounds, place, owners, groups, targets):
    rows_owned, width = table.shape
    rows = rows_owned // SPLIT
    blocks = rows // ROW_BLOCK
    requesters, _, length = codes.shape
    self_length = self_codes.shape[2]
    part = width // groups

    def requester(i):
        return jnp.minimum(i, requesters - 1)

    def node_row(i, place):
        return lax.rem(place[0], SPLIT) * blocks + jnp.maximum(i - requesters, 0)

    def list_block(i, place, bounds):
        k = requester(i)
        return (k, 0, window_start(bounds[k, 0], length))

    def grad_block(i, place, bounds):
        k = requester(i)
        return (lax.rem(k, owners) * groups + lax.div(k, owners), 0)

    def table_columns(which):
        return pl.BlockSpec((ROW_BLOCK, part), lambda i, place, bounds: (node_row(i, place), place[which]))

    def fixed(shape):
        return pl.BlockSpec(shape, lambda i, place, bounds: (0, 0))

    window = (pl.Element(1), pl.Element(1), pl.Element(WINDOW))
    return pl.pallas_call(
        functools.partial(backward_kernel, requesters, length),
        grid_spec=pltpu.PrefetchScalarGridSpec(
            num_scalar_prefetch=2,
            grid=(requesters + blocks,),
            in_specs=[
                pl.BlockSpec(window, list_block, memory_space=pltpu.SMEM),
                pl.BlockSpec(window, list_block, memory_space=pltpu.SMEM),
                pl.BlockSpec(
                    (1, 1, self_length), lambda i, place, bounds: (requester(i), 0, 0), memory_space=pltpu.SMEM
                ),
                pl.BlockSpec((targets, width), grad_block),
                pl.BlockSpec((ROW_BLOCK, width), lambda i, place, bounds: (node_row(i, place), 0)),
                table_columns(0),
                table_columns(1),
                pl.BlockSpec((width, width), lambda i, place, bounds: (1, 0), pipeline_mode=pl.Buffered(1)),
            ],
            out_specs=[
                pl.BlockSpec((ROW_BLOCK, width), lambda i, place, bounds: (jnp.maximum(i - requesters, 0), 0)),
                pl.BlockSpec((ROW_BLOCK, width), lambda i, place, bounds: (jnp.maximum(i - requesters, 0), 0)),
                fixed((part, width)),
                fixed((part, width)),
                fixed((SUBLANES, width)),
                fixed((SUBLANES, width)),
            ],
            scratch_shapes=[
                pltpu.VMEM((rows * SUBLANES, LANES), F32),
                pltpu.VMEM((rows * SUBLANES, LANES), F32),
                pltpu.VMEM((targets * SUBLANES, LANES), F32),
                pltpu.VMEM((ROW_BLOCK, width), BF16),
                pltpu.VMEM((part, width), F32),
            ],
        ),
        out_shape=[
            jax.ShapeDtypeStruct((rows, width), BF16),
            jax.ShapeDtypeStruct((rows, width), BF16),
            jax.ShapeDtypeStruct((part, width), F32),
            jax.ShapeDtypeStruct((part, width), BF16),
            jax.ShapeDtypeStruct((SUBLANES, width), F32),
            jax.ShapeDtypeStruct((SUBLANES, width), F32),
        ],
        compiler_params=pltpu.CompilerParams(vmem_limit_bytes=VMEM_BYTES),
        cost_estimate=pl.CostEstimate(
            flops=8 * rows * width * width, bytes_accessed=4 * requesters * targets * width, transcendentals=0
        ),
        name="owner_backward",
    )(
        place,
        bounds,
        codes,
        shares,
        self_codes,
        grads,
        hidden,
        table,
        table,
        mix,
    )


def table_kernel(place, grad_pre, self_sums, query, mix_self, *outs):
    turned = (((1,), (1,)), ((), ()))
    grad = lax.dot_general(grad_pre[...], query[...], turned, preferred_element_type=F32) + lax.dot_general(
        self_sums[...], mix_self[...], turned, preferred_element_type=F32
    )
    at = 0
    for out in outs:
        out[...] = grad[:, at : at + out.shape[1]].astype(out.dtype)
        at += out.shape[1]


def table_columns_grad(grad_pre, self_sums, query, mix, place, part, kept_rows=None):
    rows, width = grad_pre.shape
    blocks = rows // ROW_BLOCK

    def node_block(i, place):
        return (i, 0)

    weights = pl.BlockSpec((part, width), lambda i, place: (place[0], 0), pipeline_mode=pl.Buffered(1))
    if kept_rows is None:
        out_specs = [pl.BlockSpec((ROW_BLOCK, part // 2), node_block)] * 2
        out_shape = [jax.ShapeDtypeStruct((rows, part // 2), BF16)] * 2
    else:
        out_specs = [pl.BlockSpec((ROW_BLOCK, part), lambda i, place: (lax.rem(place[0], SPLIT) * blocks + i, 0))]
        out_shape = [jax.ShapeDtypeStruct((kept_rows, part), F32)]
    return pl.pallas_call(
        table_kernel,
        grid_spec=pltpu.PrefetchScalarGridSpec(
            num_scalar_prefetch=1,
            grid=(blocks,),
            in_specs=[pl.BlockSpec((ROW_BLOCK, width), node_block)] * 2 + [weights] * 2,
            out_specs=out_specs,
        ),
        out_shape=out_shape,
        compiler_params=pltpu.CompilerParams(vmem_limit_bytes=VMEM_BYTES),
        cost_estimate=pl.CostEstimate(
            flops=4 * rows * width * part, bytes_accessed=4 * rows * width, transcendentals=0
        ),
        name="table_columns_grad",
    )(place, grad_pre, self_sums, query, mix)


def padded(values, length):
    return jnp.pad(values, (0, length - values.shape[0]))


def local(
    feature_table,
    neighbour_query_weight,
    query_bias,
    mix_weight,
    mix_bias,
    lookup_ids,
    present_counts,
    importance,
    embed_cot,
):
    owners = lax.axis_size("table")
    groups = lax.axis_size("rep")
    devices = owners * groups
    rows_owned, width = feature_table.shape
    batch_rows, slot_count = lookup_ids.shape
    near = slot_count - 1
    owner = lax.axis_index("table").astype(I32)
    group = lax.axis_index("rep").astype(I32)

    present = (jnp.arange(near, dtype=I32)[None, :] < present_counts[:, None]).astype(F32)
    masked_weight = importance * present
    shares = lax.reduce_precision(masked_weight / jnp.sum(masked_weight, axis=1, keepdims=True), 8, 7)
    live_most = batch_rows // 2 * (near + 5)
    length = -(-live_most // LANES) * LANES
    target = jnp.arange(batch_rows, dtype=I32)
    keys = jnp.where(present > 0, lookup_ids[:, 1:] * SHIFT + target[:, None], jnp.iinfo(I32).max)
    keys, sorted_shares = lax.sort((keys.reshape(-1), shares.reshape(-1)), num_keys=1, is_stable=False)
    keys = keys[:live_most]
    sorted_shares = sorted_shares[:live_most]
    own_keys = lax.sort(lookup_ids[:, 0] * SHIFT + target)
    edges = jnp.arange(owners * SPLIT + 1, dtype=I32) * (rows_owned // SPLIT * SHIFT)
    starts = jnp.sum((keys[None, :] < edges[:, None]).astype(I32), axis=1)
    own_starts = jnp.sum((own_keys[None, :] < edges[:, None]).astype(I32), axis=1)
    own_length = SHIFT
    meta = jnp.concatenate(
        [
            starts.astype(F32),
            own_starts.astype(F32),
            jnp.stack([jnp.sum(present), jnp.sum(masked_weight)]),
        ]
    )
    meta_length = -(-meta.shape[0] // LANES) * LANES

    def as_code(key):
        return (key % (rows_owned * SHIFT)).astype(F32)

    request = jnp.concatenate(
        [
            padded(as_code(keys), length),
            padded(sorted_shares, length),
            padded(as_code(own_keys), own_length),
            padded(meta, meta_length),
            padded(lookup_ids[:, 0].astype(F32), own_length),
        ]
    )
    plane = lax.all_gather(request, "table", axis=0)

    own_ids = plane[:, -own_length:][:, :batch_rows].astype(I32).reshape(-1)
    wanted = own_ids - owner * rows_owned
    mine = (wanted >= 0) & (wanted < rows_owned)
    found = feature_table[jnp.clip(wanted, 0, rows_owned - 1)]
    found = jnp.where(mine[:, None], found, jnp.zeros((), BF16))
    self_rows = lax.psum_scatter(found, "table", scatter_dimension=0, tiled=True)
    every = lax.all_gather(plane, "rep", axis=0).reshape(devices, -1)

    def unpack(lists, start, stride):
        count = lists.shape[0]
        at = 2 * length
        codes = lists[:, :length].astype(I32).reshape(count, 1, length)
        parts = lists[:, length:at].reshape(count, 1, length)
        own_codes = lists[:, at : at + own_length].astype(I32).reshape(count, 1, own_length)
        notes = lists[:, at + own_length :]
        first = lax.dynamic_slice(notes, (0, start), (count, stride + 1))[:, ::stride]
        own_first = lax.dynamic_slice(notes, (0, start + owners * SPLIT + 1), (count, stride + 1))[:, ::stride]
        bounds = jnp.concatenate([first, own_first], axis=1).astype(I32)
        sums = jnp.sum(notes[:, 2 * (owners * SPLIT + 1) : 2 * (owners * SPLIT + 2)], axis=0)
        return codes, parts, own_codes, bounds, sums

    codes, parts, _, bounds, _ = unpack(plane, owner * SPLIT, SPLIT)
    bounds, _ = lax.optimization_barrier((bounds, found))
    hidden, pooled_parts = owner_forward(
        feature_table, neighbour_query_weight, query_bias, codes, parts, bounds, batch_rows
    )
    pooled_parts, self_rows = lax.optimization_barrier((pooled_parts, self_rows))
    pooled = lax.psum_scatter(pooled_parts, "table", scatter_dimension=0, tiled=True)
    half = lax.rem(group, SPLIT)
    pooled, lists = lax.optimization_barrier((pooled, unpack(every, owner * SPLIT + half, 1)))
    all_codes, all_parts, all_own_codes, all_bounds, sums = lists
    pooled = lax.reduce_precision(pooled, 8, 7).astype(BF16)

    joined = jnp.concatenate([self_rows, pooled], axis=1)
    mixed = jnp.dot(joined, mix_weight, preferred_element_type=F32) + mix_bias
    activation = jax.nn.relu(mixed)
    inverse = lax.rsqrt(jnp.mean(activation * activation, axis=1, keepdims=True) + 1e-06)
    embed = (activation * inverse).astype(BF16)
    cotangent = embed_cot.astype(F32)
    grad_act = inverse * cotangent - activation * (inverse * inverse * inverse) * jnp.mean(
        activation * cotangent, axis=1, keepdims=True
    )
    grad_mixed = jnp.where(mixed > 0, grad_act, 0.0).astype(BF16)
    all_mixed = lax.all_gather(grad_mixed, ("table", "rep"), axis=0, tiled=True)
    mix_part = 2 * width // devices
    columns = lax.all_to_all(
        joined.reshape(batch_rows, devices, mix_part).transpose(1, 0, 2),
        ("table", "rep"),
        split_axis=0,
        concat_axis=0,
        tiled=True,
    ).reshape(devices * batch_rows, mix_part)

    mix_rows = lax.dot_general(
        columns, all_mixed, (((0,), (0,)), ((), ())), preferred_element_type=F32
    ).astype(BF16)
    all_mixed, mix_rows = lax.optimization_barrier((all_mixed, mix_rows))
    mix_gathered = lax.all_gather(mix_rows, ("table", "rep"), axis=0, tiled=True)

    partner = group + 1 - 2 * half
    swap = [(i, i + 1 - 2 * (i % SPLIT)) for i in range(groups)]
    grad_pre, self_sums, query_part, query_send, query_bias_part, mix_bias_part = owner_backward(
        feature_table,
        hidden,
        all_mixed,
        mix_weight,
        all_codes,
        all_parts,
        all_own_codes,
        all_bounds,
        jnp.stack([group, partner]),
        owners,
        groups,
        batch_rows,
    )
    part = width // groups
    send_first, send_last = table_columns_grad(
        grad_pre, self_sums, neighbour_query_weight, mix_weight, partner.reshape(1), part
    )
    (table_grad,) = table_columns_grad(
        grad_pre, self_sums, neighbour_query_weight, mix_weight, group.reshape(1), part, rows_owned
    )
    mix_bias_grad = jnp.sum(mix_bias_part, axis=0)

    query_rows = width // devices
    query_part = query_part + lax.ppermute(query_send, "rep", swap).astype(F32)
    send_first, mix_gathered = lax.optimization_barrier((send_first, mix_gathered))
    mix_weight_grad = mix_gathered.astype(F32)
    got_first = lax.ppermute(send_first, "rep", swap)
    incoming = lax.all_to_all(
        query_part.astype(BF16).reshape(owners, query_rows, width), "table", split_axis=0, concat_axis=0, tiled=True
    )
    summed = jnp.sum(incoming.astype(F32), axis=0)
    summed, got_first = lax.optimization_barrier((summed, got_first))
    got_last = lax.ppermute(send_last, "rep", swap)
    table_got = jnp.concatenate([got_first, got_last], axis=1)
    gathered = lax.all_gather(summed.astype(BF16), ("table", "rep"), axis=0).reshape(
        owners, groups, query_rows, width
    )
    query_weight_grad = gathered.transpose(1, 0, 2, 3).reshape(width, width).astype(F32)
    bias_parts = lax.all_gather(jnp.sum(query_bias_part, axis=0), ("table", "rep"), axis=0)
    query_bias_grad = jnp.sum(bias_parts.reshape(owners, groups, width)[:, :SPLIT], axis=(0, 1))
    table_grad = lax.dynamic_update_slice(
        table_grad, table_got.astype(F32), ((1 - half) * (rows_owned // SPLIT), 0)
    )
    statistics = sums / (batch_rows * devices)
    return (
        embed,
        table_grad,
        query_weight_grad,
        query_bias_grad,
        mix_weight_grad,
        mix_bias_grad,
        statistics,
    )


def solution(mesh):
    in_specs = (
        P("table", None),
        P(),
        P(),
        P(),
        P(),
        P(("table", "rep"), None),
        P(("table", "rep")),
        P(("table", "rep"), None),
        P(("table", "rep"), None),
    )
    out_specs = (P(("table", "rep"), None), P("table", "rep"), P(), P(), P(), P(), P())
    return jax.shard_map(local, mesh=mesh, in_specs=in_specs, out_specs=out_specs, check_vma=False)
```

```python
import functools

import jax
import jax.numpy as jnp
from jax import lax
from jax.experimental import pallas as pl
from jax.experimental.pallas import tpu as pltpu
from jax.sharding import PartitionSpec as P

F32 = jnp.float32
BF16 = jnp.bfloat16
I32 = jnp.int32
LANES = 128
SUBLANES = 8
ROW_BLOCK = 512
SHIFT = 256
BIAS_ROWS = 16
SPLIT = 2
WINDOW = 1536
UNROLL = 4
VMEM_BYTES = 60 << 20


def row_at(ref, row):
    return ref[pl.ds(pl.multiple_of(row * SUBLANES, SUBLANES), SUBLANES), :]


def put_row(ref, row, value):
    ref[pl.ds(pl.multiple_of(row * SUBLANES, SUBLANES), SUBLANES), :] = value


def clear_rows(ref, rows):
    zero = jnp.zeros((SUBLANES * SUBLANES, LANES), F32)

    def step(i, carry):
        ref[pl.ds(pl.multiple_of(i * SUBLANES * SUBLANES, SUBLANES), SUBLANES * SUBLANES), :] = zero
        return carry

    lax.fori_loop(0, rows // SUBLANES, step, 0)


def walk(first, last, entry):
    count = last - first
    groups = count // UNROLL

    def group(i, carry):
        for u in range(UNROLL):
            entry(first + i * UNROLL + u)
        return carry

    def single(k, carry):
        entry(k)
        return carry

    lax.fori_loop(0, groups, group, 0)
    lax.fori_loop(first + groups * UNROLL, last, single, 0)


def window_start(first, length):
    return pl.multiple_of(jnp.minimum(lax.div(first, LANES) * LANES, length - WINDOW), LANES)


def forward_kernel(blocks, length, bounds, table, query, bias, codes, shares, hidden, pooled, hidden_rows, pooled_rows):
    step = pl.program_id(0)
    width = table.shape[1]
    chunks = width // LANES
    sub = 128

    @pl.when(step < blocks)
    def _():
        def part(j, carry):
            start = pl.multiple_of(j * sub, sub)
            pre = jnp.dot(table[pl.ds(start, sub), :], query[...], preferred_element_type=F32) + bias[...]
            tiny = jnp.finfo(BF16).tiny
            kept = jnp.where(pre > 0, jnp.maximum(pre, tiny), 0.0).astype(BF16)
            hidden[pl.ds(start, sub), :] = kept
            wide = kept.astype(F32)
            base = (step * ROW_BLOCK + start) * SUBLANES
            for g in range(sub // SUBLANES):
                for c in range(chunks):
                    hidden_rows[pl.ds(base + g * SUBLANES * SUBLANES + c, SUBLANES, stride=SUBLANES), :] = wide[
                        g * SUBLANES : (g + 1) * SUBLANES, c * LANES : (c + 1) * LANES
                    ]
            return carry

        lax.fori_loop(0, ROW_BLOCK // sub, part, 0)

    @pl.when(step >= blocks)
    def _():
        device = step - blocks
        targets = pooled.shape[0]
        clear_rows(pooled_rows, targets)

        def entry(k):
            code = codes[0, 0, k]
            node = lax.shift_right_logical(code, 8)
            target = code & (SHIFT - 1)
            put_row(
                pooled_rows,
                target,
                row_at(pooled_rows, target) + shares[0, 0, k] * row_at(hidden_rows, node),
            )

        base = window_start(bounds[device, 0], length)
        walk(bounds[device, 0] - base, bounds[device, 1] - base, entry)

        def part(g, carry):
            for c in range(chunks):
                pooled[
                    pl.ds(pl.multiple_of(g * SUBLANES, SUBLANES), SUBLANES), c * LANES : (c + 1) * LANES
                ] = pooled_rows[pl.ds(g * SUBLANES * SUBLANES + c, SUBLANES, stride=SUBLANES), :]
            return carry

        lax.fori_loop(0, targets // SUBLANES, part, 0)


def owner_forward(table, query, bias, codes, shares, bounds, targets):
    rows, width = table.shape
    blocks = rows // ROW_BLOCK
    devices, _, length = codes.shape

    def list_block(i, bounds):
        k = jnp.maximum(i - blocks, 0)
        return (k, 0, window_start(bounds[k, 0], length))

    window = (pl.Element(1), pl.Element(1), pl.Element(WINDOW))
    return pl.pallas_call(
        functools.partial(forward_kernel, blocks, length),
        grid_spec=pltpu.PrefetchScalarGridSpec(
            num_scalar_prefetch=1,
            grid=(blocks + devices,),
            in_specs=[
                pl.BlockSpec((ROW_BLOCK, width), lambda i, b: (jnp.minimum(i, blocks - 1), 0)),
                pl.BlockSpec((width, width), lambda i, b: (0, 0)),
                pl.BlockSpec((1, width), lambda i, b: (0, 0)),
                pl.BlockSpec(window, list_block, memory_space=pltpu.SMEM),
                pl.BlockSpec(window, list_block, memory_space=pltpu.SMEM),
            ],
            out_specs=[
                pl.BlockSpec((ROW_BLOCK, width), lambda i, b: (jnp.minimum(i, blocks - 1), 0)),
                pl.BlockSpec((targets, width), lambda i, b: (jnp.maximum(i - blocks, 0), 0)),
            ],
            scratch_shapes=[
                pltpu.VMEM((rows * SUBLANES, LANES), F32),
                pltpu.VMEM((targets * SUBLANES, LANES), F32),
            ],
        ),
        out_shape=[
            jax.ShapeDtypeStruct((rows, width), BF16),
            jax.ShapeDtypeStruct((devices * targets, width), F32),
        ],
        compiler_params=pltpu.CompilerParams(vmem_limit_bytes=VMEM_BYTES),
        cost_estimate=pl.CostEstimate(
            flops=2 * rows * width * width, bytes_accessed=4 * rows * width, transcendentals=0
        ),
        name="owner_forward",
    )(bounds, table, query, bias.reshape(1, width), codes, shares)


def spread_rows(source, rows_here):
    targets, width = source.shape
    chunks = width // LANES
    tile = SUBLANES * SUBLANES

    def part(g, sums):
        both = source[pl.ds(pl.multiple_of(g * 16, 16), 16), :].astype(F32)
        for h in range(2):
            for c in range(chunks):
                rows_here[pl.ds((g * 2 + h) * tile + c, SUBLANES, stride=SUBLANES), :] = both[
                    h * SUBLANES : (h + 1) * SUBLANES, c * LANES : (c + 1) * LANES
                ]
        return sums + both[:SUBLANES] + both[SUBLANES:]

    return lax.fori_loop(0, targets // 16, part, jnp.zeros((SUBLANES, width), F32))


def backward_kernel(
    requesters,
    length,
    place,
    bounds,
    codes,
    shares,
    self_codes,
    grads,
    hidden,
    table_own,
    table_other,
    mix_pooled,
    grad_pre,
    self_sums,
    weight_grad,
    weight_send,
    mix_bias_grad,
    near_total,
    self_total,
    rows_here,
    near_sums,
    weight_sum,
    bias_sum,
):
    step = pl.program_id(0)
    block, width = hidden.shape
    rows = near_total.shape[0] // SUBLANES
    part_rows = weight_sum.shape[0]
    chunks = width // LANES
    tile = SUBLANES * SUBLANES

    @pl.when(step == 0)
    def _():
        clear_rows(near_total, rows)
        clear_rows(self_total, rows)
        mix_bias_grad[...] = jnp.zeros_like(mix_bias_grad)
        bias_sum[...] = jnp.zeros_like(bias_sum)
        weight_grad[...] = jnp.zeros_like(weight_grad)
        weight_sum[...] = jnp.zeros_like(weight_sum)

    @pl.when(step < requesters)
    def _():
        mix_bias_grad[...] += spread_rows(grads, rows_here)
        first_row = lax.rem(place[0], SPLIT) * rows

        def parts_of(code):
            return lax.shift_right_logical(code, 8) - first_row, code & (SHIFT - 1)

        base = window_start(bounds[step, 0], length)

        def entry(k):
            node, target = parts_of(codes[0, 0, k])
            put_row(near_total, node, row_at(near_total, node) + shares[0, 0, k] * row_at(rows_here, target))

        walk(bounds[step, 0] - base, bounds[step, 1] - base, entry)

        def self_entry(k):
            node, target = parts_of(self_codes[0, 0, k])
            put_row(self_total, node, row_at(self_total, node) + row_at(rows_here, target))

        walk(bounds[step, 2], bounds[step, 3], self_entry)

    @pl.when(step >= requesters)
    def _():
        base = (step - requesters) * (block // SUBLANES)

        def part(g, carry):
            where = pl.ds(pl.multiple_of(g * 16, 16), 16)
            for total, sums in ((near_total, near_sums), (self_total, self_sums)):
                for c in range(chunks):
                    halves = [
                        total[pl.ds((base + g * 2 + h) * tile + c, SUBLANES, stride=SUBLANES), :] for h in range(2)
                    ]
                    sums[where, c * LANES : (c + 1) * LANES] = jnp.concatenate(halves, axis=0).astype(BF16)
            return carry

        lax.fori_loop(0, block // 16, part, 0)
        turned = (((1,), (1,)), ((), ()))
        raw = lax.dot_general(near_sums[...], mix_pooled[...], turned, preferred_element_type=F32)
        wide = jnp.where(hidden[...].astype(F32) > 0, raw, 0.0)
        bias_sum[...] += jnp.sum(wide.reshape(block // SUBLANES, SUBLANES, width), axis=0)
        kept = wide.astype(BF16)
        grad_pre[...] = kept
        down = (((0,), (0,)), ((), ()))
        weight_grad[:part_rows] += lax.dot_general(table_own[...], kept, down, preferred_element_type=F32)
        weight_sum[...] += lax.dot_general(table_other[...], kept, down, preferred_element_type=F32)

    @pl.when(step == pl.num_programs(0) - 1)
    def _():
        bias = jnp.broadcast_to(jnp.sum(bias_sum[...], axis=0, keepdims=True), (BIAS_ROWS, width))
        weight_grad[part_rows:] = bias
        weight_send[:part_rows] = weight_sum[...].astype(BF16)
        weight_send[part_rows:] = bias.astype(BF16)


def owner_backward(table, hidden, grads, mix, codes, shares, self_codes, bounds, place, owners, groups, targets):
    rows_owned, width = table.shape
    rows = rows_owned // SPLIT
    blocks = rows // ROW_BLOCK
    requesters, _, length = codes.shape
    self_length = self_codes.shape[2]
    part = width // groups

    def requester(i):
        return jnp.minimum(i, requesters - 1)

    def node_row(i, place):
        return lax.rem(place[0], SPLIT) * blocks + jnp.maximum(i - requesters, 0)

    def list_block(i, place, bounds):
        k = requester(i)
        return (k, 0, window_start(bounds[k, 0], length))

    def grad_block(i, place, bounds):
        k = requester(i)
        return (lax.rem(k, owners) * groups + lax.div(k, owners), 0)

    def table_columns(which):
        return pl.BlockSpec((ROW_BLOCK, part), lambda i, place, bounds: (node_row(i, place), place[which]))

    def fixed(shape):
        return pl.BlockSpec(shape, lambda i, place, bounds: (0, 0))

    window = (pl.Element(1), pl.Element(1), pl.Element(WINDOW))
    return pl.pallas_call(
        functools.partial(backward_kernel, requesters, length),
        grid_spec=pltpu.PrefetchScalarGridSpec(
            num_scalar_prefetch=2,
            grid=(requesters + blocks,),
            in_specs=[
                pl.BlockSpec(window, list_block, memory_space=pltpu.SMEM),
                pl.BlockSpec(window, list_block, memory_space=pltpu.SMEM),
                pl.BlockSpec(
                    (1, 1, self_length), lambda i, place, bounds: (requester(i), 0, 0), memory_space=pltpu.SMEM
                ),
                pl.BlockSpec((targets, width), grad_block),
                pl.BlockSpec((ROW_BLOCK, width), lambda i, place, bounds: (node_row(i, place), 0)),
                table_columns(0),
                table_columns(1),
                pl.BlockSpec((width, width), lambda i, place, bounds: (1, 0), pipeline_mode=pl.Buffered(1)),
            ],
            out_specs=[
                pl.BlockSpec((ROW_BLOCK, width), lambda i, place, bounds: (jnp.maximum(i - requesters, 0), 0)),
                pl.BlockSpec((ROW_BLOCK, width), lambda i, place, bounds: (jnp.maximum(i - requesters, 0), 0)),
                fixed((part + BIAS_ROWS, width)),
                fixed((part + BIAS_ROWS, width)),
                fixed((SUBLANES, width)),
            ],
            scratch_shapes=[
                pltpu.VMEM((rows * SUBLANES, LANES), F32),
                pltpu.VMEM((rows * SUBLANES, LANES), F32),
                pltpu.VMEM((targets * SUBLANES, LANES), F32),
                pltpu.VMEM((ROW_BLOCK, width), BF16),
                pltpu.VMEM((part, width), F32),
                pltpu.VMEM((SUBLANES, width), F32),
            ],
        ),
        out_shape=[
            jax.ShapeDtypeStruct((rows, width), BF16),
            jax.ShapeDtypeStruct((rows, width), BF16),
            jax.ShapeDtypeStruct((part + BIAS_ROWS, width), F32),
            jax.ShapeDtypeStruct((part + BIAS_ROWS, width), BF16),
            jax.ShapeDtypeStruct((SUBLANES, width), F32),
        ],
        compiler_params=pltpu.CompilerParams(vmem_limit_bytes=VMEM_BYTES),
        cost_estimate=pl.CostEstimate(
            flops=8 * rows * width * width, bytes_accessed=4 * requesters * targets * width, transcendentals=0
        ),
        name="owner_backward",
    )(
        place,
        bounds,
        codes,
        shares,
        self_codes,
        grads,
        hidden,
        table,
        table,
        mix,
    )


def table_kernel(place, grad_pre, self_sums, query, mix_self, *outs):
    turned = (((1,), (1,)), ((), ()))
    grad = lax.dot_general(grad_pre[...], query[...], turned, preferred_element_type=F32) + lax.dot_general(
        self_sums[...], mix_self[...], turned, preferred_element_type=F32
    )
    at = 0
    for out in outs:
        out[...] = grad[:, at : at + out.shape[1]].astype(out.dtype)
        at += out.shape[1]


def table_columns_grad(grad_pre, self_sums, query, mix, place, part, kept_rows=None):
    rows, width = grad_pre.shape
    blocks = rows // ROW_BLOCK

    def node_block(i, place):
        return (i, 0)

    weights = pl.BlockSpec((part, width), lambda i, place: (place[0], 0), pipeline_mode=pl.Buffered(1))
    if kept_rows is None:
        out_specs = [pl.BlockSpec((ROW_BLOCK, part // 2), node_block)] * 2
        out_shape = [jax.ShapeDtypeStruct((rows, part // 2), BF16)] * 2
    else:
        out_specs = [pl.BlockSpec((ROW_BLOCK, part), lambda i, place: (lax.rem(place[0], SPLIT) * blocks + i, 0))]
        out_shape = [jax.ShapeDtypeStruct((kept_rows, part), F32)]
    return pl.pallas_call(
        table_kernel,
        grid_spec=pltpu.PrefetchScalarGridSpec(
            num_scalar_prefetch=1,
            grid=(blocks,),
            in_specs=[pl.BlockSpec((ROW_BLOCK, width), node_block)] * 2 + [weights] * 2,
            out_specs=out_specs,
        ),
        out_shape=out_shape,
        compiler_params=pltpu.CompilerParams(vmem_limit_bytes=VMEM_BYTES),
        cost_estimate=pl.CostEstimate(
            flops=4 * rows * width * part, bytes_accessed=4 * rows * width, transcendentals=0
        ),
        name="table_columns_grad",
    )(place, grad_pre, self_sums, query, mix)


def padded(values, length):
    return jnp.pad(values, (0, length - values.shape[0]))


def local(
    feature_table,
    neighbour_query_weight,
    query_bias,
    mix_weight,
    mix_bias,
    lookup_ids,
    present_counts,
    importance,
    embed_cot,
):
    owners = lax.axis_size("table")
    groups = lax.axis_size("rep")
    devices = owners * groups
    rows_owned, width = feature_table.shape
    batch_rows, slot_count = lookup_ids.shape
    near = slot_count - 1
    owner = lax.axis_index("table").astype(I32)
    group = lax.axis_index("rep").astype(I32)

    present = (jnp.arange(near, dtype=I32)[None, :] < present_counts[:, None]).astype(F32)
    masked_weight = importance * present
    shares = lax.reduce_precision(masked_weight / jnp.sum(masked_weight, axis=1, keepdims=True), 8, 7)
    live_most = batch_rows // 2 * (near + 5)
    length = -(-live_most // LANES) * LANES
    target = jnp.arange(batch_rows, dtype=I32)
    keys = jnp.where(present > 0, lookup_ids[:, 1:] * SHIFT + target[:, None], jnp.iinfo(I32).max)
    keys, sorted_shares = lax.sort((keys.reshape(-1), shares.reshape(-1)), num_keys=1, is_stable=False)
    keys = keys[:live_most]
    sorted_shares = sorted_shares[:live_most]
    own_keys = lax.sort(lookup_ids[:, 0] * SHIFT + target)
    edges = jnp.arange(owners * SPLIT + 1, dtype=I32) * (rows_owned // SPLIT * SHIFT)
    starts = jnp.sum((keys[None, :] < edges[:, None]).astype(I32), axis=1)
    own_starts = jnp.sum((own_keys[None, :] < edges[:, None]).astype(I32), axis=1)
    own_length = SHIFT
    meta = jnp.concatenate(
        [
            starts.astype(F32),
            own_starts.astype(F32),
            jnp.stack([jnp.sum(present), jnp.sum(masked_weight)]),
        ]
    )
    meta_length = -(-meta.shape[0] // LANES) * LANES

    def as_code(key):
        return (key % (rows_owned * SHIFT)).astype(F32)

    request = jnp.concatenate(
        [
            padded(as_code(keys), length),
            padded(sorted_shares, length),
            padded(as_code(own_keys), own_length),
            padded(meta, meta_length),
            padded(lookup_ids[:, 0].astype(F32), own_length),
        ]
    )
    plane = lax.all_gather(request, "table", axis=0)

    own_ids = plane[:, -own_length:][:, :batch_rows].astype(I32).reshape(-1)
    wanted = own_ids - owner * rows_owned
    mine = (wanted >= 0) & (wanted < rows_owned)
    found = feature_table[jnp.clip(wanted, 0, rows_owned - 1)]
    found = jnp.where(mine[:, None], found, jnp.zeros((), BF16))
    self_rows = lax.psum_scatter(found, "table", scatter_dimension=0, tiled=True)
    every = lax.all_gather(plane, "rep", axis=0).reshape(devices, -1)

    def unpack(lists, start, stride):
        count = lists.shape[0]
        at = 2 * length
        codes = lists[:, :length].astype(I32).reshape(count, 1, length)
        parts = lists[:, length:at].reshape(count, 1, length)
        own_codes = lists[:, at : at + own_length].astype(I32).reshape(count, 1, own_length)
        notes = lists[:, at + own_length :]
        first = lax.dynamic_slice(notes, (0, start), (count, stride + 1))[:, ::stride]
        own_first = lax.dynamic_slice(notes, (0, start + owners * SPLIT + 1), (count, stride + 1))[:, ::stride]
        bounds = jnp.concatenate([first, own_first], axis=1).astype(I32)
        sums = jnp.sum(notes[:, 2 * (owners * SPLIT + 1) : 2 * (owners * SPLIT + 2)], axis=0)
        return codes, parts, own_codes, bounds, sums

    codes, parts, _, bounds, _ = unpack(plane, owner * SPLIT, SPLIT)
    bounds, _ = lax.optimization_barrier((bounds, found))
    hidden, pooled_parts = owner_forward(
        feature_table, neighbour_query_weight, query_bias, codes, parts, bounds, batch_rows
    )
    pooled_parts, self_rows = lax.optimization_barrier((pooled_parts, self_rows))
    pooled = lax.psum_scatter(pooled_parts, "table", scatter_dimension=0, tiled=True)
    half = lax.rem(group, SPLIT)
    pooled, lists = lax.optimization_barrier((pooled, unpack(every, owner * SPLIT + half, 1)))
    all_codes, all_parts, all_own_codes, all_bounds, sums = lists
    pooled = lax.reduce_precision(pooled, 8, 7).astype(BF16)

    joined = jnp.concatenate([self_rows, pooled], axis=1)
    mixed = jnp.dot(joined, mix_weight, preferred_element_type=F32) + mix_bias
    activation = jax.nn.relu(mixed)
    inverse = lax.rsqrt(jnp.mean(activation * activation, axis=1, keepdims=True) + 1e-06)
    embed = (activation * inverse).astype(BF16)
    cotangent = embed_cot.astype(F32)
    grad_act = inverse * cotangent - activation * (inverse * inverse * inverse) * jnp.mean(
        activation * cotangent, axis=1, keepdims=True
    )
    grad_mixed = jnp.where(mixed > 0, grad_act, 0.0).astype(BF16)
    all_mixed = lax.all_gather(grad_mixed, ("table", "rep"), axis=0, tiled=True)
    mix_part = 2 * width // devices
    columns = lax.all_to_all(
        joined.reshape(batch_rows, devices, mix_part).transpose(1, 0, 2),
        ("table", "rep"),
        split_axis=0,
        concat_axis=0,
        tiled=True,
    ).reshape(devices * batch_rows, mix_part)

    mix_rows = lax.dot_general(
        columns, all_mixed, (((0,), (0,)), ((), ())), preferred_element_type=F32
    ).astype(BF16)
    all_mixed, mix_rows = lax.optimization_barrier((all_mixed, mix_rows))
    mix_gathered = lax.all_gather(mix_rows, ("table", "rep"), axis=0, tiled=True)

    partner = group + 1 - 2 * half
    swap = [(i, i + 1 - 2 * (i % SPLIT)) for i in range(groups)]
    grad_pre, self_sums, query_part, query_send, mix_bias_part = owner_backward(
        feature_table,
        hidden,
        all_mixed,
        mix_weight,
        all_codes,
        all_parts,
        all_own_codes,
        all_bounds,
        jnp.stack([group, partner]),
        owners,
        groups,
        batch_rows,
    )
    part = width // groups
    send_first, send_last = table_columns_grad(
        grad_pre, self_sums, neighbour_query_weight, mix_weight, partner.reshape(1), part
    )
    (table_grad,) = table_columns_grad(
        grad_pre, self_sums, neighbour_query_weight, mix_weight, group.reshape(1), part, rows_owned
    )
    mix_bias_grad = jnp.sum(mix_bias_part, axis=0)

    query_rows = width // devices
    query_part = query_part + lax.ppermute(query_send, "rep", swap).astype(F32)
    send_first, mix_gathered = lax.optimization_barrier((send_first, mix_gathered))
    mix_weight_grad = mix_gathered.astype(F32)
    got_first = lax.ppermute(send_first, "rep", swap)
    bias_rows = SUBLANES
    outgoing = jnp.concatenate(
        [
            query_part[:part].reshape(owners, query_rows, width),
            jnp.broadcast_to(query_part[part : part + bias_rows], (owners, bias_rows, width)),
        ],
        axis=1,
    )
    incoming = lax.all_to_all(outgoing.astype(BF16), "table", split_axis=0, concat_axis=0, tiled=True)
    summed = jnp.sum(incoming.astype(F32), axis=0)
    query_bias_grad = summed[query_rows]
    summed, got_first = lax.optimization_barrier((summed, got_first))
    got_last = lax.ppermute(send_last, "rep", swap)
    table_got = jnp.concatenate([got_first, got_last], axis=1)
    gathered = lax.all_gather(summed[:query_rows].astype(BF16), ("table", "rep"), axis=0).reshape(
        owners, groups, query_rows, width
    )
    query_weight_grad = gathered.transpose(1, 0, 2, 3).reshape(width, width).astype(F32)
    table_grad = lax.dynamic_update_slice(
        table_grad, table_got.astype(F32), ((1 - half) * (rows_owned // SPLIT), 0)
    )
    statistics = sums / (batch_rows * devices)
    return (
        embed,
        table_grad,
        query_weight_grad,
        query_bias_grad,
        mix_weight_grad,
        mix_bias_grad,
        statistics,
    )


def solution(mesh):
    in_specs = (
        P("table", None),
        P(),
        P(),
        P(),
        P(),
        P(("table", "rep"), None),
        P(("table", "rep")),
        P(("table", "rep"), None),
        P(("table", "rep"), None),
    )
    out_specs = (P(("table", "rep"), None), P("table", "rep"), P(), P(), P(), P(), P())
    return jax.shard_map(local, mesh=mesh, in_specs=in_specs, out_specs=out_specs, check_vma=False)
```

```python
import functools

import jax
import jax.numpy as jnp
from jax import lax
from jax.experimental import pallas as pl
from jax.experimental.pallas import tpu as pltpu
from jax.sharding import PartitionSpec as P

F32 = jnp.float32
BF16 = jnp.bfloat16
I32 = jnp.int32
LANES = 128
SUBLANES = 8
ROW_BLOCK = 512
SHIFT = 256
BIAS_ROWS = 16
SPLIT = 2
WINDOW = 1536
UNROLL = 4
VMEM_BYTES = 60 << 20


def row_at(ref, row):
    return ref[pl.ds(pl.multiple_of(row * SUBLANES, SUBLANES), SUBLANES), :]


def put_row(ref, row, value):
    ref[pl.ds(pl.multiple_of(row * SUBLANES, SUBLANES), SUBLANES), :] = value


def clear_rows(ref, rows):
    zero = jnp.zeros((SUBLANES * SUBLANES, LANES), F32)

    def step(i, carry):
        ref[pl.ds(pl.multiple_of(i * SUBLANES * SUBLANES, SUBLANES), SUBLANES * SUBLANES), :] = zero
        return carry

    lax.fori_loop(0, rows // SUBLANES, step, 0)


def walk(first, last, entry):
    count = last - first
    groups = count // UNROLL

    def group(i, carry):
        for u in range(UNROLL):
            entry(first + i * UNROLL + u)
        return carry

    def single(k, carry):
        entry(k)
        return carry

    lax.fori_loop(0, groups, group, 0)
    lax.fori_loop(first + groups * UNROLL, last, single, 0)


def window_start(first, length):
    return pl.multiple_of(jnp.minimum(lax.div(first, LANES) * LANES, length - WINDOW), LANES)


def forward_kernel(blocks, length, bounds, table, query, bias, codes, shares, hidden, pooled, hidden_rows, pooled_rows):
    step = pl.program_id(0)
    width = table.shape[1]
    chunks = width // LANES
    sub = 128

    @pl.when(step < blocks)
    def _():
        def part(j, carry):
            start = pl.multiple_of(j * sub, sub)
            pre = jnp.dot(table[pl.ds(start, sub), :], query[...], preferred_element_type=F32) + bias[...]
            tiny = jnp.finfo(BF16).tiny
            kept = jnp.where(pre > 0, jnp.maximum(pre, tiny), 0.0).astype(BF16)
            hidden[pl.ds(start, sub), :] = kept
            wide = kept.astype(F32)
            base = (step * ROW_BLOCK + start) * SUBLANES
            for g in range(sub // SUBLANES):
                for c in range(chunks):
                    hidden_rows[pl.ds(base + g * SUBLANES * SUBLANES + c, SUBLANES, stride=SUBLANES), :] = wide[
                        g * SUBLANES : (g + 1) * SUBLANES, c * LANES : (c + 1) * LANES
                    ]
            return carry

        lax.fori_loop(0, ROW_BLOCK // sub, part, 0)

    @pl.when(step >= blocks)
    def _():
        device = step - blocks
        targets = pooled.shape[0]
        clear_rows(pooled_rows, targets)

        def entry(k):
            code = codes[0, 0, k]
            node = lax.shift_right_logical(code, 8)
            target = code & (SHIFT - 1)
            put_row(
                pooled_rows,
                target,
                row_at(pooled_rows, target) + shares[0, 0, k] * row_at(hidden_rows, node),
            )

        base = window_start(bounds[device, 0], length)
        walk(bounds[device, 0] - base, bounds[device, 1] - base, entry)

        def part(g, carry):
            for c in range(chunks):
                pooled[
                    pl.ds(pl.multiple_of(g * SUBLANES, SUBLANES), SUBLANES), c * LANES : (c + 1) * LANES
                ] = pooled_rows[pl.ds(g * SUBLANES * SUBLANES + c, SUBLANES, stride=SUBLANES), :]
            return carry

        lax.fori_loop(0, targets // SUBLANES, part, 0)


def owner_forward(table, query, bias, codes, shares, bounds, targets):
    rows, width = table.shape
    blocks = rows // ROW_BLOCK
    devices, _, length = codes.shape

    def list_block(i, bounds):
        k = jnp.maximum(i - blocks, 0)
        return (k, 0, window_start(bounds[k, 0], length))

    window = (pl.Element(1), pl.Element(1), pl.Element(WINDOW))
    return pl.pallas_call(
        functools.partial(forward_kernel, blocks, length),
        grid_spec=pltpu.PrefetchScalarGridSpec(
            num_scalar_prefetch=1,
            grid=(blocks + devices,),
            in_specs=[
                pl.BlockSpec((ROW_BLOCK, width), lambda i, b: (jnp.minimum(i, blocks - 1), 0)),
                pl.BlockSpec((width, width), lambda i, b: (0, 0)),
                pl.BlockSpec((1, width), lambda i, b: (0, 0)),
                pl.BlockSpec(window, list_block, memory_space=pltpu.SMEM),
                pl.BlockSpec(window, list_block, memory_space=pltpu.SMEM),
            ],
            out_specs=[
                pl.BlockSpec((ROW_BLOCK, width), lambda i, b: (jnp.minimum(i, blocks - 1), 0)),
                pl.BlockSpec((targets, width), lambda i, b: (jnp.maximum(i - blocks, 0), 0)),
            ],
            scratch_shapes=[
                pltpu.VMEM((rows * SUBLANES, LANES), F32),
                pltpu.VMEM((targets * SUBLANES, LANES), F32),
            ],
        ),
        out_shape=[
            jax.ShapeDtypeStruct((rows, width), BF16),
            jax.ShapeDtypeStruct((devices * targets, width), F32),
        ],
        compiler_params=pltpu.CompilerParams(vmem_limit_bytes=VMEM_BYTES),
        cost_estimate=pl.CostEstimate(
            flops=2 * rows * width * width, bytes_accessed=4 * rows * width, transcendentals=0
        ),
        name="owner_forward",
    )(bounds, table, query, bias.reshape(1, width), codes, shares)


def spread_rows(source, rows_here):
    targets, width = source.shape
    chunks = width // LANES
    tile = SUBLANES * SUBLANES

    def part(g, sums):
        both = source[pl.ds(pl.multiple_of(g * 16, 16), 16), :].astype(F32)
        for h in range(2):
            for c in range(chunks):
                rows_here[pl.ds((g * 2 + h) * tile + c, SUBLANES, stride=SUBLANES), :] = both[
                    h * SUBLANES : (h + 1) * SUBLANES, c * LANES : (c + 1) * LANES
                ]
        return sums + both[:SUBLANES] + both[SUBLANES:]

    return lax.fori_loop(0, targets // 16, part, jnp.zeros((SUBLANES, width), F32))


def backward_kernel(
    requesters,
    length,
    place,
    bounds,
    codes,
    shares,
    self_codes,
    grads,
    hidden,
    table_own,
    table_other,
    mix_pooled,
    grad_pre,
    self_sums,
    weight_grad,
    weight_send,
    mix_bias_grad,
    near_total,
    self_total,
    rows_here,
    near_sums,
    weight_sum,
    bias_sum,
):
    step = pl.program_id(0)
    block, width = hidden.shape
    rows = near_total.shape[0] // SUBLANES
    part_rows = weight_sum.shape[0]
    chunks = width // LANES
    tile = SUBLANES * SUBLANES

    @pl.when(step == 0)
    def _():
        clear_rows(near_total, rows)
        clear_rows(self_total, rows)
        mix_bias_grad[...] = jnp.zeros_like(mix_bias_grad)
        bias_sum[...] = jnp.zeros_like(bias_sum)
        weight_grad[...] = jnp.zeros_like(weight_grad)
        weight_sum[...] = jnp.zeros_like(weight_sum)

    @pl.when(step < requesters)
    def _():
        mix_bias_grad[...] += spread_rows(grads, rows_here)
        first_row = lax.rem(place[0], SPLIT) * rows

        def parts_of(code):
            return lax.shift_right_logical(code, 8) - first_row, code & (SHIFT - 1)

        base = window_start(bounds[step, 0], length)

        def entry(k):
            node, target = parts_of(codes[0, 0, k])
            put_row(near_total, node, row_at(near_total, node) + shares[0, 0, k] * row_at(rows_here, target))

        walk(bounds[step, 0] - base, bounds[step, 1] - base, entry)

        def self_entry(k):
            node, target = parts_of(self_codes[0, 0, k])
            put_row(self_total, node, row_at(self_total, node) + row_at(rows_here, target))

        walk(bounds[step, 2], bounds[step, 3], self_entry)

    @pl.when(step >= requesters)
    def _():
        base = (step - requesters) * (block // SUBLANES)

        def part(g, carry):
            where = pl.ds(pl.multiple_of(g * 16, 16), 16)
            for total, sums in ((near_total, near_sums), (self_total, self_sums)):
                for c in range(chunks):
                    halves = [
                        total[pl.ds((base + g * 2 + h) * tile + c, SUBLANES, stride=SUBLANES), :] for h in range(2)
                    ]
                    sums[where, c * LANES : (c + 1) * LANES] = jnp.concatenate(halves, axis=0).astype(BF16)
            return carry

        lax.fori_loop(0, block // 16, part, 0)
        turned = (((1,), (1,)), ((), ()))
        raw = lax.dot_general(near_sums[...], mix_pooled[...], turned, preferred_element_type=F32)
        wide = jnp.where(hidden[...].astype(F32) > 0, raw, 0.0)
        bias_sum[...] += jnp.sum(wide.reshape(block // SUBLANES, SUBLANES, width), axis=0)
        kept = wide.astype(BF16)
        grad_pre[...] = kept
        down = (((0,), (0,)), ((), ()))
        weight_grad[:part_rows] += lax.dot_general(table_own[...], kept, down, preferred_element_type=F32)
        weight_sum[...] += lax.dot_general(table_other[...], kept, down, preferred_element_type=F32)

    @pl.when(step == pl.num_programs(0) - 1)
    def _():
        bias = jnp.broadcast_to(jnp.sum(bias_sum[...], axis=0, keepdims=True), (BIAS_ROWS, width))
        weight_grad[part_rows:] = bias
        weight_send[:part_rows] = weight_sum[...].astype(BF16)
        weight_send[part_rows:] = bias.astype(BF16)


def owner_backward(table, hidden, grads, mix, codes, shares, self_codes, bounds, place, owners, groups, targets):
    rows_owned, width = table.shape
    rows = rows_owned // SPLIT
    blocks = rows // ROW_BLOCK
    requesters, _, length = codes.shape
    self_length = self_codes.shape[2]
    part = width // groups

    def requester(i):
        return jnp.minimum(i, requesters - 1)

    def node_row(i, place):
        return lax.rem(place[0], SPLIT) * blocks + jnp.maximum(i - requesters, 0)

    def list_block(i, place, bounds):
        k = requester(i)
        return (k, 0, window_start(bounds[k, 0], length))

    def grad_block(i, place, bounds):
        k = requester(i)
        return (lax.rem(k, owners) * groups + lax.div(k, owners), 0)

    def table_columns(which):
        return pl.BlockSpec((ROW_BLOCK, part), lambda i, place, bounds: (node_row(i, place), place[which]))

    def fixed(shape):
        return pl.BlockSpec(shape, lambda i, place, bounds: (0, 0))

    window = (pl.Element(1), pl.Element(1), pl.Element(WINDOW))
    return pl.pallas_call(
        functools.partial(backward_kernel, requesters, length),
        grid_spec=pltpu.PrefetchScalarGridSpec(
            num_scalar_prefetch=2,
            grid=(requesters + blocks,),
            in_specs=[
                pl.BlockSpec(window, list_block, memory_space=pltpu.SMEM),
                pl.BlockSpec(window, list_block, memory_space=pltpu.SMEM),
                pl.BlockSpec(
                    (1, 1, self_length), lambda i, place, bounds: (requester(i), 0, 0), memory_space=pltpu.SMEM
                ),
                pl.BlockSpec((targets, width), grad_block),
                pl.BlockSpec((ROW_BLOCK, width), lambda i, place, bounds: (node_row(i, place), 0)),
                table_columns(0),
                table_columns(1),
                pl.BlockSpec((width, width), lambda i, place, bounds: (1, 0), pipeline_mode=pl.Buffered(1)),
            ],
            out_specs=[
                pl.BlockSpec((ROW_BLOCK, width), lambda i, place, bounds: (jnp.maximum(i - requesters, 0), 0)),
                pl.BlockSpec((ROW_BLOCK, width), lambda i, place, bounds: (jnp.maximum(i - requesters, 0), 0)),
                fixed((part + BIAS_ROWS, width)),
                fixed((part + BIAS_ROWS, width)),
                fixed((SUBLANES, width)),
            ],
            scratch_shapes=[
                pltpu.VMEM((rows * SUBLANES, LANES), F32),
                pltpu.VMEM((rows * SUBLANES, LANES), F32),
                pltpu.VMEM((targets * SUBLANES, LANES), F32),
                pltpu.VMEM((ROW_BLOCK, width), BF16),
                pltpu.VMEM((part, width), F32),
                pltpu.VMEM((SUBLANES, width), F32),
            ],
        ),
        out_shape=[
            jax.ShapeDtypeStruct((rows, width), BF16),
            jax.ShapeDtypeStruct((rows, width), BF16),
            jax.ShapeDtypeStruct((part + BIAS_ROWS, width), F32),
            jax.ShapeDtypeStruct((part + BIAS_ROWS, width), BF16),
            jax.ShapeDtypeStruct((SUBLANES, width), F32),
        ],
        compiler_params=pltpu.CompilerParams(vmem_limit_bytes=VMEM_BYTES),
        cost_estimate=pl.CostEstimate(
            flops=8 * rows * width * width, bytes_accessed=4 * requesters * targets * width, transcendentals=0
        ),
        name="owner_backward",
    )(
        place,
        bounds,
        codes,
        shares,
        self_codes,
        grads,
        hidden,
        table,
        table,
        mix,
    )


def table_kernel(place, grad_pre, self_sums, query, mix_self, *outs):
    turned = (((1,), (1,)), ((), ()))
    grad = lax.dot_general(grad_pre[...], query[...], turned, preferred_element_type=F32) + lax.dot_general(
        self_sums[...], mix_self[...], turned, preferred_element_type=F32
    )
    at = 0
    for out in outs:
        out[...] = grad[:, at : at + out.shape[1]].astype(out.dtype)
        at += out.shape[1]


def table_columns_grad(grad_pre, self_sums, query, mix, place, part, kept_rows=None):
    rows, width = grad_pre.shape
    blocks = rows // ROW_BLOCK

    def node_block(i, place):
        return (i, 0)

    weights = pl.BlockSpec((part, width), lambda i, place: (place[0], 0), pipeline_mode=pl.Buffered(1))
    if kept_rows is None:
        out_specs = [pl.BlockSpec((ROW_BLOCK, part // 2), node_block)] * 2
        out_shape = [jax.ShapeDtypeStruct((rows, part // 2), BF16)] * 2
    else:
        out_specs = [pl.BlockSpec((ROW_BLOCK, part), lambda i, place: (lax.rem(place[0], SPLIT) * blocks + i, 0))]
        out_shape = [jax.ShapeDtypeStruct((kept_rows, part), F32)]
    return pl.pallas_call(
        table_kernel,
        grid_spec=pltpu.PrefetchScalarGridSpec(
            num_scalar_prefetch=1,
            grid=(blocks,),
            in_specs=[pl.BlockSpec((ROW_BLOCK, width), node_block)] * 2 + [weights] * 2,
            out_specs=out_specs,
        ),
        out_shape=out_shape,
        compiler_params=pltpu.CompilerParams(vmem_limit_bytes=VMEM_BYTES),
        cost_estimate=pl.CostEstimate(
            flops=4 * rows * width * part, bytes_accessed=4 * rows * width, transcendentals=0
        ),
        name="table_columns_grad",
    )(place, grad_pre, self_sums, query, mix)


def padded(values, length):
    return jnp.pad(values, (0, length - values.shape[0]))


def local(
    feature_table,
    neighbour_query_weight,
    query_bias,
    mix_weight,
    mix_bias,
    lookup_ids,
    present_counts,
    importance,
    embed_cot,
):
    owners = lax.axis_size("table")
    groups = lax.axis_size("rep")
    devices = owners * groups
    rows_owned, width = feature_table.shape
    batch_rows, slot_count = lookup_ids.shape
    near = slot_count - 1
    owner = lax.axis_index("table").astype(I32)
    group = lax.axis_index("rep").astype(I32)

    present = (jnp.arange(near, dtype=I32)[None, :] < present_counts[:, None]).astype(F32)
    masked_weight = importance * present
    shares = lax.reduce_precision(masked_weight / jnp.sum(masked_weight, axis=1, keepdims=True), 8, 7)
    live_most = batch_rows // 2 * (near + 5)
    length = -(-live_most // LANES) * LANES
    target = jnp.arange(batch_rows, dtype=I32)
    keys = jnp.where(present > 0, lookup_ids[:, 1:] * SHIFT + target[:, None], jnp.iinfo(I32).max)
    keys, sorted_shares = lax.sort((keys.reshape(-1), shares.reshape(-1)), num_keys=1, is_stable=False)
    keys = keys[:live_most]
    sorted_shares = sorted_shares[:live_most]
    own_keys = lax.sort(lookup_ids[:, 0] * SHIFT + target)
    edges = jnp.arange(owners * SPLIT + 1, dtype=I32) * (rows_owned // SPLIT * SHIFT)
    starts = jnp.sum((keys[None, :] < edges[:, None]).astype(I32), axis=1)
    own_starts = jnp.sum((own_keys[None, :] < edges[:, None]).astype(I32), axis=1)
    own_length = SHIFT
    meta = jnp.concatenate(
        [
            starts.astype(F32),
            own_starts.astype(F32),
            jnp.stack([jnp.sum(present), jnp.sum(masked_weight)]),
        ]
    )
    meta_length = -(-meta.shape[0] // LANES) * LANES

    def as_code(key):
        return (key % (rows_owned * SHIFT)).astype(F32)

    request = jnp.concatenate(
        [
            padded(as_code(keys), length),
            padded(sorted_shares, length),
            padded(as_code(own_keys), own_length),
            padded(meta, meta_length),
            padded(lookup_ids[:, 0].astype(F32), own_length),
        ]
    )
    plane = lax.all_gather(request, "table", axis=0)

    own_ids = plane[:, -own_length:][:, :batch_rows].astype(I32).reshape(-1)
    wanted = own_ids - owner * rows_owned
    mine = (wanted >= 0) & (wanted < rows_owned)
    found = feature_table[jnp.clip(wanted, 0, rows_owned - 1)]
    found = jnp.where(mine[:, None], found, jnp.zeros((), BF16))
    self_rows = lax.psum_scatter(found, "table", scatter_dimension=0, tiled=True)
    every = lax.all_gather(plane, "rep", axis=0).reshape(devices, -1)

    def unpack(lists, start, stride):
        count = lists.shape[0]
        at = 2 * length
        codes = lists[:, :length].astype(I32).reshape(count, 1, length)
        parts = lists[:, length:at].reshape(count, 1, length)
        own_codes = lists[:, at : at + own_length].astype(I32).reshape(count, 1, own_length)
        notes = lists[:, at + own_length :]
        first = lax.dynamic_slice(notes, (0, start), (count, stride + 1))[:, ::stride]
        own_first = lax.dynamic_slice(notes, (0, start + owners * SPLIT + 1), (count, stride + 1))[:, ::stride]
        bounds = jnp.concatenate([first, own_first], axis=1).astype(I32)
        sums = jnp.sum(notes[:, 2 * (owners * SPLIT + 1) : 2 * (owners * SPLIT + 2)], axis=0)
        return codes, parts, own_codes, bounds, sums

    codes, parts, _, bounds, _ = unpack(plane, owner * SPLIT, SPLIT)
    bounds, _ = lax.optimization_barrier((bounds, found))
    hidden, pooled_parts = owner_forward(
        feature_table, neighbour_query_weight, query_bias, codes, parts, bounds, batch_rows
    )
    pooled_parts, self_rows = lax.optimization_barrier((pooled_parts, self_rows))
    pooled = lax.psum_scatter(pooled_parts, "table", scatter_dimension=0, tiled=True)
    half = lax.rem(group, SPLIT)
    pooled, lists = lax.optimization_barrier((pooled, unpack(every, owner * SPLIT + half, 1)))
    all_codes, all_parts, all_own_codes, all_bounds, sums = lists
    pooled = lax.reduce_precision(pooled, 8, 7).astype(BF16)

    joined = jnp.concatenate([self_rows, pooled], axis=1)
    mixed = jnp.dot(joined, mix_weight, preferred_element_type=F32) + mix_bias
    activation = jax.nn.relu(mixed)
    inverse = lax.rsqrt(jnp.mean(activation * activation, axis=1, keepdims=True) + 1e-06)
    embed = (activation * inverse).astype(BF16)
    cotangent = embed_cot.astype(F32)
    grad_act = inverse * cotangent - activation * (inverse * inverse * inverse) * jnp.mean(
        activation * cotangent, axis=1, keepdims=True
    )
    grad_mixed = jnp.where(mixed > 0, grad_act, 0.0).astype(BF16)
    all_mixed = lax.all_gather(grad_mixed, ("table", "rep"), axis=0, tiled=True)
    mix_part = 2 * width // devices
    columns = lax.all_to_all(
        joined.reshape(batch_rows, devices, mix_part).transpose(1, 0, 2),
        ("table", "rep"),
        split_axis=0,
        concat_axis=0,
        tiled=True,
    ).reshape(devices * batch_rows, mix_part)

    mix_rows = lax.dot_general(
        columns, all_mixed, (((0,), (0,)), ((), ())), preferred_element_type=F32
    ).astype(BF16)
    all_mixed, mix_rows = lax.optimization_barrier((all_mixed, mix_rows))
    mix_gathered = lax.all_gather(mix_rows, ("table", "rep"), axis=0, tiled=True)

    partner = group + 1 - 2 * half
    swap = [(i, i + 1 - 2 * (i % SPLIT)) for i in range(groups)]
    grad_pre, self_sums, query_part, query_send, mix_bias_part = owner_backward(
        feature_table,
        hidden,
        all_mixed,
        mix_weight,
        all_codes,
        all_parts,
        all_own_codes,
        all_bounds,
        jnp.stack([group, partner]),
        owners,
        groups,
        batch_rows,
    )
    part = width // groups
    send_first, send_last = table_columns_grad(
        grad_pre, self_sums, neighbour_query_weight, mix_weight, partner.reshape(1), part
    )
    (table_grad,) = table_columns_grad(
        grad_pre, self_sums, neighbour_query_weight, mix_weight, group.reshape(1), part, rows_owned
    )
    mix_bias_grad = jnp.sum(mix_bias_part, axis=0)

    query_rows = width // devices
    query_part = query_part + lax.ppermute(query_send, "rep", swap).astype(F32)
    send_first, mix_gathered = lax.optimization_barrier((send_first, mix_gathered))
    mix_weight_grad = mix_gathered.astype(F32)
    got_first = lax.ppermute(send_first, "rep", swap)
    bias_rows = SUBLANES
    outgoing = jnp.concatenate(
        [
            query_part[:part].reshape(owners, query_rows, width),
            jnp.broadcast_to(query_part[part : part + bias_rows], (owners, bias_rows, width)),
        ],
        axis=1,
    )
    incoming = lax.all_to_all(outgoing.astype(BF16), "table", split_axis=0, concat_axis=0, tiled=True)
    summed = jnp.sum(incoming.astype(F32), axis=0)
    query_bias_grad = summed[query_rows]
    summed, got_first = lax.optimization_barrier((summed, got_first))
    got_last = lax.ppermute(send_last, "rep", swap)
    table_got = jnp.concatenate([got_first, got_last], axis=1)
    column = lax.all_to_all(
        jnp.broadcast_to(summed[:query_rows].astype(BF16), (groups, query_rows, width)),
        "rep",
        split_axis=0,
        concat_axis=0,
        tiled=True,
    )
    gathered = lax.all_to_all(
        jnp.broadcast_to(column, (owners, groups, query_rows, width)), "table", split_axis=0, concat_axis=0, tiled=True
    )
    query_weight_grad = gathered.transpose(1, 0, 2, 3).reshape(width, width).astype(F32)
    table_grad = lax.dynamic_update_slice(
        table_grad, table_got.astype(F32), ((1 - half) * (rows_owned // SPLIT), 0)
    )
    statistics = sums / (batch_rows * devices)
    return (
        embed,
        table_grad,
        query_weight_grad,
        query_bias_grad,
        mix_weight_grad,
        mix_bias_grad,
        statistics,
    )


def solution(mesh):
    in_specs = (
        P("table", None),
        P(),
        P(),
        P(),
        P(),
        P(("table", "rep"), None),
        P(("table", "rep")),
        P(("table", "rep"), None),
        P(("table", "rep"), None),
    )
    out_specs = (P(("table", "rep"), None), P("table", "rep"), P(), P(), P(), P(), P())
    return jax.shard_map(local, mesh=mesh, in_specs=in_specs, out_specs=out_specs, check_vma=False)
```

```python
import functools

import jax
import jax.numpy as jnp
from jax import lax
from jax.experimental import pallas as pl
from jax.experimental.pallas import tpu as pltpu
from jax.sharding import PartitionSpec as P

F32 = jnp.float32
BF16 = jnp.bfloat16
I32 = jnp.int32
LANES = 128
SUBLANES = 8
ROW_BLOCK = 512
SHIFT = 256
BIAS_ROWS = 16
SPLIT = 2
WINDOW = 1536
UNROLL = 4
VMEM_BYTES = 60 << 20


def row_at(ref, row):
    return ref[pl.ds(pl.multiple_of(row * SUBLANES, SUBLANES), SUBLANES), :]


def put_row(ref, row, value):
    ref[pl.ds(pl.multiple_of(row * SUBLANES, SUBLANES), SUBLANES), :] = value


def clear_rows(ref, rows):
    zero = jnp.zeros((SUBLANES * SUBLANES, LANES), F32)

    def step(i, carry):
        ref[pl.ds(pl.multiple_of(i * SUBLANES * SUBLANES, SUBLANES), SUBLANES * SUBLANES), :] = zero
        return carry

    lax.fori_loop(0, rows // SUBLANES, step, 0)


def walk(first, last, entry):
    count = last - first
    groups = count // UNROLL

    def group(i, carry):
        for u in range(UNROLL):
            entry(first + i * UNROLL + u)
        return carry

    def single(k, carry):
        entry(k)
        return carry

    lax.fori_loop(0, groups, group, 0)
    lax.fori_loop(first + groups * UNROLL, last, single, 0)


def window_start(first, length):
    return pl.multiple_of(jnp.minimum(lax.div(first, LANES) * LANES, length - WINDOW), LANES)


def forward_kernel(blocks, length, bounds, table, query, bias, codes, shares, hidden, pooled, hidden_rows, pooled_rows):
    step = pl.program_id(0)
    width = table.shape[1]
    chunks = width // LANES
    sub = 128

    @pl.when(step < blocks)
    def _():
        def part(j, carry):
            start = pl.multiple_of(j * sub, sub)
            pre = jnp.dot(table[pl.ds(start, sub), :], query[...], preferred_element_type=F32) + bias[...]
            tiny = jnp.finfo(BF16).tiny
            kept = jnp.where(pre > 0, jnp.maximum(pre, tiny), 0.0).astype(BF16)
            hidden[pl.ds(start, sub), :] = kept
            wide = kept.astype(F32)
            base = (step * ROW_BLOCK + start) * SUBLANES
            for g in range(sub // SUBLANES):
                for c in range(chunks):
                    hidden_rows[pl.ds(base + g * SUBLANES * SUBLANES + c, SUBLANES, stride=SUBLANES), :] = wide[
                        g * SUBLANES : (g + 1) * SUBLANES, c * LANES : (c + 1) * LANES
                    ]
            return carry

        lax.fori_loop(0, ROW_BLOCK // sub, part, 0)

    @pl.when(step >= blocks)
    def _():
        device = step - blocks
        targets = pooled.shape[0]
        clear_rows(pooled_rows, targets)

        def entry(k):
            code = codes[0, 0, k]
            node = lax.shift_right_logical(code, 8)
            target = code & (SHIFT - 1)
            put_row(
                pooled_rows,
                target,
                row_at(pooled_rows, target) + shares[0, 0, k] * row_at(hidden_rows, node),
            )

        base = window_start(bounds[device, 0], length)
        walk(bounds[device, 0] - base, bounds[device, 1] - base, entry)

        def part(g, carry):
            for c in range(chunks):
                pooled[
                    pl.ds(pl.multiple_of(g * SUBLANES, SUBLANES), SUBLANES), c * LANES : (c + 1) * LANES
                ] = pooled_rows[pl.ds(g * SUBLANES * SUBLANES + c, SUBLANES, stride=SUBLANES), :]
            return carry

        lax.fori_loop(0, targets // SUBLANES, part, 0)


def owner_forward(table, query, bias, codes, shares, bounds, targets):
    rows, width = table.shape
    blocks = rows // ROW_BLOCK
    devices, _, length = codes.shape

    def list_block(i, bounds):
        k = jnp.maximum(i - blocks, 0)
        return (k, 0, window_start(bounds[k, 0], length))

    window = (pl.Element(1), pl.Element(1), pl.Element(WINDOW))
    return pl.pallas_call(
        functools.partial(forward_kernel, blocks, length),
        grid_spec=pltpu.PrefetchScalarGridSpec(
            num_scalar_prefetch=1,
            grid=(blocks + devices,),
            in_specs=[
                pl.BlockSpec((ROW_BLOCK, width), lambda i, b: (jnp.minimum(i, blocks - 1), 0)),
                pl.BlockSpec((width, width), lambda i, b: (0, 0)),
                pl.BlockSpec((1, width), lambda i, b: (0, 0)),
                pl.BlockSpec(window, list_block, memory_space=pltpu.SMEM),
                pl.BlockSpec(window, list_block, memory_space=pltpu.SMEM),
            ],
            out_specs=[
                pl.BlockSpec((ROW_BLOCK, width), lambda i, b: (jnp.minimum(i, blocks - 1), 0)),
                pl.BlockSpec((targets, width), lambda i, b: (jnp.maximum(i - blocks, 0), 0)),
            ],
            scratch_shapes=[
                pltpu.VMEM((rows * SUBLANES, LANES), F32),
                pltpu.VMEM((targets * SUBLANES, LANES), F32),
            ],
        ),
        out_shape=[
            jax.ShapeDtypeStruct((rows, width), BF16),
            jax.ShapeDtypeStruct((devices * targets, width), F32),
        ],
        compiler_params=pltpu.CompilerParams(vmem_limit_bytes=VMEM_BYTES),
        cost_estimate=pl.CostEstimate(
            flops=2 * rows * width * width, bytes_accessed=4 * rows * width, transcendentals=0
        ),
        name="owner_forward",
    )(bounds, table, query, bias.reshape(1, width), codes, shares)


def spread_rows(source, rows_here):
    targets, width = source.shape
    chunks = width // LANES
    tile = SUBLANES * SUBLANES

    def part(g, sums):
        both = source[pl.ds(pl.multiple_of(g * 16, 16), 16), :].astype(F32)
        for h in range(2):
            for c in range(chunks):
                rows_here[pl.ds((g * 2 + h) * tile + c, SUBLANES, stride=SUBLANES), :] = both[
                    h * SUBLANES : (h + 1) * SUBLANES, c * LANES : (c + 1) * LANES
                ]
        return sums + both[:SUBLANES] + both[SUBLANES:]

    return lax.fori_loop(0, targets // 16, part, jnp.zeros((SUBLANES, width), F32))


def backward_kernel(
    requesters,
    length,
    place,
    bounds,
    codes,
    shares,
    self_codes,
    grads,
    hidden,
    table_own,
    table_other,
    mix_pooled,
    grad_pre,
    self_sums,
    weight_grad,
    weight_send,
    mix_bias_grad,
    near_total,
    self_total,
    rows_here,
    near_sums,
    weight_sum,
    bias_sum,
):
    step = pl.program_id(0)
    block, width = hidden.shape
    rows = near_total.shape[0] // SUBLANES
    part_rows = weight_sum.shape[0]
    chunks = width // LANES
    tile = SUBLANES * SUBLANES

    @pl.when(step == 0)
    def _():
        clear_rows(near_total, rows)
        clear_rows(self_total, rows)
        mix_bias_grad[...] = jnp.zeros_like(mix_bias_grad)
        bias_sum[...] = jnp.zeros_like(bias_sum)
        weight_grad[...] = jnp.zeros_like(weight_grad)
        weight_sum[...] = jnp.zeros_like(weight_sum)

    @pl.when(step < requesters)
    def _():
        mix_bias_grad[...] += spread_rows(grads, rows_here)
        first_row = lax.rem(place[0], SPLIT) * rows

        def parts_of(code):
            return lax.shift_right_logical(code, 8) - first_row, code & (SHIFT - 1)

        base = window_start(bounds[step, 0], length)

        def entry(k):
            node, target = parts_of(codes[0, 0, k])
            put_row(near_total, node, row_at(near_total, node) + shares[0, 0, k] * row_at(rows_here, target))

        walk(bounds[step, 0] - base, bounds[step, 1] - base, entry)

        def self_entry(k):
            node, target = parts_of(self_codes[0, 0, k])
            put_row(self_total, node, row_at(self_total, node) + row_at(rows_here, target))

        walk(bounds[step, 2], bounds[step, 3], self_entry)

    @pl.when(step >= requesters)
    def _():
        base = (step - requesters) * (block // SUBLANES)

        def part(g, carry):
            where = pl.ds(pl.multiple_of(g * 16, 16), 16)
            for total, sums in ((near_total, near_sums), (self_total, self_sums)):
                for c in range(chunks):
                    halves = [
                        total[pl.ds((base + g * 2 + h) * tile + c, SUBLANES, stride=SUBLANES), :] for h in range(2)
                    ]
                    sums[where, c * LANES : (c + 1) * LANES] = jnp.concatenate(halves, axis=0).astype(BF16)
            return carry

        lax.fori_loop(0, block // 16, part, 0)
        turned = (((1,), (1,)), ((), ()))
        raw = lax.dot_general(near_sums[...], mix_pooled[...], turned, preferred_element_type=F32)
        wide = jnp.where(hidden[...].astype(F32) > 0, raw, 0.0)
        bias_sum[...] += jnp.sum(wide.reshape(block // SUBLANES, SUBLANES, width), axis=0)
        kept = wide.astype(BF16)
        grad_pre[...] = kept
        down = (((0,), (0,)), ((), ()))
        weight_grad[:part_rows] += lax.dot_general(table_own[...], kept, down, preferred_element_type=F32)
        weight_sum[...] += lax.dot_general(table_other[...], kept, down, preferred_element_type=F32)

    @pl.when(step == pl.num_programs(0) - 1)
    def _():
        bias = jnp.broadcast_to(jnp.sum(bias_sum[...], axis=0, keepdims=True), (BIAS_ROWS, width))
        weight_grad[part_rows:] = bias
        weight_send[:part_rows] = weight_sum[...].astype(BF16)
        weight_send[part_rows:] = bias.astype(BF16)


def owner_backward(table, hidden, grads, mix, codes, shares, self_codes, bounds, place, owners, groups, targets):
    rows_owned, width = table.shape
    rows = rows_owned // SPLIT
    blocks = rows // ROW_BLOCK
    requesters, _, length = codes.shape
    self_length = self_codes.shape[2]
    part = width // groups

    def requester(i):
        return jnp.minimum(i, requesters - 1)

    def node_row(i, place):
        return lax.rem(place[0], SPLIT) * blocks + jnp.maximum(i - requesters, 0)

    def list_block(i, place, bounds):
        k = requester(i)
        return (k, 0, window_start(bounds[k, 0], length))

    def grad_block(i, place, bounds):
        k = requester(i)
        return (lax.rem(k, owners) * groups + lax.div(k, owners), 0)

    def table_columns(which):
        return pl.BlockSpec((ROW_BLOCK, part), lambda i, place, bounds: (node_row(i, place), place[which]))

    def fixed(shape):
        return pl.BlockSpec(shape, lambda i, place, bounds: (0, 0))

    window = (pl.Element(1), pl.Element(1), pl.Element(WINDOW))
    return pl.pallas_call(
        functools.partial(backward_kernel, requesters, length),
        grid_spec=pltpu.PrefetchScalarGridSpec(
            num_scalar_prefetch=2,
            grid=(requesters + blocks,),
            in_specs=[
                pl.BlockSpec(window, list_block, memory_space=pltpu.SMEM),
                pl.BlockSpec(window, list_block, memory_space=pltpu.SMEM),
                pl.BlockSpec(
                    (1, 1, self_length), lambda i, place, bounds: (requester(i), 0, 0), memory_space=pltpu.SMEM
                ),
                pl.BlockSpec((targets, width), grad_block),
                pl.BlockSpec((ROW_BLOCK, width), lambda i, place, bounds: (node_row(i, place), 0)),
                table_columns(0),
                table_columns(1),
                pl.BlockSpec((width, width), lambda i, place, bounds: (1, 0), pipeline_mode=pl.Buffered(1)),
            ],
            out_specs=[
                pl.BlockSpec((ROW_BLOCK, width), lambda i, place, bounds: (jnp.maximum(i - requesters, 0), 0)),
                pl.BlockSpec((ROW_BLOCK, width), lambda i, place, bounds: (jnp.maximum(i - requesters, 0), 0)),
                fixed((part + BIAS_ROWS, width)),
                fixed((part + BIAS_ROWS, width)),
                fixed((SUBLANES, width)),
            ],
            scratch_shapes=[
                pltpu.VMEM((rows * SUBLANES, LANES), F32),
                pltpu.VMEM((rows * SUBLANES, LANES), F32),
                pltpu.VMEM((targets * SUBLANES, LANES), F32),
                pltpu.VMEM((ROW_BLOCK, width), BF16),
                pltpu.VMEM((part, width), F32),
                pltpu.VMEM((SUBLANES, width), F32),
            ],
        ),
        out_shape=[
            jax.ShapeDtypeStruct((rows, width), BF16),
            jax.ShapeDtypeStruct((rows, width), BF16),
            jax.ShapeDtypeStruct((part + BIAS_ROWS, width), F32),
            jax.ShapeDtypeStruct((part + BIAS_ROWS, width), BF16),
            jax.ShapeDtypeStruct((SUBLANES, width), F32),
        ],
        compiler_params=pltpu.CompilerParams(vmem_limit_bytes=VMEM_BYTES),
        cost_estimate=pl.CostEstimate(
            flops=8 * rows * width * width, bytes_accessed=4 * requesters * targets * width, transcendentals=0
        ),
        name="owner_backward",
    )(
        place,
        bounds,
        codes,
        shares,
        self_codes,
        grads,
        hidden,
        table,
        table,
        mix,
    )


def table_kernel(place, grad_pre, self_sums, query, mix_self, *outs):
    turned = (((1,), (1,)), ((), ()))
    grad = lax.dot_general(grad_pre[...], query[...], turned, preferred_element_type=F32) + lax.dot_general(
        self_sums[...], mix_self[...], turned, preferred_element_type=F32
    )
    at = 0
    for out in outs:
        out[...] = grad[:, at : at + out.shape[1]].astype(out.dtype)
        at += out.shape[1]


def table_columns_grad(grad_pre, self_sums, query, mix, place, part, kept_rows=None):
    rows, width = grad_pre.shape
    blocks = rows // ROW_BLOCK

    def node_block(i, place):
        return (i, 0)

    weights = pl.BlockSpec((part, width), lambda i, place: (place[0], 0), pipeline_mode=pl.Buffered(1))
    if kept_rows is None:
        out_specs = [pl.BlockSpec((ROW_BLOCK, part // 2), node_block)] * 2
        out_shape = [jax.ShapeDtypeStruct((rows, part // 2), BF16)] * 2
    else:
        out_specs = [pl.BlockSpec((ROW_BLOCK, part), lambda i, place: (lax.rem(place[0], SPLIT) * blocks + i, 0))]
        out_shape = [jax.ShapeDtypeStruct((kept_rows, part), F32)]
    return pl.pallas_call(
        table_kernel,
        grid_spec=pltpu.PrefetchScalarGridSpec(
            num_scalar_prefetch=1,
            grid=(blocks,),
            in_specs=[pl.BlockSpec((ROW_BLOCK, width), node_block)] * 2 + [weights] * 2,
            out_specs=out_specs,
        ),
        out_shape=out_shape,
        compiler_params=pltpu.CompilerParams(vmem_limit_bytes=VMEM_BYTES),
        cost_estimate=pl.CostEstimate(
            flops=4 * rows * width * part, bytes_accessed=4 * rows * width, transcendentals=0
        ),
        name="table_columns_grad",
    )(place, grad_pre, self_sums, query, mix)


def padded(values, length):
    return jnp.pad(values, (0, length - values.shape[0]))


def local(
    feature_table,
    neighbour_query_weight,
    query_bias,
    mix_weight,
    mix_bias,
    lookup_ids,
    present_counts,
    importance,
    embed_cot,
):
    owners = lax.axis_size("table")
    groups = lax.axis_size("rep")
    devices = owners * groups
    rows_owned, width = feature_table.shape
    batch_rows, slot_count = lookup_ids.shape
    near = slot_count - 1
    owner = lax.axis_index("table").astype(I32)
    group = lax.axis_index("rep").astype(I32)

    present = (jnp.arange(near, dtype=I32)[None, :] < present_counts[:, None]).astype(F32)
    masked_weight = importance * present
    shares = lax.reduce_precision(masked_weight / jnp.sum(masked_weight, axis=1, keepdims=True), 8, 7)
    live_most = batch_rows // 2 * (near + 5)
    length = -(-live_most // LANES) * LANES
    target = jnp.arange(batch_rows, dtype=I32)
    keys = jnp.where(present > 0, lookup_ids[:, 1:] * SHIFT + target[:, None], jnp.iinfo(I32).max)
    keys, sorted_shares = lax.sort((keys.reshape(-1), shares.reshape(-1)), num_keys=1, is_stable=False)
    keys = keys[:live_most]
    sorted_shares = sorted_shares[:live_most]
    own_keys = lax.sort(lookup_ids[:, 0] * SHIFT + target)
    edges = jnp.arange(owners * SPLIT + 1, dtype=I32) * (rows_owned // SPLIT * SHIFT)
    starts = jnp.sum((keys[None, :] < edges[:, None]).astype(I32), axis=1)
    own_starts = jnp.sum((own_keys[None, :] < edges[:, None]).astype(I32), axis=1)
    own_length = SHIFT
    meta = jnp.concatenate(
        [
            starts.astype(F32),
            own_starts.astype(F32),
            jnp.stack([jnp.sum(present), jnp.sum(masked_weight)]),
        ]
    )
    meta_length = -(-meta.shape[0] // LANES) * LANES

    def as_code(key):
        return (key % (rows_owned * SHIFT)).astype(F32)

    request = jnp.concatenate(
        [
            padded(as_code(keys), length),
            padded(sorted_shares, length),
            padded(as_code(own_keys), own_length),
            padded(meta, meta_length),
            padded(lookup_ids[:, 0].astype(F32), own_length),
        ]
    )
    plane = lax.all_gather(request, "table", axis=0)

    own_ids = plane[:, -own_length:][:, :batch_rows].astype(I32).reshape(-1)
    wanted = own_ids - owner * rows_owned
    mine = (wanted >= 0) & (wanted < rows_owned)
    found = feature_table[jnp.clip(wanted, 0, rows_owned - 1)]
    found = jnp.where(mine[:, None], found, jnp.zeros((), BF16))
    self_rows = lax.psum_scatter(found, "table", scatter_dimension=0, tiled=True)
    every = lax.all_gather(plane, "rep", axis=0).reshape(devices, -1)

    def unpack(lists, start, stride):
        count = lists.shape[0]
        at = 2 * length
        codes = lists[:, :length].astype(I32).reshape(count, 1, length)
        parts = lists[:, length:at].reshape(count, 1, length)
        own_codes = lists[:, at : at + own_length].astype(I32).reshape(count, 1, own_length)
        notes = lists[:, at + own_length :]
        first = lax.dynamic_slice(notes, (0, start), (count, stride + 1))[:, ::stride]
        own_first = lax.dynamic_slice(notes, (0, start + owners * SPLIT + 1), (count, stride + 1))[:, ::stride]
        bounds = jnp.concatenate([first, own_first], axis=1).astype(I32)
        sums = jnp.sum(notes[:, 2 * (owners * SPLIT + 1) : 2 * (owners * SPLIT + 2)], axis=0)
        return codes, parts, own_codes, bounds, sums

    codes, parts, _, bounds, _ = unpack(plane, owner * SPLIT, SPLIT)
    bounds, _ = lax.optimization_barrier((bounds, found))
    hidden, pooled_parts = owner_forward(
        feature_table, neighbour_query_weight, query_bias, codes, parts, bounds, batch_rows
    )
    pooled_parts, self_rows = lax.optimization_barrier((pooled_parts, self_rows))
    pooled = lax.psum_scatter(pooled_parts, "table", scatter_dimension=0, tiled=True)
    half = lax.rem(group, SPLIT)
    pooled, lists = lax.optimization_barrier((pooled, unpack(every, owner * SPLIT + half, 1)))
    all_codes, all_parts, all_own_codes, all_bounds, sums = lists
    pooled = lax.reduce_precision(pooled, 8, 7).astype(BF16)

    joined = jnp.concatenate([self_rows, pooled], axis=1)
    mixed = jnp.dot(joined, mix_weight, preferred_element_type=F32) + mix_bias
    activation = jax.nn.relu(mixed)
    inverse = lax.rsqrt(jnp.mean(activation * activation, axis=1, keepdims=True) + 1e-06)
    embed = (activation * inverse).astype(BF16)
    cotangent = embed_cot.astype(F32)
    grad_act = inverse * cotangent - activation * (inverse * inverse * inverse) * jnp.mean(
        activation * cotangent, axis=1, keepdims=True
    )
    grad_mixed = jnp.where(mixed > 0, grad_act, 0.0).astype(BF16)
    all_mixed = lax.all_gather(grad_mixed, ("table", "rep"), axis=0, tiled=True)
    mix_part = 2 * width // devices
    columns = lax.all_to_all(
        joined.reshape(batch_rows, devices, mix_part).transpose(1, 0, 2),
        ("table", "rep"),
        split_axis=0,
        concat_axis=0,
        tiled=True,
    ).reshape(devices * batch_rows, mix_part)

    mix_rows = lax.dot_general(
        columns, all_mixed, (((0,), (0,)), ((), ())), preferred_element_type=F32
    ).astype(BF16)
    all_mixed, mix_rows = lax.optimization_barrier((all_mixed, mix_rows))
    mix_gathered = lax.all_gather(mix_rows, ("table", "rep"), axis=0, tiled=True)

    partner = group + 1 - 2 * half
    swap = [(i, i + 1 - 2 * (i % SPLIT)) for i in range(groups)]
    grad_pre, self_sums, query_part, query_send, mix_bias_part = owner_backward(
        feature_table,
        hidden,
        all_mixed,
        mix_weight,
        all_codes,
        all_parts,
        all_own_codes,
        all_bounds,
        jnp.stack([group, partner]),
        owners,
        groups,
        batch_rows,
    )
    part = width // groups
    send_first, send_last = table_columns_grad(
        grad_pre, self_sums, neighbour_query_weight, mix_weight, partner.reshape(1), part
    )
    (table_grad,) = table_columns_grad(
        grad_pre, self_sums, neighbour_query_weight, mix_weight, group.reshape(1), part, rows_owned
    )
    mix_bias_grad = jnp.sum(mix_bias_part, axis=0)

    query_rows = width // devices
    query_part = query_part + lax.ppermute(query_send, "rep", swap).astype(F32)
    send_first, mix_gathered = lax.optimization_barrier((send_first, mix_gathered))
    mix_weight_grad = mix_gathered.astype(F32)
    got_first = lax.ppermute(send_first, "rep", swap)
    bias_rows = SUBLANES
    outgoing = jnp.concatenate(
        [
            query_part[:part].reshape(owners, query_rows, width),
            jnp.broadcast_to(query_part[part : part + bias_rows], (owners, bias_rows, width)),
        ],
        axis=1,
    )
    incoming = lax.all_to_all(outgoing.astype(BF16), "table", split_axis=0, concat_axis=0, tiled=True)
    summed = jnp.sum(incoming.astype(F32), axis=0)
    query_bias_grad = summed[query_rows]
    summed, got_first, table_grad, mix_weight_grad = lax.optimization_barrier(
        (summed, got_first, table_grad, mix_weight_grad)
    )
    got_last = lax.ppermute(send_last, "rep", swap)
    table_got = jnp.concatenate([got_first, got_last], axis=1)
    column = lax.all_to_all(
        jnp.broadcast_to(summed[:query_rows].astype(BF16), (groups, query_rows, width)),
        "rep",
        split_axis=0,
        concat_axis=0,
        tiled=True,
    )
    gathered = lax.all_to_all(
        jnp.broadcast_to(column, (owners, groups, query_rows, width)), "table", split_axis=0, concat_axis=0, tiled=True
    )
    query_weight_grad = gathered.transpose(1, 0, 2, 3).reshape(width, width).astype(F32)
    table_grad = lax.dynamic_update_slice(
        table_grad, table_got.astype(F32), ((1 - half) * (rows_owned // SPLIT), 0)
    )
    statistics = sums / (batch_rows * devices)
    return (
        embed,
        table_grad,
        query_weight_grad,
        query_bias_grad,
        mix_weight_grad,
        mix_bias_grad,
        statistics,
    )


def solution(mesh):
    in_specs = (
        P("table", None),
        P(),
        P(),
        P(),
        P(),
        P(("table", "rep"), None),
        P(("table", "rep")),
        P(("table", "rep"), None),
        P(("table", "rep"), None),
    )
    out_specs = (P(("table", "rep"), None), P("table", "rep"), P(), P(), P(), P(), P())
    return jax.shard_map(local, mesh=mesh, in_specs=in_specs, out_specs=out_specs, check_vma=False)
```

```python
import functools

import jax
import jax.numpy as jnp
from jax import lax
from jax.experimental import pallas as pl
from jax.experimental.layout import Layout, with_layout_constraint
from jax.experimental.pallas import tpu as pltpu
from jax.sharding import PartitionSpec as P

F32 = jnp.float32
BF16 = jnp.bfloat16
I32 = jnp.int32
LANES = 128
SUBLANES = 8
ROW_BLOCK = 512
SHIFT = 256
BIAS_ROWS = 16
SPLIT = 2
WINDOW = 1536
UNROLL = 4
VMEM_BYTES = 60 << 20


def row_at(ref, row):
    return ref[pl.ds(pl.multiple_of(row * SUBLANES, SUBLANES), SUBLANES), :]


def put_row(ref, row, value):
    ref[pl.ds(pl.multiple_of(row * SUBLANES, SUBLANES), SUBLANES), :] = value


def clear_rows(ref, rows):
    zero = jnp.zeros((SUBLANES * SUBLANES, LANES), F32)

    def step(i, carry):
        ref[pl.ds(pl.multiple_of(i * SUBLANES * SUBLANES, SUBLANES), SUBLANES * SUBLANES), :] = zero
        return carry

    lax.fori_loop(0, rows // SUBLANES, step, 0)


def walk(first, last, entry):
    count = last - first
    groups = count // UNROLL

    def group(i, carry):
        for u in range(UNROLL):
            entry(first + i * UNROLL + u)
        return carry

    def single(k, carry):
        entry(k)
        return carry

    lax.fori_loop(0, groups, group, 0)
    lax.fori_loop(first + groups * UNROLL, last, single, 0)


def window_start(first, length):
    return pl.multiple_of(jnp.minimum(lax.div(first, LANES) * LANES, length - WINDOW), LANES)


def forward_kernel(blocks, length, bounds, table, query, bias, codes, shares, hidden, pooled, hidden_rows, pooled_rows):
    step = pl.program_id(0)
    width = table.shape[1]
    chunks = width // LANES
    sub = 128

    @pl.when(step < blocks)
    def _():
        def part(j, carry):
            start = pl.multiple_of(j * sub, sub)
            pre = jnp.dot(table[pl.ds(start, sub), :], query[...], preferred_element_type=F32) + bias[...]
            tiny = jnp.finfo(BF16).tiny
            kept = jnp.where(pre > 0, jnp.maximum(pre, tiny), 0.0).astype(BF16)
            hidden[pl.ds(start, sub), :] = kept
            wide = kept.astype(F32)
            base = (step * ROW_BLOCK + start) * SUBLANES
            for g in range(sub // SUBLANES):
                for c in range(chunks):
                    hidden_rows[pl.ds(base + g * SUBLANES * SUBLANES + c, SUBLANES, stride=SUBLANES), :] = wide[
                        g * SUBLANES : (g + 1) * SUBLANES, c * LANES : (c + 1) * LANES
                    ]
            return carry

        lax.fori_loop(0, ROW_BLOCK // sub, part, 0)

    @pl.when(step >= blocks)
    def _():
        device = step - blocks
        targets = pooled.shape[0]
        clear_rows(pooled_rows, targets)

        def entry(k):
            code = codes[0, 0, k]
            node = lax.shift_right_logical(code, 8)
            target = code & (SHIFT - 1)
            put_row(
                pooled_rows,
                target,
                row_at(pooled_rows, target) + shares[0, 0, k] * row_at(hidden_rows, node),
            )

        base = window_start(bounds[device, 0], length)
        walk(bounds[device, 0] - base, bounds[device, 1] - base, entry)

        def part(g, carry):
            for c in range(chunks):
                pooled[
                    pl.ds(pl.multiple_of(g * SUBLANES, SUBLANES), SUBLANES), c * LANES : (c + 1) * LANES
                ] = pooled_rows[pl.ds(g * SUBLANES * SUBLANES + c, SUBLANES, stride=SUBLANES), :]
            return carry

        lax.fori_loop(0, targets // SUBLANES, part, 0)


def owner_forward(table, query, bias, codes, shares, bounds, targets):
    rows, width = table.shape
    blocks = rows // ROW_BLOCK
    devices, _, length = codes.shape

    def list_block(i, bounds):
        k = jnp.maximum(i - blocks, 0)
        return (k, 0, window_start(bounds[k, 0], length))

    window = (pl.Element(1), pl.Element(1), pl.Element(WINDOW))
    return pl.pallas_call(
        functools.partial(forward_kernel, blocks, length),
        grid_spec=pltpu.PrefetchScalarGridSpec(
            num_scalar_prefetch=1,
            grid=(blocks + devices,),
            in_specs=[
                pl.BlockSpec((ROW_BLOCK, width), lambda i, b: (jnp.minimum(i, blocks - 1), 0)),
                pl.BlockSpec((width, width), lambda i, b: (0, 0)),
                pl.BlockSpec((1, width), lambda i, b: (0, 0)),
                pl.BlockSpec(window, list_block, memory_space=pltpu.SMEM),
                pl.BlockSpec(window, list_block, memory_space=pltpu.SMEM),
            ],
            out_specs=[
                pl.BlockSpec((ROW_BLOCK, width), lambda i, b: (jnp.minimum(i, blocks - 1), 0)),
                pl.BlockSpec((targets, width), lambda i, b: (jnp.maximum(i - blocks, 0), 0)),
            ],
            scratch_shapes=[
                pltpu.VMEM((rows * SUBLANES, LANES), F32),
                pltpu.VMEM((targets * SUBLANES, LANES), F32),
            ],
        ),
        out_shape=[
            jax.ShapeDtypeStruct((rows, width), BF16),
            jax.ShapeDtypeStruct((devices * targets, width), F32),
        ],
        compiler_params=pltpu.CompilerParams(vmem_limit_bytes=VMEM_BYTES),
        cost_estimate=pl.CostEstimate(
            flops=2 * rows * width * width, bytes_accessed=4 * rows * width, transcendentals=0
        ),
        name="owner_forward",
    )(bounds, table, query, bias.reshape(1, width), codes, shares)


def spread_rows(source, rows_here):
    targets, width = source.shape
    chunks = width // LANES
    tile = SUBLANES * SUBLANES

    def part(g, sums):
        both = source[pl.ds(pl.multiple_of(g * 16, 16), 16), :].astype(F32)
        for h in range(2):
            for c in range(chunks):
                rows_here[pl.ds((g * 2 + h) * tile + c, SUBLANES, stride=SUBLANES), :] = both[
                    h * SUBLANES : (h + 1) * SUBLANES, c * LANES : (c + 1) * LANES
                ]
        return sums + both[:SUBLANES] + both[SUBLANES:]

    return lax.fori_loop(0, targets // 16, part, jnp.zeros((SUBLANES, width), F32))


def backward_kernel(
    requesters,
    length,
    place,
    bounds,
    codes,
    shares,
    self_codes,
    grads,
    hidden,
    table_own,
    table_other,
    mix_pooled,
    grad_pre,
    self_sums,
    weight_grad,
    weight_send,
    mix_bias_grad,
    near_total,
    self_total,
    rows_here,
    near_sums,
    weight_sum,
    bias_sum,
):
    step = pl.program_id(0)
    block, width = hidden.shape
    rows = near_total.shape[0] // SUBLANES
    part_rows = weight_sum.shape[0]
    chunks = width // LANES
    tile = SUBLANES * SUBLANES

    @pl.when(step == 0)
    def _():
        clear_rows(near_total, rows)
        clear_rows(self_total, rows)
        mix_bias_grad[...] = jnp.zeros_like(mix_bias_grad)
        bias_sum[...] = jnp.zeros_like(bias_sum)
        weight_grad[...] = jnp.zeros_like(weight_grad)
        weight_sum[...] = jnp.zeros_like(weight_sum)

    @pl.when(step < requesters)
    def _():
        mix_bias_grad[...] += spread_rows(grads, rows_here)
        first_row = lax.rem(place[0], SPLIT) * rows

        def parts_of(code):
            return lax.shift_right_logical(code, 8) - first_row, code & (SHIFT - 1)

        base = window_start(bounds[step, 0], length)

        def entry(k):
            node, target = parts_of(codes[0, 0, k])
            put_row(near_total, node, row_at(near_total, node) + shares[0, 0, k] * row_at(rows_here, target))

        walk(bounds[step, 0] - base, bounds[step, 1] - base, entry)

        def self_entry(k):
            node, target = parts_of(self_codes[0, 0, k])
            put_row(self_total, node, row_at(self_total, node) + row_at(rows_here, target))

        walk(bounds[step, 2], bounds[step, 3], self_entry)

    @pl.when(step >= requesters)
    def _():
        base = (step - requesters) * (block // SUBLANES)

        def part(g, carry):
            where = pl.ds(pl.multiple_of(g * 16, 16), 16)
            for total, sums in ((near_total, near_sums), (self_total, self_sums)):
                for c in range(chunks):
                    halves = [
                        total[pl.ds((base + g * 2 + h) * tile + c, SUBLANES, stride=SUBLANES), :] for h in range(2)
                    ]
                    sums[where, c * LANES : (c + 1) * LANES] = jnp.concatenate(halves, axis=0).astype(BF16)
            return carry

        lax.fori_loop(0, block // 16, part, 0)
        turned = (((1,), (1,)), ((), ()))
        raw = lax.dot_general(near_sums[...], mix_pooled[...], turned, preferred_element_type=F32)
        wide = jnp.where(hidden[...].astype(F32) > 0, raw, 0.0)
        bias_sum[...] += jnp.sum(wide.reshape(block // SUBLANES, SUBLANES, width), axis=0)
        kept = wide.astype(BF16)
        grad_pre[...] = kept
        down = (((0,), (0,)), ((), ()))
        weight_grad[:part_rows] += lax.dot_general(table_own[...], kept, down, preferred_element_type=F32)
        weight_sum[...] += lax.dot_general(table_other[...], kept, down, preferred_element_type=F32)

    @pl.when(step == pl.num_programs(0) - 1)
    def _():
        bias = jnp.broadcast_to(jnp.sum(bias_sum[...], axis=0, keepdims=True), (BIAS_ROWS, width))
        weight_grad[part_rows:] = bias
        weight_send[:part_rows] = weight_sum[...].astype(BF16)
        weight_send[part_rows:] = bias.astype(BF16)


def owner_backward(table, hidden, grads, mix, codes, shares, self_codes, bounds, place, owners, groups, targets):
    rows_owned, width = table.shape
    rows = rows_owned // SPLIT
    blocks = rows // ROW_BLOCK
    requesters, _, length = codes.shape
    self_length = self_codes.shape[2]
    part = width // groups

    def requester(i):
        return jnp.minimum(i, requesters - 1)

    def node_row(i, place):
        return lax.rem(place[0], SPLIT) * blocks + jnp.maximum(i - requesters, 0)

    def list_block(i, place, bounds):
        k = requester(i)
        return (k, 0, window_start(bounds[k, 0], length))

    def grad_block(i, place, bounds):
        k = requester(i)
        return (lax.rem(k, owners) * groups + lax.div(k, owners), 0)

    def table_columns(which):
        return pl.BlockSpec((ROW_BLOCK, part), lambda i, place, bounds: (node_row(i, place), place[which]))

    def fixed(shape):
        return pl.BlockSpec(shape, lambda i, place, bounds: (0, 0))

    window = (pl.Element(1), pl.Element(1), pl.Element(WINDOW))
    return pl.pallas_call(
        functools.partial(backward_kernel, requesters, length),
        grid_spec=pltpu.PrefetchScalarGridSpec(
            num_scalar_prefetch=2,
            grid=(requesters + blocks,),
            in_specs=[
                pl.BlockSpec(window, list_block, memory_space=pltpu.SMEM),
                pl.BlockSpec(window, list_block, memory_space=pltpu.SMEM),
                pl.BlockSpec(
                    (1, 1, self_length), lambda i, place, bounds: (requester(i), 0, 0), memory_space=pltpu.SMEM
                ),
                pl.BlockSpec((targets, width), grad_block),
                pl.BlockSpec((ROW_BLOCK, width), lambda i, place, bounds: (node_row(i, place), 0)),
                table_columns(0),
                table_columns(1),
                pl.BlockSpec((width, width), lambda i, place, bounds: (1, 0), pipeline_mode=pl.Buffered(1)),
            ],
            out_specs=[
                pl.BlockSpec((ROW_BLOCK, width), lambda i, place, bounds: (jnp.maximum(i - requesters, 0), 0)),
                pl.BlockSpec((ROW_BLOCK, width), lambda i, place, bounds: (jnp.maximum(i - requesters, 0), 0)),
                fixed((part + BIAS_ROWS, width)),
                fixed((part + BIAS_ROWS, width)),
                fixed((SUBLANES, width)),
            ],
            scratch_shapes=[
                pltpu.VMEM((rows * SUBLANES, LANES), F32),
                pltpu.VMEM((rows * SUBLANES, LANES), F32),
                pltpu.VMEM((targets * SUBLANES, LANES), F32),
                pltpu.VMEM((ROW_BLOCK, width), BF16),
                pltpu.VMEM((part, width), F32),
                pltpu.VMEM((SUBLANES, width), F32),
            ],
        ),
        out_shape=[
            jax.ShapeDtypeStruct((rows, width), BF16),
            jax.ShapeDtypeStruct((rows, width), BF16),
            jax.ShapeDtypeStruct((part + BIAS_ROWS, width), F32),
            jax.ShapeDtypeStruct((part + BIAS_ROWS, width), BF16),
            jax.ShapeDtypeStruct((SUBLANES, width), F32),
        ],
        compiler_params=pltpu.CompilerParams(vmem_limit_bytes=VMEM_BYTES),
        cost_estimate=pl.CostEstimate(
            flops=8 * rows * width * width, bytes_accessed=4 * requesters * targets * width, transcendentals=0
        ),
        name="owner_backward",
    )(
        place,
        bounds,
        codes,
        shares,
        self_codes,
        grads,
        hidden,
        table,
        table,
        mix,
    )


def table_kernel(place, grad_pre, self_sums, query, mix_self, *outs):
    turned = (((1,), (1,)), ((), ()))
    grad = lax.dot_general(grad_pre[...], query[...], turned, preferred_element_type=F32) + lax.dot_general(
        self_sums[...], mix_self[...], turned, preferred_element_type=F32
    )
    at = 0
    for out in outs:
        out[...] = grad[:, at : at + out.shape[1]].astype(out.dtype)
        at += out.shape[1]


def table_columns_grad(grad_pre, self_sums, query, mix, place, part, kept_rows=None):
    rows, width = grad_pre.shape
    blocks = rows // ROW_BLOCK

    def node_block(i, place):
        return (i, 0)

    weights = pl.BlockSpec((part, width), lambda i, place: (place[0], 0), pipeline_mode=pl.Buffered(1))
    if kept_rows is None:
        out_specs = [pl.BlockSpec((ROW_BLOCK, part // 2), node_block)] * 2
        out_shape = [jax.ShapeDtypeStruct((rows, part // 2), BF16)] * 2
    else:
        out_specs = [pl.BlockSpec((ROW_BLOCK, part), lambda i, place: (lax.rem(place[0], SPLIT) * blocks + i, 0))]
        out_shape = [jax.ShapeDtypeStruct((kept_rows, part), F32)]
    return pl.pallas_call(
        table_kernel,
        grid_spec=pltpu.PrefetchScalarGridSpec(
            num_scalar_prefetch=1,
            grid=(blocks,),
            in_specs=[pl.BlockSpec((ROW_BLOCK, width), node_block)] * 2 + [weights] * 2,
            out_specs=out_specs,
        ),
        out_shape=out_shape,
        compiler_params=pltpu.CompilerParams(vmem_limit_bytes=VMEM_BYTES),
        cost_estimate=pl.CostEstimate(
            flops=4 * rows * width * part, bytes_accessed=4 * rows * width, transcendentals=0
        ),
        name="table_columns_grad",
    )(place, grad_pre, self_sums, query, mix)


def padded(values, length):
    return jnp.pad(values, (0, length - values.shape[0]))


def local(
    feature_table,
    neighbour_query_weight,
    query_bias,
    mix_weight,
    mix_bias,
    lookup_ids,
    present_counts,
    importance,
    embed_cot,
):
    owners = lax.axis_size("table")
    groups = lax.axis_size("rep")
    devices = owners * groups
    rows_owned, width = feature_table.shape
    batch_rows, slot_count = lookup_ids.shape
    near = slot_count - 1
    owner = lax.axis_index("table").astype(I32)
    group = lax.axis_index("rep").astype(I32)

    present = (jnp.arange(near, dtype=I32)[None, :] < present_counts[:, None]).astype(F32)
    masked_weight = importance * present
    shares = lax.reduce_precision(masked_weight / jnp.sum(masked_weight, axis=1, keepdims=True), 8, 7)
    live_most = batch_rows // 2 * (near + 5)
    length = -(-live_most // LANES) * LANES
    target = jnp.arange(batch_rows, dtype=I32)
    keys = jnp.where(present > 0, lookup_ids[:, 1:] * SHIFT + target[:, None], jnp.iinfo(I32).max)
    keys, sorted_shares = lax.sort((keys.reshape(-1), shares.reshape(-1)), num_keys=1, is_stable=False)
    keys = keys[:live_most]
    sorted_shares = sorted_shares[:live_most]
    edges = jnp.arange(owners * SPLIT + 1, dtype=I32) * (rows_owned // SPLIT * SHIFT)
    starts = jnp.sum((keys[None, :] < edges[:, None]).astype(I32), axis=1)
    own_length = SHIFT
    meta = jnp.concatenate(
        [
            starts.astype(F32),
            jnp.stack([jnp.sum(present), jnp.sum(masked_weight)]),
        ]
    )
    meta_length = -(-meta.shape[0] // LANES) * LANES

    def as_code(key):
        return (key % (rows_owned * SHIFT)).astype(F32)

    request = jnp.concatenate(
        [
            padded(as_code(keys), length),
            padded(sorted_shares, length),
            padded(meta, meta_length),
            padded(lookup_ids[:, 0].astype(F32), own_length),
        ]
    )
    plane = lax.all_gather(request, "table", axis=0)

    own_ids = plane[:, -own_length:][:, :batch_rows].astype(I32).reshape(-1)
    wanted = own_ids - owner * rows_owned
    mine = (wanted >= 0) & (wanted < rows_owned)
    found = feature_table[jnp.clip(wanted, 0, rows_owned - 1)]
    found = jnp.where(mine[:, None], found, jnp.zeros((), BF16))
    self_rows = lax.psum_scatter(found, "table", scatter_dimension=0, tiled=True)
    every = lax.all_gather(plane, "rep", axis=0).reshape(devices, -1)

    def unpack(lists, start, stride):
        count = lists.shape[0]
        at = 2 * length
        codes = lists[:, :length].astype(I32).reshape(count, 1, length)
        parts = lists[:, length:at].reshape(count, 1, length)
        notes = lists[:, at : at + meta_length]
        bounds = lax.dynamic_slice(notes, (0, start), (count, stride + 1))[:, ::stride].astype(I32)
        sums = jnp.sum(notes[:, owners * SPLIT + 1 : owners * SPLIT + 3], axis=0)
        return codes, parts, bounds, sums

    def own_lists(lists, start):
        ids = lists[:, -own_length:][:, :batch_rows].astype(I32)
        keys = lax.sort(ids * SHIFT + target[None, :], dimension=1)
        ends = (start + jnp.arange(2, dtype=I32)) * (rows_owned // SPLIT * SHIFT)
        own_bounds = jnp.sum((keys[:, None, :] < ends[None, :, None]).astype(I32), axis=2)
        own_codes = jnp.pad(keys % (rows_owned * SHIFT), ((0, 0), (0, own_length - batch_rows)))
        return own_codes.reshape(-1, 1, own_length), own_bounds

    codes, parts, bounds, _ = unpack(plane, owner * SPLIT, SPLIT)
    bounds, _ = lax.optimization_barrier((bounds, found))
    hidden, pooled_parts = owner_forward(
        feature_table, neighbour_query_weight, query_bias, codes, parts, bounds, batch_rows
    )
    pooled_parts, self_rows = lax.optimization_barrier((pooled_parts, self_rows))
    pooled = lax.psum_scatter(pooled_parts, "table", scatter_dimension=0, tiled=True)
    half = lax.rem(group, SPLIT)
    all_codes, all_parts, all_bounds, sums = unpack(every, owner * SPLIT + half, 1)
    all_own_codes, own_bounds = own_lists(every, owner * SPLIT + half)
    all_bounds = jnp.concatenate([all_bounds, own_bounds], axis=1)
    rows_major = Layout(major_to_minor=(0, 1, 2))
    all_codes = with_layout_constraint(all_codes, rows_major)
    all_parts = with_layout_constraint(all_parts, rows_major)
    pooled, lists = lax.optimization_barrier((pooled, (all_codes, all_parts, all_own_codes, all_bounds, sums)))
    all_codes, all_parts, all_own_codes, all_bounds, sums = lists
    pooled = lax.reduce_precision(pooled, 8, 7).astype(BF16)

    joined = jnp.concatenate([self_rows, pooled], axis=1)
    mixed = jnp.dot(joined, mix_weight, preferred_element_type=F32) + mix_bias
    activation = jax.nn.relu(mixed)
    inverse = lax.rsqrt(jnp.mean(activation * activation, axis=1, keepdims=True) + 1e-06)
    embed = (activation * inverse).astype(BF16)
    cotangent = embed_cot.astype(F32)
    grad_act = inverse * cotangent - activation * (inverse * inverse * inverse) * jnp.mean(
        activation * cotangent, axis=1, keepdims=True
    )
    grad_mixed = jnp.where(mixed > 0, grad_act, 0.0).astype(BF16)
    all_mixed = lax.all_gather(grad_mixed, ("table", "rep"), axis=0, tiled=True)
    mix_part = 2 * width // devices
    columns = lax.all_to_all(
        joined.reshape(batch_rows, devices, mix_part).transpose(1, 0, 2),
        ("table", "rep"),
        split_axis=0,
        concat_axis=0,
        tiled=True,
    ).reshape(devices * batch_rows, mix_part)

    mix_rows = lax.dot_general(
        columns, all_mixed, (((0,), (0,)), ((), ())), preferred_element_type=F32
    ).astype(BF16)
    all_mixed, mix_rows = lax.optimization_barrier((all_mixed, mix_rows))
    mix_gathered = lax.all_gather(mix_rows, ("table", "rep"), axis=0, tiled=True)

    partner = group + 1 - 2 * half
    swap = [(i, i + 1 - 2 * (i % SPLIT)) for i in range(groups)]
    grad_pre, self_sums, query_part, query_send, mix_bias_part = owner_backward(
        feature_table,
        hidden,
        all_mixed,
        mix_weight,
        all_codes,
        all_parts,
        all_own_codes,
        all_bounds,
        jnp.stack([group, partner]),
        owners,
        groups,
        batch_rows,
    )
    part = width // groups
    send_first, send_last = table_columns_grad(
        grad_pre, self_sums, neighbour_query_weight, mix_weight, partner.reshape(1), part
    )
    (table_grad,) = table_columns_grad(
        grad_pre, self_sums, neighbour_query_weight, mix_weight, group.reshape(1), part, rows_owned
    )
    mix_bias_grad = jnp.sum(mix_bias_part, axis=0)

    query_rows = width // devices
    query_part = query_part + lax.ppermute(query_send, "rep", swap).astype(F32)
    send_first, mix_gathered = lax.optimization_barrier((send_first, mix_gathered))
    mix_weight_grad = mix_gathered.astype(F32)
    got_first = lax.ppermute(send_first, "rep", swap)
    bias_rows = SUBLANES
    outgoing = jnp.concatenate(
        [
            query_part[:part].reshape(owners, query_rows, width),
            jnp.broadcast_to(query_part[part : part + bias_rows], (owners, bias_rows, width)),
        ],
        axis=1,
    )
    incoming = lax.all_to_all(outgoing.astype(BF16), "table", split_axis=0, concat_axis=0, tiled=True)
    summed = jnp.sum(incoming.astype(F32), axis=0)
    query_bias_grad = summed[query_rows]
    summed, got_first, table_grad = lax.optimization_barrier((summed, got_first, table_grad))
    got_last = lax.ppermute(send_last, "rep", swap)
    table_got = jnp.concatenate([got_first, got_last], axis=1)
    column = lax.all_to_all(
        jnp.broadcast_to(summed[:query_rows].astype(BF16), (groups, query_rows, width)),
        "rep",
        split_axis=0,
        concat_axis=0,
        tiled=True,
    )
    gathered = lax.all_to_all(
        jnp.broadcast_to(column, (owners, groups, query_rows, width)), "table", split_axis=0, concat_axis=0, tiled=True
    )
    query_weight_grad = gathered.transpose(1, 0, 2, 3).reshape(width, width).astype(F32)
    table_grad = lax.dynamic_update_slice(
        table_grad, table_got.astype(F32), ((1 - half) * (rows_owned // SPLIT), 0)
    )
    statistics = sums / (batch_rows * devices)
    return (
        embed,
        table_grad,
        query_weight_grad,
        query_bias_grad,
        mix_weight_grad,
        mix_bias_grad,
        statistics,
    )


def solution(mesh):
    in_specs = (
        P("table", None),
        P(),
        P(),
        P(),
        P(),
        P(("table", "rep"), None),
        P(("table", "rep")),
        P(("table", "rep"), None),
        P(("table", "rep"), None),
    )
    out_specs = (P(("table", "rep"), None), P("table", "rep"), P(), P(), P(), P(), P())
    return jax.shard_map(local, mesh=mesh, in_specs=in_specs, out_specs=out_specs, check_vma=False)
```

```python
import functools

import jax
import jax.numpy as jnp
from jax import lax
from jax.experimental import pallas as pl
from jax.experimental.layout import Layout, with_layout_constraint
from jax.experimental.pallas import tpu as pltpu
from jax.sharding import PartitionSpec as P

F32 = jnp.float32
BF16 = jnp.bfloat16
I32 = jnp.int32
LANES = 128
SUBLANES = 8
ROW_BLOCK = 512
SHIFT = 256
BIAS_ROWS = 16
SPLIT = 2
WINDOW = 1536
UNROLL = 4
VMEM_BYTES = 60 << 20


def row_at(ref, row):
    return ref[pl.ds(pl.multiple_of(row * SUBLANES, SUBLANES), SUBLANES), :]


def put_row(ref, row, value):
    ref[pl.ds(pl.multiple_of(row * SUBLANES, SUBLANES), SUBLANES), :] = value


def clear_rows(ref, rows):
    zero = jnp.zeros((SUBLANES * SUBLANES, LANES), F32)

    def step(i, carry):
        ref[pl.ds(pl.multiple_of(i * SUBLANES * SUBLANES, SUBLANES), SUBLANES * SUBLANES), :] = zero
        return carry

    lax.fori_loop(0, rows // SUBLANES, step, 0)


def walk(first, last, entry):
    count = last - first
    groups = count // UNROLL

    def group(i, carry):
        for u in range(UNROLL):
            entry(first + i * UNROLL + u)
        return carry

    def single(k, carry):
        entry(k)
        return carry

    lax.fori_loop(0, groups, group, 0)
    lax.fori_loop(first + groups * UNROLL, last, single, 0)


def window_start(first, length):
    return pl.multiple_of(jnp.minimum(lax.div(first, LANES) * LANES, length - WINDOW), LANES)


def forward_kernel(blocks, length, bounds, table, query, bias, codes, shares, hidden, pooled, hidden_rows, pooled_rows):
    step = pl.program_id(0)
    width = table.shape[1]
    chunks = width // LANES
    sub = 128

    @pl.when(step < blocks)
    def _():
        def part(j, carry):
            start = pl.multiple_of(j * sub, sub)
            pre = jnp.dot(table[pl.ds(start, sub), :], query[...], preferred_element_type=F32) + bias[...]
            tiny = jnp.finfo(BF16).tiny
            kept = jnp.where(pre > 0, jnp.maximum(pre, tiny), 0.0).astype(BF16)
            hidden[pl.ds(start, sub), :] = kept
            wide = kept.astype(F32)
            base = (step * ROW_BLOCK + start) * SUBLANES
            for g in range(sub // SUBLANES):
                for c in range(chunks):
                    hidden_rows[pl.ds(base + g * SUBLANES * SUBLANES + c, SUBLANES, stride=SUBLANES), :] = wide[
                        g * SUBLANES : (g + 1) * SUBLANES, c * LANES : (c + 1) * LANES
                    ]
            return carry

        lax.fori_loop(0, ROW_BLOCK // sub, part, 0)

    @pl.when(step >= blocks)
    def _():
        device = step - blocks
        targets = pooled.shape[0]
        clear_rows(pooled_rows, targets)

        def entry(k):
            code = codes[0, 0, k]
            node = lax.shift_right_logical(code, 8)
            target = code & (SHIFT - 1)
            put_row(
                pooled_rows,
                target,
                row_at(pooled_rows, target) + shares[0, 0, k] * row_at(hidden_rows, node),
            )

        base = window_start(bounds[device, 0], length)
        walk(bounds[device, 0] - base, bounds[device, 1] - base, entry)

        def part(g, carry):
            for c in range(chunks):
                pooled[
                    pl.ds(pl.multiple_of(g * SUBLANES, SUBLANES), SUBLANES), c * LANES : (c + 1) * LANES
                ] = pooled_rows[pl.ds(g * SUBLANES * SUBLANES + c, SUBLANES, stride=SUBLANES), :]
            return carry

        lax.fori_loop(0, targets // SUBLANES, part, 0)


def owner_forward(table, query, bias, codes, shares, bounds, targets):
    rows, width = table.shape
    blocks = rows // ROW_BLOCK
    devices, _, length = codes.shape

    def list_block(i, bounds):
        k = jnp.maximum(i - blocks, 0)
        return (k, 0, window_start(bounds[k, 0], length))

    window = (pl.Element(1), pl.Element(1), pl.Element(WINDOW))
    return pl.pallas_call(
        functools.partial(forward_kernel, blocks, length),
        grid_spec=pltpu.PrefetchScalarGridSpec(
            num_scalar_prefetch=1,
            grid=(blocks + devices,),
            in_specs=[
                pl.BlockSpec((ROW_BLOCK, width), lambda i, b: (jnp.minimum(i, blocks - 1), 0)),
                pl.BlockSpec((width, width), lambda i, b: (0, 0)),
                pl.BlockSpec((1, width), lambda i, b: (0, 0)),
                pl.BlockSpec(window, list_block, memory_space=pltpu.SMEM),
                pl.BlockSpec(window, list_block, memory_space=pltpu.SMEM),
            ],
            out_specs=[
                pl.BlockSpec((ROW_BLOCK, width), lambda i, b: (jnp.minimum(i, blocks - 1), 0)),
                pl.BlockSpec((targets, width), lambda i, b: (jnp.maximum(i - blocks, 0), 0)),
            ],
            scratch_shapes=[
                pltpu.VMEM((rows * SUBLANES, LANES), F32),
                pltpu.VMEM((targets * SUBLANES, LANES), F32),
            ],
        ),
        out_shape=[
            jax.ShapeDtypeStruct((rows, width), BF16),
            jax.ShapeDtypeStruct((devices * targets, width), F32),
        ],
        compiler_params=pltpu.CompilerParams(vmem_limit_bytes=VMEM_BYTES),
        cost_estimate=pl.CostEstimate(
            flops=2 * rows * width * width, bytes_accessed=4 * rows * width, transcendentals=0
        ),
        name="owner_forward",
    )(bounds, table, query, bias.reshape(1, width), codes, shares)


def spread_rows(source, rows_here):
    targets, width = source.shape
    chunks = width // LANES
    tile = SUBLANES * SUBLANES

    def part(g, sums):
        both = source[pl.ds(pl.multiple_of(g * 16, 16), 16), :].astype(F32)
        for h in range(2):
            for c in range(chunks):
                rows_here[pl.ds((g * 2 + h) * tile + c, SUBLANES, stride=SUBLANES), :] = both[
                    h * SUBLANES : (h + 1) * SUBLANES, c * LANES : (c + 1) * LANES
                ]
        return sums + both[:SUBLANES] + both[SUBLANES:]

    return lax.fori_loop(0, targets // 16, part, jnp.zeros((SUBLANES, width), F32))


def backward_kernel(
    requesters,
    length,
    place,
    bounds,
    codes,
    shares,
    self_codes,
    grads,
    hidden,
    table_own,
    table_other,
    mix_pooled,
    grad_pre,
    self_sums,
    weight_grad,
    weight_send,
    mix_bias_grad,
    near_total,
    self_total,
    rows_here,
    near_sums,
    weight_sum,
    bias_sum,
):
    step = pl.program_id(0)
    block, width = hidden.shape
    rows = near_total.shape[0] // SUBLANES
    part_rows = weight_sum.shape[0]
    chunks = width // LANES
    tile = SUBLANES * SUBLANES

    @pl.when(step == 0)
    def _():
        clear_rows(near_total, rows)
        clear_rows(self_total, rows)
        mix_bias_grad[...] = jnp.zeros_like(mix_bias_grad)
        bias_sum[...] = jnp.zeros_like(bias_sum)
        weight_grad[...] = jnp.zeros_like(weight_grad)
        weight_sum[...] = jnp.zeros_like(weight_sum)

    @pl.when(step < requesters)
    def _():
        mix_bias_grad[...] += spread_rows(grads, rows_here)
        first_row = lax.rem(place[0], SPLIT) * rows

        def parts_of(code):
            return lax.shift_right_logical(code, 8) - first_row, code & (SHIFT - 1)

        base = window_start(bounds[step, 0], length)

        def entry(k):
            node, target = parts_of(codes[0, 0, k])
            put_row(near_total, node, row_at(near_total, node) + shares[0, 0, k] * row_at(rows_here, target))

        walk(bounds[step, 0] - base, bounds[step, 1] - base, entry)

        def self_entry(k):
            node, target = parts_of(self_codes[0, 0, k])
            put_row(self_total, node, row_at(self_total, node) + row_at(rows_here, target))

        walk(bounds[step, 2], bounds[step, 3], self_entry)

    @pl.when(step >= requesters)
    def _():
        base = (step - requesters) * (block // SUBLANES)

        def part(g, carry):
            where = pl.ds(pl.multiple_of(g * 16, 16), 16)
            for total, sums in ((near_total, near_sums), (self_total, self_sums)):
                for c in range(chunks):
                    halves = [
                        total[pl.ds((base + g * 2 + h) * tile + c, SUBLANES, stride=SUBLANES), :] for h in range(2)
                    ]
                    sums[where, c * LANES : (c + 1) * LANES] = jnp.concatenate(halves, axis=0).astype(BF16)
            return carry

        lax.fori_loop(0, block // 16, part, 0)
        turned = (((1,), (1,)), ((), ()))
        raw = lax.dot_general(near_sums[...], mix_pooled[...], turned, preferred_element_type=F32)
        wide = jnp.where(hidden[...].astype(F32) > 0, raw, 0.0)
        bias_sum[...] += jnp.sum(wide.reshape(block // SUBLANES, SUBLANES, width), axis=0)
        kept = wide.astype(BF16)
        grad_pre[...] = kept
        down = (((0,), (0,)), ((), ()))
        weight_grad[:part_rows] += lax.dot_general(table_own[...], kept, down, preferred_element_type=F32)
        weight_sum[...] += lax.dot_general(table_other[...], kept, down, preferred_element_type=F32)

    @pl.when(step == pl.num_programs(0) - 1)
    def _():
        bias = jnp.broadcast_to(jnp.sum(bias_sum[...], axis=0, keepdims=True), (BIAS_ROWS, width))
        weight_grad[part_rows:] = bias
        weight_send[:part_rows] = weight_sum[...].astype(BF16)
        weight_send[part_rows:] = bias.astype(BF16)


def owner_backward(table, hidden, grads, mix, codes, shares, self_codes, bounds, place, owners, groups, targets):
    rows_owned, width = table.shape
    rows = rows_owned // SPLIT
    blocks = rows // ROW_BLOCK
    requesters, _, length = codes.shape
    self_length = self_codes.shape[2]
    part = width // groups

    def requester(i):
        return jnp.minimum(i, requesters - 1)

    def node_row(i, place):
        return lax.rem(place[0], SPLIT) * blocks + jnp.maximum(i - requesters, 0)

    def list_block(i, place, bounds):
        k = requester(i)
        return (k, 0, window_start(bounds[k, 0], length))

    def grad_block(i, place, bounds):
        k = requester(i)
        return (lax.rem(k, owners) * groups + lax.div(k, owners), 0)

    def table_columns(which):
        return pl.BlockSpec((ROW_BLOCK, part), lambda i, place, bounds: (node_row(i, place), place[which]))

    def fixed(shape):
        return pl.BlockSpec(shape, lambda i, place, bounds: (0, 0))

    window = (pl.Element(1), pl.Element(1), pl.Element(WINDOW))
    return pl.pallas_call(
        functools.partial(backward_kernel, requesters, length),
        grid_spec=pltpu.PrefetchScalarGridSpec(
            num_scalar_prefetch=2,
            grid=(requesters + blocks,),
            in_specs=[
                pl.BlockSpec(window, list_block, memory_space=pltpu.SMEM),
                pl.BlockSpec(window, list_block, memory_space=pltpu.SMEM),
                pl.BlockSpec(
                    (1, 1, self_length), lambda i, place, bounds: (requester(i), 0, 0), memory_space=pltpu.SMEM
                ),
                pl.BlockSpec((targets, width), grad_block),
                pl.BlockSpec((ROW_BLOCK, width), lambda i, place, bounds: (node_row(i, place), 0)),
                table_columns(0),
                table_columns(1),
                pl.BlockSpec((width, width), lambda i, place, bounds: (1, 0), pipeline_mode=pl.Buffered(1)),
            ],
            out_specs=[
                pl.BlockSpec((ROW_BLOCK, width), lambda i, place, bounds: (jnp.maximum(i - requesters, 0), 0)),
                pl.BlockSpec((ROW_BLOCK, width), lambda i, place, bounds: (jnp.maximum(i - requesters, 0), 0)),
                fixed((part + BIAS_ROWS, width)),
                fixed((part + BIAS_ROWS, width)),
                fixed((SUBLANES, width)),
            ],
            scratch_shapes=[
                pltpu.VMEM((rows * SUBLANES, LANES), F32),
                pltpu.VMEM((rows * SUBLANES, LANES), F32),
                pltpu.VMEM((targets * SUBLANES, LANES), F32),
                pltpu.VMEM((ROW_BLOCK, width), BF16),
                pltpu.VMEM((part, width), F32),
                pltpu.VMEM((SUBLANES, width), F32),
            ],
        ),
        out_shape=[
            jax.ShapeDtypeStruct((rows, width), BF16),
            jax.ShapeDtypeStruct((rows, width), BF16),
            jax.ShapeDtypeStruct((part + BIAS_ROWS, width), F32),
            jax.ShapeDtypeStruct((part + BIAS_ROWS, width), BF16),
            jax.ShapeDtypeStruct((SUBLANES, width), F32),
        ],
        compiler_params=pltpu.CompilerParams(vmem_limit_bytes=VMEM_BYTES),
        cost_estimate=pl.CostEstimate(
            flops=8 * rows * width * width, bytes_accessed=4 * requesters * targets * width, transcendentals=0
        ),
        name="owner_backward",
    )(
        place,
        bounds,
        codes,
        shares,
        self_codes,
        grads,
        hidden,
        table,
        table,
        mix,
    )


def table_kernel(place, grad_pre, self_sums, query, mix_self, *outs):
    turned = (((1,), (1,)), ((), ()))
    grad = lax.dot_general(grad_pre[...], query[...], turned, preferred_element_type=F32) + lax.dot_general(
        self_sums[...], mix_self[...], turned, preferred_element_type=F32
    )
    at = 0
    for out in outs:
        out[...] = grad[:, at : at + out.shape[1]].astype(out.dtype)
        at += out.shape[1]


def table_columns_grad(grad_pre, self_sums, query, mix, place, part, kept_rows=None):
    rows, width = grad_pre.shape
    blocks = rows // ROW_BLOCK

    def node_block(i, place):
        return (i, 0)

    weights = pl.BlockSpec((part, width), lambda i, place: (place[0], 0), pipeline_mode=pl.Buffered(1))
    if kept_rows is None:
        out_specs = [pl.BlockSpec((ROW_BLOCK, part // 2), node_block)] * 2
        out_shape = [jax.ShapeDtypeStruct((rows, part // 2), BF16)] * 2
    else:
        out_specs = [pl.BlockSpec((ROW_BLOCK, part), lambda i, place: (lax.rem(place[0], SPLIT) * blocks + i, 0))]
        out_shape = [jax.ShapeDtypeStruct((kept_rows, part), F32)]
    return pl.pallas_call(
        table_kernel,
        grid_spec=pltpu.PrefetchScalarGridSpec(
            num_scalar_prefetch=1,
            grid=(blocks,),
            in_specs=[pl.BlockSpec((ROW_BLOCK, width), node_block)] * 2 + [weights] * 2,
            out_specs=out_specs,
        ),
        out_shape=out_shape,
        compiler_params=pltpu.CompilerParams(vmem_limit_bytes=VMEM_BYTES),
        cost_estimate=pl.CostEstimate(
            flops=4 * rows * width * part, bytes_accessed=4 * rows * width, transcendentals=0
        ),
        name="table_columns_grad",
    )(place, grad_pre, self_sums, query, mix)


def padded(values, length):
    return jnp.pad(values, (0, length - values.shape[0]))


def local(
    feature_table,
    neighbour_query_weight,
    query_bias,
    mix_weight,
    mix_bias,
    lookup_ids,
    present_counts,
    importance,
    embed_cot,
):
    owners = lax.axis_size("table")
    groups = lax.axis_size("rep")
    devices = owners * groups
    rows_owned, width = feature_table.shape
    batch_rows, slot_count = lookup_ids.shape
    near = slot_count - 1
    owner = lax.axis_index("table").astype(I32)
    group = lax.axis_index("rep").astype(I32)

    present = (jnp.arange(near, dtype=I32)[None, :] < present_counts[:, None]).astype(F32)
    masked_weight = importance * present
    shares = lax.reduce_precision(masked_weight / jnp.sum(masked_weight, axis=1, keepdims=True), 8, 7)
    live_most = batch_rows // 2 * (near + 5)
    length = -(-live_most // LANES) * LANES
    target = jnp.arange(batch_rows, dtype=I32)
    keys = jnp.where(present > 0, lookup_ids[:, 1:] * SHIFT + target[:, None], jnp.iinfo(I32).max)
    keys, sorted_shares = lax.sort((keys.reshape(-1), shares.reshape(-1)), num_keys=1, is_stable=False)
    keys = keys[:live_most]
    sorted_shares = sorted_shares[:live_most]
    edges = jnp.arange(owners * SPLIT + 1, dtype=I32) * (rows_owned // SPLIT * SHIFT)
    starts = jnp.sum((keys[None, :] < edges[:, None]).astype(I32), axis=1)
    own_length = SHIFT
    meta = jnp.concatenate(
        [
            starts.astype(F32),
            jnp.stack([jnp.sum(present), jnp.sum(masked_weight)]),
        ]
    )
    meta_length = -(-meta.shape[0] // LANES) * LANES

    def as_code(key):
        return (key % (rows_owned * SHIFT)).astype(F32)

    request = jnp.concatenate(
        [
            padded(as_code(keys), length),
            padded(sorted_shares, length),
            padded(meta, meta_length),
            padded(lookup_ids[:, 0].astype(F32), own_length),
        ]
    )
    plane = lax.all_gather(request, "table", axis=0)

    own_ids = plane[:, -own_length:][:, :batch_rows].astype(I32).reshape(-1)
    wanted = own_ids - owner * rows_owned
    mine = (wanted >= 0) & (wanted < rows_owned)
    found = feature_table[jnp.clip(wanted, 0, rows_owned - 1)]
    found = jnp.where(mine[:, None], found, jnp.zeros((), BF16))
    self_rows = lax.psum_scatter(found, "table", scatter_dimension=0, tiled=True)
    every = lax.all_gather(plane, "rep", axis=0).reshape(devices, -1)

    def unpack(lists, start, stride):
        count = lists.shape[0]
        at = 2 * length
        codes = lists[:, :length].astype(I32).reshape(count, 1, length)
        parts = lists[:, length:at].reshape(count, 1, length)
        notes = lists[:, at : at + meta_length]
        bounds = lax.dynamic_slice(notes, (0, start), (count, stride + 1))[:, ::stride].astype(I32)
        sums = jnp.sum(notes[:, owners * SPLIT + 1 : owners * SPLIT + 3], axis=0)
        return codes, parts, bounds, sums

    def own_lists(lists, start):
        ids = lists[:, -own_length:][:, :batch_rows].astype(I32)
        keys = lax.sort(ids * SHIFT + target[None, :], dimension=1)
        ends = (start + jnp.arange(2, dtype=I32)) * (rows_owned // SPLIT * SHIFT)
        own_bounds = jnp.sum((keys[:, None, :] < ends[None, :, None]).astype(I32), axis=2)
        own_codes = jnp.pad(keys % (rows_owned * SHIFT), ((0, 0), (0, own_length - batch_rows)))
        return own_codes.reshape(-1, 1, own_length), own_bounds

    codes, parts, bounds, _ = unpack(plane, owner * SPLIT, SPLIT)
    bounds, _ = lax.optimization_barrier((bounds, found))
    hidden, pooled_parts = owner_forward(
        feature_table, neighbour_query_weight, query_bias, codes, parts, bounds, batch_rows
    )
    pooled_parts, self_rows = lax.optimization_barrier((pooled_parts, self_rows))
    pooled = lax.psum_scatter(pooled_parts, "table", scatter_dimension=0, tiled=True)
    half = lax.rem(group, SPLIT)
    all_codes, all_parts, all_bounds, sums = unpack(every, owner * SPLIT + half, 1)
    all_own_codes, own_bounds = own_lists(every, owner * SPLIT + half)
    all_bounds = jnp.concatenate([all_bounds, own_bounds], axis=1)
    rows_major = Layout(major_to_minor=(0, 1, 2))
    all_codes = with_layout_constraint(all_codes, rows_major)
    all_parts = with_layout_constraint(all_parts, rows_major)
    pooled, lists = lax.optimization_barrier((pooled, (all_codes, all_parts, all_own_codes, all_bounds, sums)))
    all_codes, all_parts, all_own_codes, all_bounds, sums = lists
    pooled = lax.reduce_precision(pooled, 8, 7).astype(BF16)

    joined = jnp.concatenate([self_rows, pooled], axis=1)
    mixed = jnp.dot(joined, mix_weight, preferred_element_type=F32) + mix_bias
    activation = jax.nn.relu(mixed)
    inverse = lax.rsqrt(jnp.mean(activation * activation, axis=1, keepdims=True) + 1e-06)
    embed = (activation * inverse).astype(BF16)
    cotangent = embed_cot.astype(F32)
    grad_act = inverse * cotangent - activation * (inverse * inverse * inverse) * jnp.mean(
        activation * cotangent, axis=1, keepdims=True
    )
    grad_mixed = jnp.where(mixed > 0, grad_act, 0.0).astype(BF16)
    all_mixed = lax.all_gather(grad_mixed, ("table", "rep"), axis=0, tiled=True)
    mix_part = 2 * width // devices
    columns = lax.all_to_all(
        joined.reshape(batch_rows, devices, mix_part).transpose(1, 0, 2),
        ("table", "rep"),
        split_axis=0,
        concat_axis=0,
        tiled=True,
    ).reshape(devices * batch_rows, mix_part)

    mix_rows = lax.dot_general(
        columns, all_mixed, (((0,), (0,)), ((), ())), preferred_element_type=F32
    ).astype(BF16)
    all_mixed, mix_rows = lax.optimization_barrier((all_mixed, mix_rows))
    mix_gathered = lax.all_gather(mix_rows, ("table", "rep"), axis=0, tiled=True)

    partner = group + 1 - 2 * half
    swap = [(i, i + 1 - 2 * (i % SPLIT)) for i in range(groups)]
    grad_pre, self_sums, query_part, query_send, mix_bias_part = owner_backward(
        feature_table,
        hidden,
        all_mixed,
        mix_weight,
        all_codes,
        all_parts,
        all_own_codes,
        all_bounds,
        jnp.stack([group, partner]),
        owners,
        groups,
        batch_rows,
    )
    part = width // groups
    send_first, send_last = table_columns_grad(
        grad_pre, self_sums, neighbour_query_weight, mix_weight, partner.reshape(1), part
    )
    (table_grad,) = table_columns_grad(
        grad_pre, self_sums, neighbour_query_weight, mix_weight, group.reshape(1), part, rows_owned
    )
    mix_bias_grad = jnp.sum(mix_bias_part, axis=0)

    query_rows = width // devices
    query_part = query_part + lax.ppermute(query_send, "rep", swap).astype(F32)
    send_first, mix_gathered = lax.optimization_barrier((send_first, mix_gathered))
    mix_weight_grad = mix_gathered.astype(F32)
    got_first = lax.ppermute(send_first, "rep", swap)
    bias_rows = SUBLANES
    outgoing = jnp.concatenate(
        [
            query_part[:part].reshape(owners, query_rows, width),
            jnp.broadcast_to(query_part[part : part + bias_rows], (owners, bias_rows, width)),
        ],
        axis=1,
    )
    incoming = lax.all_to_all(outgoing.astype(BF16), "table", split_axis=0, concat_axis=0, tiled=True)
    summed = jnp.sum(incoming.astype(F32), axis=0)
    query_bias_grad = summed[query_rows]
    column = lax.all_to_all(
        jnp.broadcast_to(summed[:query_rows].astype(BF16), (groups, query_rows, width)),
        "rep",
        split_axis=0,
        concat_axis=0,
        tiled=True,
    )
    column, got_first = lax.optimization_barrier((column, got_first))
    got_last = lax.ppermute(send_last, "rep", swap)
    table_got = jnp.concatenate([got_first, got_last], axis=1)
    gathered = lax.all_to_all(
        jnp.broadcast_to(column, (owners, groups, query_rows, width)), "table", split_axis=0, concat_axis=0, tiled=True
    )
    query_weight_grad = gathered.transpose(1, 0, 2, 3).reshape(width, width).astype(F32)
    table_grad = lax.dynamic_update_slice(
        table_grad, table_got.astype(F32), ((1 - half) * (rows_owned // SPLIT), 0)
    )
    statistics = sums / (batch_rows * devices)
    return (
        embed,
        table_grad,
        query_weight_grad,
        query_bias_grad,
        mix_weight_grad,
        mix_bias_grad,
        statistics,
    )


def solution(mesh):
    in_specs = (
        P("table", None),
        P(),
        P(),
        P(),
        P(),
        P(("table", "rep"), None),
        P(("table", "rep")),
        P(("table", "rep"), None),
        P(("table", "rep"), None),
    )
    out_specs = (P(("table", "rep"), None), P("table", "rep"), P(), P(), P(), P(), P())
    return jax.shard_map(local, mesh=mesh, in_specs=in_specs, out_specs=out_specs, check_vma=False)
```

```python
import functools

import jax
import jax.numpy as jnp
from jax import lax
from jax.experimental import pallas as pl
from jax.experimental.layout import Layout, with_layout_constraint
from jax.experimental.pallas import tpu as pltpu
from jax.sharding import PartitionSpec as P

F32 = jnp.float32
BF16 = jnp.bfloat16
I32 = jnp.int32
LANES = 128
SUBLANES = 8
ROW_BLOCK = 512
SHIFT = 256
BIAS_ROWS = 16
SPLIT = 2
WINDOW = 1536
UNROLL = 4
VMEM_BYTES = 60 << 20


def row_at(ref, row):
    return ref[pl.ds(pl.multiple_of(row * SUBLANES, SUBLANES), SUBLANES), :]


def put_row(ref, row, value):
    ref[pl.ds(pl.multiple_of(row * SUBLANES, SUBLANES), SUBLANES), :] = value


def clear_rows(ref, rows):
    zero = jnp.zeros((SUBLANES * SUBLANES, LANES), F32)

    def step(i, carry):
        ref[pl.ds(pl.multiple_of(i * SUBLANES * SUBLANES, SUBLANES), SUBLANES * SUBLANES), :] = zero
        return carry

    lax.fori_loop(0, rows // SUBLANES, step, 0)


def walk(first, last, entry):
    count = last - first
    groups = count // UNROLL

    def group(i, carry):
        for u in range(UNROLL):
            entry(first + i * UNROLL + u)
        return carry

    def single(k, carry):
        entry(k)
        return carry

    lax.fori_loop(0, groups, group, 0)
    lax.fori_loop(first + groups * UNROLL, last, single, 0)


def window_start(first, length):
    return pl.multiple_of(jnp.minimum(lax.div(first, LANES) * LANES, length - WINDOW), LANES)


def forward_kernel(blocks, length, bounds, table, query, bias, codes, shares, hidden, pooled, hidden_rows, pooled_rows):
    step = pl.program_id(0)
    width = table.shape[1]
    chunks = width // LANES
    sub = 128

    @pl.when(step < blocks)
    def _():
        def part(j, carry):
            start = pl.multiple_of(j * sub, sub)
            pre = jnp.dot(table[pl.ds(start, sub), :], query[...], preferred_element_type=F32) + bias[...]
            tiny = jnp.finfo(BF16).tiny
            kept = jnp.where(pre > 0, jnp.maximum(pre, tiny), 0.0).astype(BF16)
            hidden[pl.ds(start, sub), :] = kept
            wide = kept.astype(F32)
            base = (step * ROW_BLOCK + start) * SUBLANES
            for g in range(sub // SUBLANES):
                for c in range(chunks):
                    hidden_rows[pl.ds(base + g * SUBLANES * SUBLANES + c, SUBLANES, stride=SUBLANES), :] = wide[
                        g * SUBLANES : (g + 1) * SUBLANES, c * LANES : (c + 1) * LANES
                    ]
            return carry

        lax.fori_loop(0, ROW_BLOCK // sub, part, 0)

    @pl.when(step >= blocks)
    def _():
        device = step - blocks
        targets = pooled.shape[0]
        clear_rows(pooled_rows, targets)

        def entry(k):
            code = codes[0, 0, k]
            node = lax.shift_right_logical(code, 8)
            target = code & (SHIFT - 1)
            put_row(
                pooled_rows,
                target,
                row_at(pooled_rows, target) + shares[0, 0, k] * row_at(hidden_rows, node),
            )

        base = window_start(bounds[device, 0], length)
        walk(bounds[device, 0] - base, bounds[device, 1] - base, entry)

        def part(g, carry):
            for c in range(chunks):
                pooled[
                    pl.ds(pl.multiple_of(g * SUBLANES, SUBLANES), SUBLANES), c * LANES : (c + 1) * LANES
                ] = pooled_rows[pl.ds(g * SUBLANES * SUBLANES + c, SUBLANES, stride=SUBLANES), :]
            return carry

        lax.fori_loop(0, targets // SUBLANES, part, 0)


def owner_forward(table, query, bias, codes, shares, bounds, targets):
    rows, width = table.shape
    blocks = rows // ROW_BLOCK
    devices, _, length = codes.shape

    def list_block(i, bounds):
        k = jnp.maximum(i - blocks, 0)
        return (k, 0, window_start(bounds[k, 0], length))

    window = (pl.Element(1), pl.Element(1), pl.Element(WINDOW))
    return pl.pallas_call(
        functools.partial(forward_kernel, blocks, length),
        grid_spec=pltpu.PrefetchScalarGridSpec(
            num_scalar_prefetch=1,
            grid=(blocks + devices,),
            in_specs=[
                pl.BlockSpec((ROW_BLOCK, width), lambda i, b: (jnp.minimum(i, blocks - 1), 0)),
                pl.BlockSpec((width, width), lambda i, b: (0, 0)),
                pl.BlockSpec((1, width), lambda i, b: (0, 0)),
                pl.BlockSpec(window, list_block, memory_space=pltpu.SMEM),
                pl.BlockSpec(window, list_block, memory_space=pltpu.SMEM),
            ],
            out_specs=[
                pl.BlockSpec((ROW_BLOCK, width), lambda i, b: (jnp.minimum(i, blocks - 1), 0)),
                pl.BlockSpec((targets, width), lambda i, b: (jnp.maximum(i - blocks, 0), 0)),
            ],
            scratch_shapes=[
                pltpu.VMEM((rows * SUBLANES, LANES), F32),
                pltpu.VMEM((targets * SUBLANES, LANES), F32),
            ],
        ),
        out_shape=[
            jax.ShapeDtypeStruct((rows, width), BF16),
            jax.ShapeDtypeStruct((devices * targets, width), F32),
        ],
        compiler_params=pltpu.CompilerParams(vmem_limit_bytes=VMEM_BYTES),
        cost_estimate=pl.CostEstimate(
            flops=2 * rows * width * width, bytes_accessed=4 * rows * width, transcendentals=0
        ),
        name="owner_forward",
    )(bounds, table, query, bias.reshape(1, width), codes, shares)


def spread_rows(source, rows_here):
    targets, width = source.shape
    chunks = width // LANES
    tile = SUBLANES * SUBLANES

    def part(g, sums):
        both = source[pl.ds(pl.multiple_of(g * 16, 16), 16), :].astype(F32)
        for h in range(2):
            for c in range(chunks):
                rows_here[pl.ds((g * 2 + h) * tile + c, SUBLANES, stride=SUBLANES), :] = both[
                    h * SUBLANES : (h + 1) * SUBLANES, c * LANES : (c + 1) * LANES
                ]
        return sums + both[:SUBLANES] + both[SUBLANES:]

    return lax.fori_loop(0, targets // 16, part, jnp.zeros((SUBLANES, width), F32))


def backward_kernel(
    requesters,
    length,
    place,
    bounds,
    codes,
    shares,
    self_codes,
    grads,
    hidden,
    table_own,
    table_other,
    mix_pooled,
    grad_pre,
    self_sums,
    weight_grad,
    weight_send,
    mix_bias_grad,
    near_total,
    self_total,
    rows_here,
    near_sums,
    weight_sum,
    bias_sum,
):
    step = pl.program_id(0)
    block, width = hidden.shape
    rows = near_total.shape[0] // SUBLANES
    part_rows = weight_sum.shape[0]
    chunks = width // LANES
    tile = SUBLANES * SUBLANES

    @pl.when(step == 0)
    def _():
        clear_rows(near_total, rows)
        clear_rows(self_total, rows)
        mix_bias_grad[...] = jnp.zeros_like(mix_bias_grad)
        bias_sum[...] = jnp.zeros_like(bias_sum)
        weight_grad[...] = jnp.zeros_like(weight_grad)
        weight_sum[...] = jnp.zeros_like(weight_sum)

    @pl.when(step < requesters)
    def _():
        mix_bias_grad[...] += spread_rows(grads, rows_here)
        first_row = lax.rem(place[0], SPLIT) * rows

        def parts_of(code):
            return lax.shift_right_logical(code, 8) - first_row, code & (SHIFT - 1)

        base = window_start(bounds[step, 0], length)

        def entry(k):
            node, target = parts_of(codes[0, 0, k])
            put_row(near_total, node, row_at(near_total, node) + shares[0, 0, k] * row_at(rows_here, target))

        walk(bounds[step, 0] - base, bounds[step, 1] - base, entry)

        def self_entry(k):
            node, target = parts_of(self_codes[0, 0, k])
            put_row(self_total, node, row_at(self_total, node) + row_at(rows_here, target))

        walk(bounds[step, 2], bounds[step, 3], self_entry)

    @pl.when(step >= requesters)
    def _():
        base = (step - requesters) * (block // SUBLANES)

        def part(g, carry):
            where = pl.ds(pl.multiple_of(g * 16, 16), 16)
            for total, sums in ((near_total, near_sums), (self_total, self_sums)):
                for c in range(chunks):
                    halves = [
                        total[pl.ds((base + g * 2 + h) * tile + c, SUBLANES, stride=SUBLANES), :] for h in range(2)
                    ]
                    sums[where, c * LANES : (c + 1) * LANES] = jnp.concatenate(halves, axis=0).astype(BF16)
            return carry

        lax.fori_loop(0, block // 16, part, 0)
        turned = (((1,), (1,)), ((), ()))
        raw = lax.dot_general(near_sums[...], mix_pooled[...], turned, preferred_element_type=F32)
        wide = jnp.where(hidden[...].astype(F32) > 0, raw, 0.0)
        bias_sum[...] += jnp.sum(wide.reshape(block // SUBLANES, SUBLANES, width), axis=0)
        kept = wide.astype(BF16)
        grad_pre[...] = kept
        down = (((0,), (0,)), ((), ()))
        weight_grad[:part_rows] += lax.dot_general(table_own[...], kept, down, preferred_element_type=F32)
        weight_sum[...] += lax.dot_general(table_other[...], kept, down, preferred_element_type=F32)

    @pl.when(step == pl.num_programs(0) - 1)
    def _():
        bias = jnp.broadcast_to(jnp.sum(bias_sum[...], axis=0, keepdims=True), (BIAS_ROWS, width))
        weight_grad[part_rows:] = bias
        weight_send[:part_rows] = weight_sum[...].astype(BF16)
        weight_send[part_rows:] = bias.astype(BF16)


def owner_backward(table, hidden, grads, mix, codes, shares, self_codes, bounds, place, owners, groups, targets):
    rows_owned, width = table.shape
    rows = rows_owned // SPLIT
    blocks = rows // ROW_BLOCK
    requesters, _, length = codes.shape
    self_length = self_codes.shape[2]
    part = width // groups

    def requester(i):
        return jnp.minimum(i, requesters - 1)

    def node_row(i, place):
        return lax.rem(place[0], SPLIT) * blocks + jnp.maximum(i - requesters, 0)

    def list_block(i, place, bounds):
        k = requester(i)
        return (k, 0, window_start(bounds[k, 0], length))

    def grad_block(i, place, bounds):
        k = requester(i)
        return (lax.rem(k, owners) * groups + lax.div(k, owners), 0)

    def table_columns(which):
        return pl.BlockSpec((ROW_BLOCK, part), lambda i, place, bounds: (node_row(i, place), place[which]))

    def fixed(shape):
        return pl.BlockSpec(shape, lambda i, place, bounds: (0, 0))

    window = (pl.Element(1), pl.Element(1), pl.Element(WINDOW))
    return pl.pallas_call(
        functools.partial(backward_kernel, requesters, length),
        grid_spec=pltpu.PrefetchScalarGridSpec(
            num_scalar_prefetch=2,
            grid=(requesters + blocks,),
            in_specs=[
                pl.BlockSpec(window, list_block, memory_space=pltpu.SMEM),
                pl.BlockSpec(window, list_block, memory_space=pltpu.SMEM),
                pl.BlockSpec(
                    (1, 1, self_length), lambda i, place, bounds: (requester(i), 0, 0), memory_space=pltpu.SMEM
                ),
                pl.BlockSpec((targets, width), grad_block),
                pl.BlockSpec((ROW_BLOCK, width), lambda i, place, bounds: (node_row(i, place), 0)),
                table_columns(0),
                table_columns(1),
                pl.BlockSpec((width, width), lambda i, place, bounds: (1, 0), pipeline_mode=pl.Buffered(1)),
            ],
            out_specs=[
                pl.BlockSpec((ROW_BLOCK, width), lambda i, place, bounds: (jnp.maximum(i - requesters, 0), 0)),
                pl.BlockSpec((ROW_BLOCK, width), lambda i, place, bounds: (jnp.maximum(i - requesters, 0), 0)),
                fixed((part + BIAS_ROWS, width)),
                fixed((part + BIAS_ROWS, width)),
                fixed((SUBLANES, width)),
            ],
            scratch_shapes=[
                pltpu.VMEM((rows * SUBLANES, LANES), F32),
                pltpu.VMEM((rows * SUBLANES, LANES), F32),
                pltpu.VMEM((targets * SUBLANES, LANES), F32),
                pltpu.VMEM((ROW_BLOCK, width), BF16),
                pltpu.VMEM((part, width), F32),
                pltpu.VMEM((SUBLANES, width), F32),
            ],
        ),
        out_shape=[
            jax.ShapeDtypeStruct((rows, width), BF16),
            jax.ShapeDtypeStruct((rows, width), BF16),
            jax.ShapeDtypeStruct((part + BIAS_ROWS, width), F32),
            jax.ShapeDtypeStruct((part + BIAS_ROWS, width), BF16),
            jax.ShapeDtypeStruct((SUBLANES, width), F32),
        ],
        compiler_params=pltpu.CompilerParams(vmem_limit_bytes=VMEM_BYTES),
        cost_estimate=pl.CostEstimate(
            flops=8 * rows * width * width, bytes_accessed=4 * requesters * targets * width, transcendentals=0
        ),
        name="owner_backward",
    )(
        place,
        bounds,
        codes,
        shares,
        self_codes,
        grads,
        hidden,
        table,
        table,
        mix,
    )


def table_kernel(place, grad_pre, self_sums, query, mix_self, *outs):
    turned = (((1,), (1,)), ((), ()))
    grad = lax.dot_general(grad_pre[...], query[...], turned, preferred_element_type=F32) + lax.dot_general(
        self_sums[...], mix_self[...], turned, preferred_element_type=F32
    )
    at = 0
    for out in outs:
        out[...] = grad[:, at : at + out.shape[1]].astype(out.dtype)
        at += out.shape[1]


def table_columns_grad(grad_pre, self_sums, query, mix, place, part, kept_rows=None):
    rows, width = grad_pre.shape
    blocks = rows // ROW_BLOCK

    def node_block(i, place):
        return (i, 0)

    weights = pl.BlockSpec((part, width), lambda i, place: (place[0], 0), pipeline_mode=pl.Buffered(1))
    if kept_rows is None:
        out_specs = [pl.BlockSpec((ROW_BLOCK, part // 2), node_block)] * 2
        out_shape = [jax.ShapeDtypeStruct((rows, part // 2), BF16)] * 2
    else:
        out_specs = [pl.BlockSpec((ROW_BLOCK, part), lambda i, place: (lax.rem(place[0], SPLIT) * blocks + i, 0))]
        out_shape = [jax.ShapeDtypeStruct((kept_rows, part), F32)]
    return pl.pallas_call(
        table_kernel,
        grid_spec=pltpu.PrefetchScalarGridSpec(
            num_scalar_prefetch=1,
            grid=(blocks,),
            in_specs=[pl.BlockSpec((ROW_BLOCK, width), node_block)] * 2 + [weights] * 2,
            out_specs=out_specs,
        ),
        out_shape=out_shape,
        compiler_params=pltpu.CompilerParams(vmem_limit_bytes=VMEM_BYTES),
        cost_estimate=pl.CostEstimate(
            flops=4 * rows * width * part, bytes_accessed=4 * rows * width, transcendentals=0
        ),
        name="table_columns_grad",
    )(place, grad_pre, self_sums, query, mix)


def padded(values, length):
    return jnp.pad(values, (0, length - values.shape[0]))


def local(
    feature_table,
    neighbour_query_weight,
    query_bias,
    mix_weight,
    mix_bias,
    lookup_ids,
    present_counts,
    importance,
    embed_cot,
):
    owners = lax.axis_size("table")
    groups = lax.axis_size("rep")
    devices = owners * groups
    rows_owned, width = feature_table.shape
    batch_rows, slot_count = lookup_ids.shape
    near = slot_count - 1
    owner = lax.axis_index("table").astype(I32)
    group = lax.axis_index("rep").astype(I32)

    present = (jnp.arange(near, dtype=I32)[None, :] < present_counts[:, None]).astype(F32)
    masked_weight = importance * present
    shares = lax.reduce_precision(masked_weight / jnp.sum(masked_weight, axis=1, keepdims=True), 8, 7)
    live_most = batch_rows // 2 * (near + 5)
    length = -(-live_most // LANES) * LANES
    target = jnp.arange(batch_rows, dtype=I32)
    keys = jnp.where(present > 0, lookup_ids[:, 1:] * SHIFT + target[:, None], jnp.iinfo(I32).max)
    keys, sorted_shares = lax.sort((keys.reshape(-1), shares.reshape(-1)), num_keys=1, is_stable=False)
    keys = keys[:live_most]
    sorted_shares = sorted_shares[:live_most]
    edges = jnp.arange(owners * SPLIT + 1, dtype=I32) * (rows_owned // SPLIT * SHIFT)
    starts = jnp.sum((keys[None, :] < edges[:, None]).astype(I32), axis=1)
    own_length = SHIFT
    meta = jnp.concatenate(
        [
            starts.astype(F32),
            jnp.stack([jnp.sum(present), jnp.sum(masked_weight)]),
        ]
    )
    meta_length = -(-meta.shape[0] // LANES) * LANES

    def as_code(key):
        return (key % (rows_owned * SHIFT)).astype(F32)

    request = jnp.concatenate(
        [
            padded(as_code(keys), length),
            padded(sorted_shares, length),
            padded(meta, meta_length),
            padded(lookup_ids[:, 0].astype(F32), own_length),
        ]
    )
    plane = lax.all_gather(request, "table", axis=0)

    own_ids = plane[:, -own_length:][:, :batch_rows].astype(I32).reshape(-1)
    wanted = own_ids - owner * rows_owned
    mine = (wanted >= 0) & (wanted < rows_owned)
    found = feature_table[jnp.clip(wanted, 0, rows_owned - 1)]
    found = jnp.where(mine[:, None], found, jnp.zeros((), BF16))
    self_rows = lax.psum_scatter(found, "table", scatter_dimension=0, tiled=True)
    every = lax.all_gather(plane, "rep", axis=0).reshape(devices, -1)

    def unpack(lists, start, stride):
        count = lists.shape[0]
        at = 2 * length
        codes = lists[:, :length].astype(I32).reshape(count, 1, length)
        parts = lists[:, length:at].reshape(count, 1, length)
        notes = lists[:, at : at + meta_length]
        bounds = lax.dynamic_slice(notes, (0, start), (count, stride + 1))[:, ::stride].astype(I32)
        sums = jnp.sum(notes[:, owners * SPLIT + 1 : owners * SPLIT + 3], axis=0)
        return codes, parts, bounds, sums

    def own_lists(lists, start):
        ids = lists[:, -own_length:][:, :batch_rows].astype(I32)
        keys = lax.sort(ids * SHIFT + target[None, :], dimension=1)
        ends = (start + jnp.arange(2, dtype=I32)) * (rows_owned // SPLIT * SHIFT)
        own_bounds = jnp.sum((keys[:, None, :] < ends[None, :, None]).astype(I32), axis=2)
        own_codes = jnp.pad(keys % (rows_owned * SHIFT), ((0, 0), (0, own_length - batch_rows)))
        return own_codes.reshape(-1, 1, own_length), own_bounds

    codes, parts, bounds, _ = unpack(plane, owner * SPLIT, SPLIT)
    bounds, _ = lax.optimization_barrier((bounds, found))
    hidden, pooled_parts = owner_forward(
        feature_table, neighbour_query_weight, query_bias, codes, parts, bounds, batch_rows
    )
    pooled_parts, self_rows = lax.optimization_barrier((pooled_parts, self_rows))
    pooled = lax.psum_scatter(pooled_parts, "table", scatter_dimension=0, tiled=True)
    half = lax.rem(group, SPLIT)
    all_codes, all_parts, all_bounds, sums = unpack(every, owner * SPLIT + half, 1)
    all_own_codes, own_bounds = own_lists(every, owner * SPLIT + half)
    all_bounds = jnp.concatenate([all_bounds, own_bounds], axis=1)
    rows_major = Layout(major_to_minor=(0, 1, 2))
    all_codes = with_layout_constraint(all_codes, rows_major)
    all_parts = with_layout_constraint(all_parts, rows_major)
    pooled, lists = lax.optimization_barrier((pooled, (all_codes, all_parts, all_own_codes, all_bounds, sums)))
    all_codes, all_parts, all_own_codes, all_bounds, sums = lists
    pooled = lax.reduce_precision(pooled, 8, 7).astype(BF16)

    joined = jnp.concatenate([self_rows, pooled], axis=1)
    mixed = jnp.dot(joined, mix_weight, preferred_element_type=F32) + mix_bias
    activation = jax.nn.relu(mixed)
    inverse = lax.rsqrt(jnp.mean(activation * activation, axis=1, keepdims=True) + 1e-06)
    embed = (activation * inverse).astype(BF16)
    cotangent = embed_cot.astype(F32)
    grad_act = inverse * cotangent - activation * (inverse * inverse * inverse) * jnp.mean(
        activation * cotangent, axis=1, keepdims=True
    )
    grad_mixed = jnp.where(mixed > 0, grad_act, 0.0).astype(BF16)
    all_mixed = lax.all_gather(grad_mixed, ("table", "rep"), axis=0, tiled=True)
    mix_part = 2 * width // devices
    columns = lax.all_to_all(
        joined.reshape(batch_rows, devices, mix_part).transpose(1, 0, 2),
        ("table", "rep"),
        split_axis=0,
        concat_axis=0,
        tiled=True,
    ).reshape(devices * batch_rows, mix_part)

    mix_rows = lax.dot_general(
        columns, all_mixed, (((0,), (0,)), ((), ())), preferred_element_type=F32
    ).astype(BF16)
    all_mixed, mix_rows = lax.optimization_barrier((all_mixed, mix_rows))
    mix_gathered = lax.all_gather(mix_rows, ("table", "rep"), axis=0, tiled=True)

    partner = group + 1 - 2 * half
    swap = [(i, i + 1 - 2 * (i % SPLIT)) for i in range(groups)]
    grad_pre, self_sums, query_part, query_send, mix_bias_part = owner_backward(
        feature_table,
        hidden,
        all_mixed,
        mix_weight,
        all_codes,
        all_parts,
        all_own_codes,
        all_bounds,
        jnp.stack([group, partner]),
        owners,
        groups,
        batch_rows,
    )
    part = width // groups
    send_first, send_last = table_columns_grad(
        grad_pre, self_sums, neighbour_query_weight, mix_weight, partner.reshape(1), part
    )
    (table_grad,) = table_columns_grad(
        grad_pre, self_sums, neighbour_query_weight, mix_weight, group.reshape(1), part, rows_owned
    )
    mix_bias_grad = jnp.sum(mix_bias_part, axis=0)

    query_rows = width // devices
    query_part = query_part + lax.ppermute(query_send, "rep", swap).astype(F32)
    send_first, mix_gathered = lax.optimization_barrier((send_first, mix_gathered))
    mix_weight_grad = mix_gathered.astype(F32)
    got_first = lax.ppermute(send_first, "rep", swap)
    bias_rows = SUBLANES
    outgoing = jnp.concatenate(
        [
            query_part[:part].reshape(owners, query_rows, width),
            jnp.broadcast_to(query_part[part : part + bias_rows], (owners, bias_rows, width)),
        ],
        axis=1,
    )
    incoming = lax.all_to_all(outgoing.astype(BF16), "table", split_axis=0, concat_axis=0, tiled=True)
    summed = jnp.sum(incoming.astype(F32), axis=0)
    query_bias_grad = summed[query_rows]
    column = lax.all_to_all(
        jnp.broadcast_to(summed[:query_rows].astype(BF16), (groups, query_rows, width)),
        "rep",
        split_axis=0,
        concat_axis=0,
        tiled=True,
    )
    column, got_first, mix_weight_grad = lax.optimization_barrier((column, got_first, mix_weight_grad))
    got_last = lax.ppermute(send_last, "rep", swap)
    table_got = jnp.concatenate([got_first, got_last], axis=1)
    gathered = lax.all_to_all(
        jnp.broadcast_to(column, (owners, groups, query_rows, width)), "table", split_axis=0, concat_axis=0, tiled=True
    )
    query_weight_grad = gathered.transpose(1, 0, 2, 3).reshape(width, width).astype(F32)
    table_grad = lax.dynamic_update_slice(
        table_grad, table_got.astype(F32), ((1 - half) * (rows_owned // SPLIT), 0)
    )
    statistics = sums / (batch_rows * devices)
    return (
        embed,
        table_grad,
        query_weight_grad,
        query_bias_grad,
        mix_weight_grad,
        mix_bias_grad,
        statistics,
    )


def solution(mesh):
    in_specs = (
        P("table", None),
        P(),
        P(),
        P(),
        P(),
        P(("table", "rep"), None),
        P(("table", "rep")),
        P(("table", "rep"), None),
        P(("table", "rep"), None),
    )
    out_specs = (P(("table", "rep"), None), P("table", "rep"), P(), P(), P(), P(), P())
    return jax.shard_map(local, mesh=mesh, in_specs=in_specs, out_specs=out_specs, check_vma=False)
```
